256 devices in a mesh: seq: 8 (over z), files: 32 (over x, y, core).
Axes of the slice: x: 4, y: 4, z: 8, core: 2. Of those that a mesh axis runs over, the one named last changes fastest.
Arguments:
- q_lin: bfloat16 [32, 2048, 320], P('files', 'seq'), may hold values from -6 to 6
- k_lin: bfloat16 [32, 2048, 320], P('files', 'seq'), may hold values from -6 to 6
- v_lin: bfloat16 [32, 2048, 2560], P('files', 'seq'), may hold values from -6 to 6
- q_soft: bfloat16 [32, 2048, 1280], P('files', 'seq'), may hold values from -48 to 48
- k_soft: bfloat16 [32, 2048, 1280], P('files', 'seq'), may hold values from -6 to 6
- v_soft: bfloat16 [32, 2048, 1280], P('files', 'seq'), may hold values from -6 to 6
- import_ids: int32 [32, 8, 8], P('files', 'seq'), may hold values from -1 to 63, as said below
- import_counts: int32 [32, 8], P('files', 'seq'), may hold values from 6 to 8, as said below
Outputs:
- lin_out: bfloat16 [32, 2048, 2560], P('files', 'seq')
- soft_out: bfloat16 [32, 2048, 1280], P('files', 'seq')
The draws below stay inside these ranges and needn't reach their ends.
Inputs may be any that keep to these rules, and one draw needn't show every extreme that they name: `import_ids`: entries before the count name distinct file groups other than the reader's own, entry = group * 2 + block; entries from the count on are -1. For each sequence shard index, some file group is listed before the count by every other file group's list of that index. `import_counts`: some sequence shard lists 8 blocks.
All inputs are finite; a program needn't handle non-finite values.
Results may differ from the reference program's by a relative error of at most 0.005.
Values may be sent and summed in bfloat16 or wider, within the bound.
No kernel may reach another device: no remote copies, remote signals or barrier semaphores. Data moves between devices by JAX's collectives and lax.ppermute only.
A program may use at most 192 MiB of HBM per device.

```python
import math
import jax
import jax.numpy as jnp
import numpy as np
from jax import lax

D = 2560
HEADS = 20
FEAT = 16
FEATS = 153
SM_HEADS = 10
SM_HD = 128
SM_W = 1280
BLK = 128
TOK_DEV = 256
MAXB = 8
BLOCKS_DEV = 2
GROUPS = 32
SHARDS = 8
SEQ_LEN = 2048


def score_pair(key):
    key_keys = jax.random.fold_in(key, 101)
    key_query = jax.random.fold_in(key, 102)
    shape = (GROUPS, SEQ_LEN, SM_W)
    keys = jnp.clip(jax.random.normal(key_keys, shape, jnp.float32), -6.0, 6.0)
    query = jnp.clip(jax.random.normal(key_query, shape, jnp.float32), -6.0, 6.0)
    return (query, keys)


def draw_q_soft(key, part):
    return score_pair(key)[0].astype(jnp.bfloat16)


def draw_k_soft(key, part):
    return score_pair(key)[1].astype(jnp.bfloat16)


def import_lists(key):
    base = jax.random.fold_in(key, 7)
    key_order = jax.random.fold_in(base, 1)
    key_block = jax.random.fold_in(base, 2)
    key_light = jax.random.fold_in(base, 4)
    key_place = jax.random.fold_in(base, 5)
    key_hot = jax.random.fold_in(base, 6)
    key_slot = jax.random.fold_in(base, 8)
    others = GROUPS - 1
    scores = jax.random.randint(key_order, (GROUPS, SHARDS, others), 0, 1 << 20) * others + jnp.arange(others)
    hot_owner = jax.random.randint(key_hot, (SHARDS,), 0, GROUPS)
    target = (hot_owner[None, :] - jnp.arange(GROUPS)[:, None] - 1) % GROUPS
    scores = jnp.where(jnp.arange(others)[None, None, :] == target[..., None], -1, scores)
    order = jnp.argsort(scores, axis=-1, stable=True)[..., :MAXB]
    low = 3 * MAXB // 4
    counts = low + jax.random.randint(key_light, (GROUPS, SHARDS), 0, MAXB - low + 1)
    counts = counts.reshape(-1)
    place = jax.random.randint(key_place, (), 0, GROUPS * SHARDS)
    counts = counts.at[place].set(MAXB).reshape(GROUPS, SHARDS).astype(jnp.int32)
    slot = jax.random.randint(key_slot, (GROUPS, SHARDS), 0, 1 << 20) % counts
    position = jnp.arange(MAXB)[None, None, :]
    source = jnp.where(position == 0, slot[..., None], jnp.where(position == slot[..., None], 0, position))
    order = jnp.take_along_axis(order, source, axis=-1)
    owner = (jnp.arange(GROUPS)[:, None, None] + 1 + order) % GROUPS
    block = jax.random.randint(key_block, (GROUPS, SHARDS, MAXB), 0, BLOCKS_DEV)
    entries = owner * BLOCKS_DEV + block
    entries = jnp.where(jnp.arange(MAXB) < counts[..., None], entries, -1).astype(jnp.int32)
    return (entries, counts)


def draw_import_ids(key, part):
    return import_lists(key)[0]


def draw_import_counts(key, part):
    return import_lists(key)[1]


def shard_levels(stream_key, shape, shards, low, largest):
    def one(dim, parts):
        steps = jax.random.uniform(jax.random.fold_in(jax.random.fold_in(stream_key, 6), dim), (parts,), jnp.float32, low / len(shards), largest / len(shards))
        return jnp.repeat(jnp.exp(steps), shape[dim] // parts).reshape((-1,) + (1,) * (len(shape) - dim - 1))

    factor_of = one(*shards[0])
    for cut in shards[1:]:
        factor_of = factor_of * one(*cut)
    return factor_of


def noise(own_key, dims, deviation, limit, cuts=(), held_as=jnp.bfloat16):
    values = jax.random.normal(own_key, dims, jnp.float32) * deviation
    if len(cuts) > 0:
        values = shard_levels(own_key, dims, cuts, -0.22, 0.18) * values
    return jnp.clip(values, min=-limit, max=limit).astype(held_as)


def setup_inputs(seed: int = 0) -> dict:
    streams_of = jax.random.split(jax.random.key(seed), 9)
    q_lin = noise(streams_of[0], (GROUPS, SEQ_LEN, HEADS * FEAT), 1.0, 6.0, ((0, 32), (1, 8)))
    k_lin = noise(streams_of[1], (GROUPS, SEQ_LEN, HEADS * FEAT), 1.0, 6.0, ((0, 32), (1, 8)))
    v_lin = noise(streams_of[2], (GROUPS, SEQ_LEN, D), 1.0, 6.0, ((0, 32), (1, 8)))
    q_soft = draw_q_soft(jax.random.fold_in(streams_of[8], 71), 0)
    k_soft = draw_k_soft(jax.random.fold_in(streams_of[8], 71), 0)
    v_soft = noise(streams_of[5], (GROUPS, SEQ_LEN, SM_W), 1.0, 6.0, ((0, 32), (1, 8)))
    import_ids = draw_import_ids(jax.random.fold_in(streams_of[8], 71), 0)
    import_counts = draw_import_counts(jax.random.fold_in(streams_of[8], 71), 0)
    return dict(q_lin=q_lin, k_lin=k_lin, v_lin=v_lin, q_soft=q_soft, k_soft=k_soft, v_soft=v_soft, import_ids=import_ids, import_counts=import_counts)


inv_root_two = 0.7071067811865476
highest_precision = lax.Precision.HIGHEST

def feature_map(inputs):
    count_in = inputs.shape[-1]
    rows, cols = np.triu_indices(count_in)
    factor = np.where(rows == cols, inv_root_two, 1.0).astype(np.float32)
    quadratic = inputs[..., rows] * inputs[..., cols] * factor
    ones = jnp.ones(inputs.shape[:-1] + (1,), inputs.dtype)
    return jnp.concatenate([ones, inputs, quadratic], axis=-1)

def rounded(values):
    return lax.optimization_barrier(values.astype(jnp.bfloat16)).astype(jnp.float32)

def linear_group(inputs):
    query_rows, key_rows, value_rows = inputs
    head_dim = D // HEADS
    nblocks = SEQ_LEN // BLK
    feat_q = feature_map(query_rows.astype(jnp.float32).reshape(SEQ_LEN, HEADS, FEAT) * 0.5).astype(jnp.bfloat16)
    feat_k = feature_map(key_rows.astype(jnp.float32).reshape(SEQ_LEN, HEADS, FEAT) * 0.5).astype(jnp.bfloat16)
    block_qs = feat_q.reshape(nblocks, BLK, HEADS, FEATS)
    block_ks = feat_k.reshape(nblocks, BLK, HEADS, FEATS)
    block_vs = value_rows.reshape(nblocks, BLK, HEADS, head_dim)
    causal_masking = jnp.tril(jnp.ones((BLK, BLK), jnp.float32))

    def advance(carry, block):
        running_state, norm_sum = carry
        query_tile_rows = block[0].astype(jnp.float32)
        key_tile_rows = block[1].astype(jnp.float32)
        value_tile_rows = block[2].astype(jnp.float32)
        weight_matrix = jnp.einsum('evy,ivy->vei', query_tile_rows, key_tile_rows, precision=highest_precision) * causal_masking
        numerator = jnp.einsum('hqk,khd->qhd', rounded(weight_matrix), value_tile_rows, precision=highest_precision)
        numerator = numerator + jnp.einsum('qhf,hfd->qhd', query_tile_rows, running_state, precision=highest_precision)
        denominator = lax.optimization_barrier(jnp.sum(weight_matrix, axis=-1)).T + jnp.einsum('qhf,hf->qh', query_tile_rows, norm_sum, precision=highest_precision)
        output = (numerator / denominator[..., None]).astype(jnp.bfloat16)
        running_state = running_state + jnp.einsum('sir,sig->irg', key_tile_rows, value_tile_rows, precision=highest_precision)
        norm_sum = norm_sum + lax.optimization_barrier(jnp.sum(key_tile_rows, axis=0))
        return ((running_state, norm_sum), output)
    start = (jnp.zeros((HEADS, FEATS, head_dim), jnp.float32), jnp.zeros((HEADS, FEATS), jnp.float32))
    final, outputs = lax.scan(advance, start, (block_qs, block_ks, block_vs))
    return outputs.reshape(SEQ_LEN, D)

def reference(q_lin, k_lin, v_lin, q_soft, k_soft, v_soft, import_ids, import_counts):
    lin_out = lax.map(linear_group, (q_lin, k_lin, v_lin))
    key_all = k_soft.reshape(GROUPS, SHARDS, BLOCKS_DEV, BLK, SM_W)
    value_all = v_soft.reshape(GROUPS, SHARDS, BLOCKS_DEV, BLK, SM_W)
    scale = 1.0 / math.sqrt(SM_HD)

    def soft_group(inputs):
        query_rows, key_rows, value_rows, id_rows, counts = inputs
        query5 = query_rows.astype(jnp.float32).reshape(SHARDS, BLOCKS_DEV, BLK, SM_HEADS, SM_HD)
        own_keys = key_rows.astype(jnp.float32).reshape(SHARDS, BLOCKS_DEV, BLK, SM_HEADS, SM_HD)
        own_vals = value_rows.astype(jnp.float32).reshape(SHARDS, BLOCKS_DEV, BLK, SM_HEADS, SM_HD)
        own_scores = jnp.einsum('sbqhd,sbkhd->shbqk', query5, own_keys, precision=highest_precision) * scale
        own_scores = own_scores.reshape(SHARDS, SM_HEADS, TOK_DEV, BLK)
        safe_ids = jnp.maximum(id_rows, 0)
        owner = safe_ids // BLOCKS_DEV
        within = safe_ids % BLOCKS_DEV
        shard_index = jnp.arange(SHARDS)[:, None]
        imp_keys = key_all[owner, shard_index, within].astype(jnp.float32).reshape(SHARDS, MAXB * BLK, SM_HEADS, SM_HD)
        imp_vals = value_all[owner, shard_index, within].astype(jnp.float32).reshape(SHARDS, MAXB * BLK, SM_HEADS, SM_HD)
        query4 = query5.reshape(SHARDS, TOK_DEV, SM_HEADS, SM_HD)
        imp_scores = jnp.einsum('sqhd,skhd->shqk', query4, imp_keys, precision=highest_precision) * scale
        listed = jnp.repeat(jnp.arange(MAXB)[None, :] < counts[:, None], BLK, axis=1)
        imp_scores = jnp.where(listed[:, None, None, :], imp_scores, -jnp.inf)
        top = jnp.maximum(lax.optimization_barrier(jnp.max(own_scores, axis=-1)), lax.optimization_barrier(jnp.max(imp_scores, axis=-1)))
        own_prob = jnp.exp(own_scores - top[..., None])
        imp_prob = jnp.exp(imp_scores - top[..., None])
        total = lax.optimization_barrier(jnp.sum(own_prob, axis=-1)) + lax.optimization_barrier(jnp.sum(imp_prob, axis=-1))
        own_prob5 = rounded(own_prob).reshape(SHARDS, SM_HEADS, BLOCKS_DEV, BLK, BLK)
        own_num = jnp.einsum('shbqk,sbkhd->sbqhd', own_prob5, own_vals, precision=highest_precision)
        own_num = own_num.reshape(SHARDS, TOK_DEV, SM_HEADS, SM_HD)
        imp_num = jnp.einsum('shqk,skhd->sqhd', rounded(imp_prob), imp_vals, precision=highest_precision)
        output = (own_num + imp_num) / jnp.transpose(total, (0, 2, 1))[..., None]
        return output.astype(jnp.bfloat16).reshape(SEQ_LEN, SM_W)
    soft_out = lax.map(soft_group, (q_soft, k_soft, v_soft, import_ids, import_counts))
    return (lin_out, soft_out)
```

```python
import functools
import math

import jax
import jax.numpy as jnp
import numpy as np
from jax import lax
from jax.experimental import pallas as pl
from jax.experimental.pallas import tpu as pltpu
from jax.sharding import PartitionSpec as P

D = 2560
HEADS = 20
FEAT = 16
FEATS = 153
FROWS = 160
FPAD = 256
SM_HEADS = 10
SM_HD = 128
SM_W = 1280
BLK = 128
TOK = 256
LISTED = 8
HALF = 640
HALF_HEADS = 5
QROWS = 272
SIDE = 4
CORES = 2

inv_root_two = 0.7071067811865476
TO_LOG2 = math.log2(math.e) / math.sqrt(SM_HD)
NEG = -1e30
BF = jnp.bfloat16
F32 = jnp.float32
NT = (((1,), (1,)), ((), ()))
VMEM_LIMIT = 60 * 1024 * 1024


def along(what, step):
    pairs = []
    for x in range(SIDE):
        for y in range(SIDE):
            for c in range(CORES):
                on_x = (c == 0) == (what == "kv")
                x2 = (x + step) % SIDE if on_x else x
                y2 = y if on_x else (y + step) % SIDE
                pairs.append(((x * SIDE + y) * CORES + c, (x2 * SIDE + y2) * CORES + c))
    return pairs


def move(a, what, step):
    return lax.ppermute(a, "files", along(what, step))


def swap_cores(a):
    return lax.ppermute(a, "files", [(i, i ^ 1) for i in range(SIDE * SIDE * CORES)])


def feature_tables():
    rows, cols = np.triu_indices(FEAT)
    select = np.zeros((8, 2, FPAD, 128), np.float32)
    for j in range(8):
        for f in range(FEAT):
            select[j, 0, 1 + f, j * FEAT + f] = 0.5
        for n in range(len(rows)):
            select[j, 0, 1 + FEAT + n, j * FEAT + rows[n]] = 0.5
            select[j, 1, 1 + FEAT + n, j * FEAT + cols[n]] = 0.5
    first = np.zeros(FPAD, np.float32)
    first[0] = 1.0
    second = np.zeros(FPAD, np.float32)
    second[: 1 + FEAT] = 1.0
    factor = np.zeros(FPAD, np.float32)
    factor[:FEATS] = 1.0
    factor[1 + FEAT : FEATS] = np.where(rows == cols, inv_root_two, 1.0).astype(np.float32)
    vectors = np.stack([first, second, factor])
    tall = np.broadcast_to(vectors[:, :FROWS, None], (3, FROWS, 128))
    wide = np.zeros((8, FPAD), np.float32)
    wide[:3] = vectors
    return select.astype(jnp.bfloat16), np.ascontiguousarray(tall), wide


def pad_lanes(src_ref, dst_ref):
    dst_ref[:, 0:256] = src_ref[:, 0:256]
    dst_ref[:, 256:384] = jnp.zeros((TOK, 128), BF)
    dst_ref[:, 256:320] = src_ref[:, 256:320]


def head_group(ref, h):
    return ref[:, pl.ds(pl.multiple_of((h >> 3) * 128, 128), 128)]


def lanes_of(h):
    return pl.ds(pl.multiple_of(h * 128, 128), 128)


def features_tall(x, select, tall):
    a = lax.dot_general(select[0, :FROWS], x, NT, preferred_element_type=F32)
    b = lax.dot_general(select[1, :FROWS], x, NT, preferred_element_type=F32)
    first, second, factor = (jnp.concatenate([tall[i], tall[i]], axis=1) for i in range(3))
    return ((a + first) * (b + second) * factor).astype(BF)


def features_wide(x, select, wide):
    a = lax.dot_general(x, select[0], NT, preferred_element_type=F32)
    b = lax.dot_general(x, select[1], NT, preferred_element_type=F32)
    return ((a + wide[0:1]) * (b + wide[1:2]) * wide[2:3]).astype(BF)


def state_kernel(k_ref, v_ref, select_ref, tall_ref, out_ref, x_ref):
    pad_lanes(k_ref, x_ref)
    row = lax.broadcasted_iota(jnp.int32, (FROWS, 128), 0)
    ones = jnp.ones((8, TOK), BF)

    def head(h, carry):
        phi = features_tall(head_group(x_ref, h), select_ref[h & 7], tall_ref)
        state = jnp.dot(phi, v_ref[:, lanes_of(h)], preferred_element_type=F32)
        rest = jnp.concatenate([phi[128:FROWS], jnp.zeros((256 - FROWS, TOK), BF)], axis=0)
        n0 = lax.dot_general(ones, phi[:128], NT, preferred_element_type=F32)[0:1]
        n1 = lax.dot_general(ones, rest, NT, preferred_element_type=F32)[0:1]
        h0, h1 = n0.astype(BF).astype(F32), n1.astype(BF).astype(F32)
        for i, r in enumerate((h0, h1, n0 - h0, n1 - h1)):
            state = jnp.where(row == FEATS + i, r, state)
        out_ref[h] = state.astype(BF)
        return carry

    lax.fori_loop(0, HEADS, head, 0, unroll=4)


def prefix_kernel(place_ref, in_ref, out_ref):
    rows = in_ref.shape[1]
    row = lax.broadcasted_iota(jnp.int32, (rows, 128), 0) + (place_ref[0] & 1) * (FROWS // 2)
    row = jnp.where(row >= FROWS, row - FROWS, row)
    row = jnp.where(row >= FROWS, row - FROWS, row)
    high = (row == FEATS) | (row == FEATS + 1)
    low = (row == FEATS + 2) | (row == FEATS + 3)
    total = jnp.zeros((rows, 128), F32)
    for z in range(in_ref.shape[0]):
        both = total + pltpu.roll(total, rows - 2, 0)
        top = both.astype(BF).astype(F32)
        rest = pltpu.roll(both - top, 2, 0)
        out_ref[z] = jnp.where(high, top, jnp.where(low, rest, total)).astype(BF)
        total = total + in_ref[z].astype(F32)


def local_kernel(q_ref, k_ref, v_ref, select_ref, tall_ref, wide_ref, num_ref, den_ref, phi_ref, xq_ref, xk_ref):
    pad_lanes(q_ref, xq_ref)
    pad_lanes(k_ref, xk_ref)
    causal = lax.broadcasted_iota(jnp.int32, (TOK, TOK), 0) >= lax.broadcasted_iota(jnp.int32, (TOK, TOK), 1)
    lane = lax.broadcasted_iota(jnp.int32, (TOK, 128), 1)
    den_ref[...] = jnp.zeros((TOK, 128), F32)

    def head(h, carry):
        select = select_ref[h & 7]
        phi_q = features_wide(head_group(xq_ref, h), select, wide_ref)
        phi_k = features_tall(head_group(xk_ref, h), select, tall_ref)
        phi_k = jnp.concatenate([phi_k, jnp.zeros((FPAD - FROWS, TOK), BF)], axis=0)
        weight = jnp.dot(phi_q, phi_k, preferred_element_type=F32)
        weight = jnp.where(causal, weight, 0.0)
        num_ref[:, lanes_of(h)] = jnp.dot(weight.astype(BF), v_ref[:, lanes_of(h)], preferred_element_type=F32)
        den = jnp.sum(weight[:, :128] + weight[:, 128:], axis=1, keepdims=True)
        den_ref[...] = jnp.where(lane == h, den, den_ref[...])
        phi_ref[h] = phi_q
        return carry

    lax.fori_loop(0, HEADS, head, 0, unroll=2)


def finish_kernel(num_ref, den_ref, phi_ref, state_ref, out_ref):
    lane = lax.broadcasted_iota(jnp.int32, (TOK, 128), 1)

    def head(h, carry):
        phi = phi_ref[h]
        state = state_ref[h]
        padded = jnp.concatenate([state, jnp.zeros((FPAD - FROWS, 128), BF)], axis=0)
        carried = jnp.dot(phi, padded, preferred_element_type=F32)
        tail = state[FROWS - 16 : FROWS].astype(F32)
        at = FEATS - (FROWS - 16)
        n0 = tail[at : at + 1] + tail[at + 2 : at + 3]
        n1 = tail[at + 1 : at + 2] + tail[at + 3 : at + 4]
        phi32 = phi.astype(F32)
        den = jnp.where(lane == h, den_ref[...], 0.0) + phi32[:, :128] * n0 + phi32[:, 128:] * n1
        den = jnp.sum(den, axis=1, keepdims=True)
        out_ref[:, lanes_of(h)] = ((num_ref[:, lanes_of(h)] + carried) / den).astype(BF)
        return carry

    lax.fori_loop(0, HEADS, head, 0, unroll=4)


def pack_kernel(me_ref, ids_ref, count_ref, q_ref, k_ref, v_ref, kv_ref, kv_send_ref, q_out_ref, q_send_ref):
    core = me_ref[0] & 1
    lane = lax.broadcasted_iota(jnp.int32, (QROWS - TOK, HALF), 1)
    listed = jnp.full((QROWS - TOK, HALF), -1.0, F32)
    for i in range(LISTED):
        entry = jnp.where(i < count_ref[0], ids_ref[i], -1).astype(F32)
        listed = jnp.where(lane == i, entry, listed)
    for half, kv, q in ((core, kv_ref, q_out_ref), (1 - core, kv_send_ref, q_send_ref)):
        at = pl.ds(pl.multiple_of(half * HALF, 128), HALF)
        kv[0] = k_ref[:, at]
        kv[1] = v_ref[:, at]
        q[0:TOK] = q_ref[:, at]
        q[TOK:QROWS] = listed.astype(BF)


def attend_kernel(own, readers, me_ref, ids_ref, *refs):
    q_in, kv_in = refs[:readers], refs[readers : readers + 8]
    outs = refs[readers + 8 : readers + 8 + readers // 2]
    q_buf, kv_buf, o_buf, s_buf, m_buf, l_buf, a_buf, found, sems = refs[readers + 8 + readers // 2 :]
    copies = [pltpu.make_async_copy(q_in[i], q_buf.at[i], sems.at[i]) for i in range(readers)]
    copies += [pltpu.make_async_copy(kv_in[i], kv_buf.at[i], sems.at[readers + i]) for i in range(8)]
    for c in copies:
        c.start()
    me = me_ref[0]
    core, y, x = me & 1, (me >> 1) & (SIDE - 1), me >> 3
    lane = lax.broadcasted_iota(jnp.int32, (TOK, 128), 1)
    for c in copies:
        c.wait()

    def heads():
        return [(h, slice(h * 128, (h + 1) * 128)) for h in range(HALF_HEADS)]

    def reader(r, carry):
        count = jnp.int32(0)
        for i in range(LISTED):
            entry = ids_ref[r, i]
            xo, yo, co = entry >> 4, (entry >> 2) & (SIDE - 1), (entry >> 1) & 1
            mine = (entry >= 0) & jnp.where(core == 0, yo == y, xo == x)
            away = jnp.where(core == 0, xo - x, yo - y) & (SIDE - 1)
            found[count] = (away * 2 + (co ^ core)) * 2 + (entry & 1)
            count = count + mine.astype(jnp.int32)

        m_buf[...] = jnp.full(m_buf.shape, NEG, F32)
        l_buf[...] = jnp.zeros(l_buf.shape, F32)
        a_buf[...] = jnp.zeros(a_buf.shape, F32)

        def score(j, carry):
            slot, rows = found[j] >> 1, pl.ds(pl.multiple_of((found[j] & 1) * BLK, BLK), BLK)
            for h, at in heads():
                s = lax.dot_general(q_buf[r, 0:TOK, at], kv_buf[slot, 0, rows, at], NT, preferred_element_type=F32)
                s_buf[j, h] = s
                m_buf[h] = jnp.maximum(m_buf[h], s)
            return carry

        lax.fori_loop(0, count, score, 0)
        if own:
            for h, at in heads():
                parts = [
                    lax.dot_general(
                        q_buf[r, b * BLK : (b + 1) * BLK, at],
                        kv_buf[r, 0, b * BLK : (b + 1) * BLK, at],
                        NT,
                        preferred_element_type=F32,
                    )
                    for b in range(2)
                ]
                s = jnp.concatenate(parts, axis=0)
                s_buf[LISTED, h] = s
                m_buf[h] = jnp.maximum(m_buf[h], s)
        for h, at in heads():
            m_buf[h] = jnp.broadcast_to(jnp.max(m_buf[h], axis=1, keepdims=True) * TO_LOG2, (TOK, 128))

        def weigh(j, carry):
            slot, rows = found[j] >> 1, pl.ds(pl.multiple_of((found[j] & 1) * BLK, BLK), BLK)
            for h, at in heads():
                p = jnp.exp2(s_buf[j, h] * TO_LOG2 - m_buf[h])
                l_buf[h] = l_buf[h] + p
                a_buf[h] = a_buf[h] + jnp.dot(p.astype(BF), kv_buf[slot, 1, rows, at], preferred_element_type=F32)
            return carry

        lax.fori_loop(0, count, weigh, 0)
        if own:
            for h, at in heads():
                p = jnp.exp2(s_buf[LISTED, h] * TO_LOG2 - m_buf[h])
                l_buf[h] = l_buf[h] + p
                p = p.astype(BF)
                parts = [
                    jnp.dot(
                        p[b * BLK : (b + 1) * BLK],
                        kv_buf[r, 1, b * BLK : (b + 1) * BLK, at],
                        preferred_element_type=F32,
                    )
                    for b in range(2)
                ]
                a_buf[h] = a_buf[h] + jnp.concatenate(parts, axis=0)
        packed = jnp.zeros((TOK, 128), F32)
        for h, at in heads():
            total = jnp.sum(l_buf[h], axis=1, keepdims=True)
            empty = total == 0.0
            safe = jnp.where(empty, 1.0, total)
            o_buf[r, 0:TOK, at] = (a_buf[h] / safe).astype(BF)
            size = jnp.where(empty, NEG, m_buf[h][:, 0:1] + jnp.log2(safe))
            top = size.astype(BF).astype(F32)
            middle = (size - top).astype(BF).astype(F32)
            packed = jnp.where(lane == h, top, packed)
            packed = jnp.where(lane == HALF_HEADS + h, middle, packed)
            packed = jnp.where(lane == 2 * HALF_HEADS + h, size - top - middle, packed)
        o_buf[r, TOK:QROWS, :] = jnp.zeros((QROWS - TOK, HALF), BF)
        o_buf[r, TOK:QROWS, 0:TOK] = packed.T[0 : QROWS - TOK].astype(BF)
        return carry

    lax.fori_loop(0, readers, reader, 0)
    back = [
        pltpu.make_async_copy(o_buf.at[2 * i : 2 * i + 2], outs[i], sems.at[readers + 8 + i])
        for i in range(readers // 2)
    ]
    for c in back:
        c.start()
    for c in back:
        c.wait()


def join_kernel(*refs):
    parts, outs = refs[:4], refs[4:]
    for r in range(2):
        sizes = []
        for p in parts:
            packed = p[r, TOK:QROWS, 0:TOK].astype(F32)
            packed = jnp.concatenate([packed, jnp.zeros((128 - (QROWS - TOK), TOK), F32)], axis=0).T
            sizes.append(packed + pltpu.roll(packed, 128 - HALF_HEADS, 1) + pltpu.roll(packed, 128 - 2 * HALF_HEADS, 1))
        top = functools.reduce(jnp.maximum, sizes)
        shares = [jnp.exp2(s - top) for s in sizes]
        total = functools.reduce(jnp.add, shares)
        shares = [s / total for s in shares]
        for h in range(HALF_HEADS):
            at = slice(h * 128, (h + 1) * 128)
            o = sum(s[:, h : h + 1] * p[r, 0:TOK, at].astype(F32) for s, p in zip(shares, parts, strict=True))
            outs[r][:, at] = o.astype(BF)


def place_kernel(me_ref, mine_ref, other_ref, out_ref):
    core = me_ref[0] & 1
    out_ref[:, pl.ds(pl.multiple_of(core * HALF, 128), HALF)] = mine_ref[...]
    out_ref[:, pl.ds(pl.multiple_of((1 - core) * HALF, 128), HALF)] = other_ref[...]


def shape(*dims, dtype=BF):
    return jax.ShapeDtypeStruct(dims, dtype)


SMEM = pl.BlockSpec(memory_space=pltpu.SMEM)
VMEM = pl.BlockSpec(memory_space=pltpu.VMEM)
ANY = pl.BlockSpec(memory_space=pl.ANY)
PARAMS = pltpu.CompilerParams(vmem_limit_bytes=VMEM_LIMIT)


def cost(flops, moved):
    return pl.CostEstimate(flops=int(flops), bytes_accessed=int(moved), transcendentals=0)


def attend(own, me, ids, queries, blocks):
    readers = len(queries)
    return pl.pallas_call(
        functools.partial(attend_kernel, own, readers),
        name="attend_own" if own else "attend_far",
        out_shape=[shape(2, QROWS, HALF)] * (readers // 2),
        in_specs=[SMEM, SMEM] + [ANY] * (readers + 8),
        out_specs=[ANY] * (readers // 2),
        scratch_shapes=[
            pltpu.VMEM((readers, QROWS, HALF), BF),
            pltpu.VMEM((8, 2, TOK, HALF), BF),
            pltpu.VMEM((readers, QROWS, HALF), BF),
            pltpu.VMEM((LISTED + 1, HALF_HEADS, TOK, 128), F32),
            pltpu.VMEM((HALF_HEADS, TOK, 128), F32),
            pltpu.VMEM((HALF_HEADS, TOK, 128), F32),
            pltpu.VMEM((HALF_HEADS, TOK, 128), F32),
            pltpu.SMEM((LISTED + 1,), jnp.int32),
            pltpu.SemaphoreType.DMA((readers + 8 + readers // 2,)),
        ],
        compiler_params=PARAMS,
        cost_estimate=cost(readers * 4e8, 8e6),
    )(me, ids, *queries, *blocks)


def body(q_lin, k_lin, v_lin, q_soft, k_soft, v_soft, import_ids, import_counts):
    select, tall, wide = (jnp.asarray(t) for t in feature_tables())
    me = lax.axis_index("files").astype(jnp.int32).reshape(1)
    place = lax.axis_index("seq").astype(jnp.int32).reshape(1)
    shards = lax.axis_size("seq")

    kv_a, kv_send, q_a, q_send = pl.pallas_call(
        pack_kernel,
        name="pack",
        out_shape=[shape(2, TOK, HALF), shape(2, TOK, HALF), shape(QROWS, HALF), shape(QROWS, HALF)],
        in_specs=[SMEM] * 3 + [VMEM] * 3,
        out_specs=[VMEM] * 4,
        compiler_params=PARAMS,
        cost_estimate=cost(0, 4e6),
    )(me, import_ids[0, 0], import_counts[0], q_soft[0], k_soft[0], v_soft[0])

    kv_b, q_b = swap_cores(kv_send), swap_cores(q_send)
    kv_a_left, kv_a_right = move(kv_a, "kv", 1), move(kv_a, "kv", -1)
    kv_b_left, kv_b_right = move(kv_b, "kv", 1), move(kv_b, "kv", -1)
    q_a_left, q_a_right = move(q_a, "q", 1), move(q_a, "q", -1)
    q_b_left, q_b_right = move(q_b, "q", 1), move(q_b, "q", -1)
    kv_a_far, kv_b_far = move(kv_a_left, "kv", 1), move(kv_b_right, "kv", -1)
    q_a_far, q_b_far = move(q_a_left, "q", 1), move(q_b_right, "q", -1)

    state = pl.pallas_call(
        state_kernel,
        name="state",
        out_shape=shape(HEADS, FROWS, 128),
        in_specs=[VMEM] * 4,
        out_specs=VMEM,
        scratch_shapes=[pltpu.VMEM((TOK, 384), BF)],
        compiler_params=PARAMS,
        cost_estimate=cost(1e9, 4e6),
    )(k_lin[0], v_lin[0], select, tall)
    slices = lax.all_to_all(state.reshape(shards, HEADS * FROWS // shards, 128), "seq", 0, 0, tiled=True)

    num, den, phi = pl.pallas_call(
        local_kernel,
        name="local",
        out_shape=[shape(TOK, D, dtype=F32), shape(TOK, 128, dtype=F32), shape(HEADS, TOK, FPAD)],
        in_specs=[VMEM] * 6,
        out_specs=[VMEM] * 3,
        scratch_shapes=[pltpu.VMEM((TOK, 384), BF), pltpu.VMEM((TOK, 384), BF)],
        compiler_params=PARAMS,
        cost_estimate=cost(4e9, 8e6),
    )(q_lin[0], k_lin[0], v_lin[0], select, tall, wide)

    prefix = pl.pallas_call(
        prefix_kernel,
        name="prefix",
        out_shape=shape(*slices.shape),
        in_specs=[SMEM, VMEM],
        out_specs=VMEM,
        compiler_params=PARAMS,
        cost_estimate=cost(0, 2e6),
    )(place, slices)
    before = lax.all_to_all(prefix, "seq", 0, 0, tiled=True).reshape(HEADS, FROWS, 128)

    blocks = (kv_a, kv_b, kv_a_right, kv_b_right, kv_a_far, kv_b_far, kv_a_left, kv_b_left)

    def lists(queries):
        return jnp.stack([q[TOK, :LISTED] for q in queries]).astype(jnp.int32)

    far = (q_a_left, q_b_left, q_a_right, q_b_right, q_a_far, q_b_far)
    to_left, to_right, to_far = attend(False, me, lists(far), far, blocks)
    from_right, from_left, from_far = move(to_left, "q", -1), move(to_right, "q", 1), move(to_far, "q", 2)
    (here,) = attend(True, me, lists((q_a, q_b)), (q_a, q_b), blocks)
    mine, send = pl.pallas_call(
        join_kernel,
        name="join",
        out_shape=[shape(TOK, HALF)] * 2,
        in_specs=[VMEM] * 4,
        out_specs=[VMEM] * 2,
        compiler_params=PARAMS,
        cost_estimate=cost(0, 4e6),
    )(here, from_right, from_left, from_far)
    other = swap_cores(send)
    soft_out = pl.pallas_call(
        place_kernel,
        name="place",
        out_shape=shape(TOK, SM_W),
        in_specs=[SMEM, VMEM, VMEM],
        out_specs=VMEM,
        compiler_params=PARAMS,
        cost_estimate=cost(0, 1e6),
    )(me, mine, other)

    lin_out = pl.pallas_call(
        finish_kernel,
        name="finish",
        out_shape=shape(TOK, D),
        in_specs=[VMEM] * 4,
        out_specs=VMEM,
        compiler_params=PARAMS,
        cost_estimate=cost(4e8, 8e6),
    )(num, den, phi, before)
    return lin_out[None], soft_out[None]


def solution(mesh):
    wide = P("files", "seq", None)
    return jax.shard_map(
        body,
        mesh=mesh,
        in_specs=(wide,) * 7 + (P("files", "seq"),),
        out_specs=(wide, wide),
        check_vma=False,
    )
```

```python
import functools
import math

import jax
import jax.numpy as jnp
import numpy as np
from jax import lax
from jax.experimental import pallas as pl
from jax.experimental.pallas import tpu as pltpu
from jax.sharding import PartitionSpec as P

D = 2560
HEADS = 20
FEAT = 16
FEATS = 153
FROWS = 160
FPAD = 256
SM_HD = 128
SM_W = 1280
BLK = 128
TOK = 256
LISTED = 8
GROUP = 4
HALF = 640
HALF_HEADS = 5
QROWS = 272
SIDE = 4
CORES = 2

inv_root_two = 0.7071067811865476
TO_LOG2 = math.log2(math.e) / math.sqrt(SM_HD)
NEG = -1e30
BF = jnp.bfloat16
F32 = jnp.float32
NT = (((1,), (1,)), ((), ()))


def along(what, step):
    pairs = []
    for x in range(SIDE):
        for y in range(SIDE):
            for c in range(CORES):
                on_x = (c == 0) == (what == "kv")
                x2 = (x + step) % SIDE if on_x else x
                y2 = y if on_x else (y + step) % SIDE
                pairs.append(((x * SIDE + y) * CORES + c, (x2 * SIDE + y2) * CORES + c))
    return pairs


def move(a, what, step):
    return lax.ppermute(a, "files", along(what, step))


def swap_cores(a):
    return lax.ppermute(a, "files", [(i, i ^ 1) for i in range(SIDE * SIDE * CORES)])


def feature_tables():
    rows, cols = np.triu_indices(FEAT)
    one = np.zeros((GROUP, 2, FPAD, GROUP * FEAT), np.float32)
    for j in range(GROUP):
        for f in range(FEAT):
            one[j, 0, 1 + f, j * FEAT + f] = 0.5
        for n in range(len(rows)):
            one[j, 0, 1 + FEAT + n, j * FEAT + rows[n]] = 0.5
            one[j, 1, 1 + FEAT + n, j * FEAT + cols[n]] = 0.5
    first = np.zeros(FPAD, np.float32)
    first[0] = 1.0
    second = np.zeros(FPAD, np.float32)
    second[: 1 + FEAT] = 1.0
    factor = np.zeros(FPAD, np.float32)
    factor[:FEATS] = 1.0
    factor[1 + FEAT : FEATS] = np.where(rows == cols, inv_root_two, 1.0).astype(np.float32)
    vectors = np.stack([first, second, factor])
    tall = np.ascontiguousarray(np.broadcast_to(vectors[:, :FROWS, None], (3, FROWS, 128)))
    wide = np.zeros((8, FPAD), np.float32)
    wide[:3] = vectors
    by_row = np.ascontiguousarray(one[:, :, :FROWS]).reshape(GROUP, 2 * FROWS, GROUP * FEAT)
    by_lane = np.ascontiguousarray(one.transpose(0, 3, 1, 2)).reshape(GROUP, GROUP * FEAT, 2 * FPAD)
    return by_row.astype(jnp.bfloat16), by_lane.astype(jnp.bfloat16), tall, wide


def column(j):
    return slice(j * 128, (j + 1) * 128)


def with_ones(values):
    return jnp.concatenate([values, jnp.ones(values.shape, BF)], axis=1)


def state_kernel(k_ref, v_ref, select_ref, tall_ref, out_ref, phi_ref):
    row = lax.broadcasted_iota(jnp.int32, (FROWS, 128), 0)
    lane = lax.broadcasted_iota(jnp.int32, (FROWS, 128), 1)
    first, second, factor = (jnp.concatenate([tall_ref[i], tall_ref[i]], axis=1) for i in range(3))
    norms = jnp.zeros((FROWS, 128), F32)
    for j in range(GROUP):
        ab = jnp.dot(select_ref[j], k_ref[...], preferred_element_type=F32)
        phi = ((ab[:FROWS] + first) * (ab[FROWS:] + second) * factor).astype(BF)
        phi_ref[j] = phi
        both = jnp.dot(phi, with_ones(v_ref[:, column(j)]), preferred_element_type=F32)
        norms = jnp.where(lane == j, both[:, 128:], norms)
        out_ref[j] = both[:, :128].astype(BF)
    flat = jnp.concatenate([norms, jnp.zeros((256 - FROWS, 128), F32)], axis=0).T
    high = flat.astype(BF).astype(F32)
    low = flat - high
    at = row[FROWS - 16 :] - FEATS
    for j in range(GROUP):
        tail = jnp.zeros((16, 128), F32)
        pieces = (high[j : j + 1, :128], high[j : j + 1, 128:], low[j : j + 1, :128], low[j : j + 1, 128:])
        old = out_ref[j, FROWS - 16 :].astype(F32)
        for i, piece in enumerate(pieces):
            tail = jnp.where(at == i, piece, tail)
        out_ref[j, FROWS - 16 :] = jnp.where(at < 0, old, tail).astype(BF)


def prefix_kernel(place_ref, in_ref, out_ref):
    rows = in_ref.shape[1]
    row = lax.broadcasted_iota(jnp.int32, (rows, 128), 0) + (place_ref[0] & 1) * (FROWS // 2)
    row = jnp.where(row >= FROWS, row - FROWS, row)
    row = jnp.where(row >= FROWS, row - FROWS, row)
    high = (row == FEATS) | (row == FEATS + 1)
    low = (row == FEATS + 2) | (row == FEATS + 3)
    total = jnp.zeros((rows, 128), F32)
    for z in range(in_ref.shape[0]):
        both = total + pltpu.roll(total, rows - 2, 0)
        top = both.astype(BF).astype(F32)
        rest = pltpu.roll(both - top, 2, 0)
        out_ref[z] = jnp.where(high, top, jnp.where(low, rest, total)).astype(BF)
        total = total + in_ref[z].astype(F32)


def local_kernel(q_ref, phi_k_ref, v_ref, select_ref, wide_ref, num_ref, den_ref, phi_ref):
    causal = lax.broadcasted_iota(jnp.int32, (TOK, TOK), 0) >= lax.broadcasted_iota(jnp.int32, (TOK, TOK), 1)
    lane = lax.broadcasted_iota(jnp.int32, (TOK, 128), 1)
    x = q_ref[...].T
    den = jnp.zeros((TOK, 128), F32)
    for j in range(GROUP):
        a = jnp.dot(x, select_ref[j, :, :FPAD], preferred_element_type=F32)
        b = jnp.dot(x, select_ref[j, :, FPAD:], preferred_element_type=F32)
        phi_q = ((a + wide_ref[0:1]) * (b + wide_ref[1:2]) * wide_ref[2:3]).astype(BF)
        phi_ref[j] = phi_q
        phi_k = jnp.concatenate([phi_k_ref[j], jnp.zeros((FPAD - FROWS, TOK), BF)], axis=0)
        weight = jnp.where(causal, jnp.dot(phi_q, phi_k, preferred_element_type=F32), 0.0)
        both = jnp.dot(weight.astype(BF), with_ones(v_ref[:, column(j)]), preferred_element_type=F32)
        num_ref[:, column(j)] = both[:, :128]
        den = jnp.where(lane == j, both[:, 128:], den)
    den_ref[...] = den


def finish_kernel(num_ref, den_ref, phi_ref, state_ref, out_ref):
    lane = lax.broadcasted_iota(jnp.int32, (TOK, 128), 1)
    for j in range(GROUP):
        phi = phi_ref[j]
        state = state_ref[j]
        padded = jnp.concatenate([state, jnp.zeros((FPAD - FROWS, 128), BF)], axis=0)
        carried = jnp.dot(phi, padded, preferred_element_type=F32)
        tail = state[FROWS - 16 : FROWS].astype(F32)
        at = FEATS - (FROWS - 16)
        n0 = tail[at : at + 1] + tail[at + 2 : at + 3]
        n1 = tail[at + 1 : at + 2] + tail[at + 3 : at + 4]
        phi32 = phi.astype(F32)
        den = jnp.where(lane == j, den_ref[...], 0.0) + phi32[:, :128] * n0 + phi32[:, 128:] * n1
        den = jnp.sum(den, axis=1, keepdims=True)
        out_ref[:, column(j)] = ((num_ref[:, column(j)] + carried) / den).astype(BF)


def halves(core, refs):
    at = pl.ds(pl.multiple_of(core * HALF, 128), HALF)
    return [r.at[:, at] for r in refs]


def listed_rows(ids_ref, count_ref):
    lane = lax.broadcasted_iota(jnp.int32, (QROWS - TOK, HALF), 1)
    listed = jnp.full((QROWS - TOK, HALF), -1.0, F32)
    for i in range(LISTED):
        entry = jnp.where(i < count_ref[0], ids_ref[i], -1).astype(F32)
        listed = jnp.where(lane == i, entry, listed)
    return listed.astype(BF)


def pack_kernel(me_ref, ids_ref, count_ref, k_ref, v_ref, q_ref, out_ref, sems):
    copies = [
        pltpu.make_async_copy(half, out_ref.at[pl.ds(i * TOK, TOK)], sems.at[i])
        for i, half in enumerate(halves(1 - (me_ref[0] & 1), (k_ref, v_ref, q_ref)))
    ]
    for c in copies:
        c.start()
    out_ref[3 * TOK :] = listed_rows(ids_ref, count_ref)
    for c in copies:
        c.wait()


def pair_kernel(me_ref, ids_ref, count_ref, k_ref, v_ref, q_ref, mate_ref, kv_ref, both_ref, sems):
    targets = (kv_ref.at[0, 0], kv_ref.at[0, 1], both_ref.at[0, pl.ds(0, TOK)])
    copies = [
        pltpu.make_async_copy(half, to, sems.at[i])
        for i, (half, to) in enumerate(zip(halves(me_ref[0] & 1, (k_ref, v_ref, q_ref)), targets, strict=True))
    ]
    for c in copies:
        c.start()
    both_ref[0, TOK:QROWS] = listed_rows(ids_ref, count_ref)
    kv_ref[1, 0] = mate_ref[0:TOK]
    kv_ref[1, 1] = mate_ref[TOK : 2 * TOK]
    both_ref[1] = mate_ref[2 * TOK :]
    for c in copies:
        c.wait()


def attend_kernel(own, readers, me_ref, *refs):
    groups = readers // 2
    q_in, kv_in, outs = refs[:groups], refs[groups : groups + SIDE], refs[groups + SIDE : readers + SIDE]
    q_buf, g_buf, s_buf, m_buf, a_buf, wanted, ids, found, counts, q_sems, id_sem, g_sems = refs[readers + SIDE :]
    copies = [pltpu.make_async_copy(q_in[i], q_buf.at[pl.ds(2 * i, 2)], q_sems.at[i]) for i in range(groups)]
    for c in copies:
        c.start()
    me = me_ref[0]
    core, y, x = me & 1, (me >> 1) & (SIDE - 1), me >> 3
    lane = lax.broadcasted_iota(jnp.int32, (TOK, 128), 1)
    wanted[...] = jnp.full(wanted.shape, -1, jnp.int32)
    for c in copies:
        c.wait()
    for r in range(readers):
        wanted[r : r + 1] = q_buf[r, TOK:QROWS, 0:128].astype(F32).astype(jnp.int32)[0:1]
    pltpu.async_copy(wanted, ids, id_sem).wait()

    def search(r, carry):
        count = jnp.int32(0)
        for i in range(LISTED):
            entry = ids[r, i]
            xo, yo, co = entry >> 4, (entry >> 2) & (SIDE - 1), (entry >> 1) & 1
            mine = (entry >= 0) & jnp.where(core == 0, yo == y, xo == x)
            away = jnp.where(core == 0, xo - x, yo - y) & (SIDE - 1)
            found[r, count] = (away * 2 + (co ^ core)) * 2 + (entry & 1)
            count = count + mine.astype(jnp.int32)
        counts[r] = count
        return carry

    lax.fori_loop(0, readers, search, 0)
    heads = [(h, slice(h * 128, (h + 1) * 128)) for h in range(HALF_HEADS)]

    def fetch(r, slot):
        def one(i, carry):
            code = found[r, i]
            rows = pl.ds(pl.multiple_of((code & 1) * BLK, BLK), BLK)
            for away in range(SIDE):

                @pl.when((code >> 2) == away)
                def _():
                    source = kv_in[away].at[(code >> 1) & 1, :, rows, :]
                    pltpu.make_async_copy(source, g_buf.at[slot, i], g_sems.at[slot, i]).start()

            return carry

        lax.fori_loop(0, counts[r], one, 0)

    def arrived(r, slot):
        def one(i, carry):
            source = kv_in[0].at[0, :, pl.ds(0, BLK), :]
            pltpu.make_async_copy(source, g_buf.at[slot, i], g_sems.at[slot, i]).wait()
            return carry

        lax.fori_loop(0, counts[r], one, 0)

    def blank(slot, i):
        g_buf[slot, i, 1] = jnp.zeros((BLK, HALF), BF)

    def reader(r, slot, out_ref):
        count = counts[r]
        pairs = (count + 1) >> 1

        @pl.when((count & 1) == 1)
        def _():
            blank(slot, count)

        if not own:

            @pl.when(count == 0)
            def _():
                blank(slot, 0)
                blank(slot, 1)

        def blocks(j, kind, at):
            return jnp.concatenate([g_buf[slot, 2 * j, kind, :, at], g_buf[slot, 2 * j + 1, kind, :, at]], axis=0)

        def score(j, fresh):
            for h, at in heads:
                s = lax.dot_general(q_buf[r, 0:TOK, at], blocks(j, 0, at), NT, preferred_element_type=F32)
                s0, s1 = s[:, :128], jnp.where(2 * j + 1 < count, s[:, 128:], NEG)
                if fresh:
                    s0 = jnp.where(count > 0, s0, NEG)
                s_buf[j, h, :, 0:128] = s0
                s_buf[j, h, :, 128:256] = s1
                m = jnp.maximum(s0, s1)
                m_buf[h] = m if fresh else jnp.maximum(m_buf[h], m)

        def weigh(j, fresh):
            for h, at in heads:
                m = m_buf[h]
                p = jnp.exp2(s_buf[j, h] * TO_LOG2 - jnp.concatenate([m, m], axis=1)).astype(BF)
                a = jnp.dot(p, with_ones(blocks(j, 1, at)), preferred_element_type=F32)
                a_buf[h] = a if fresh else a_buf[h] + a

        if own:
            for h, at in heads:
                parts = []
                for b in range(2):
                    rows = slice(b * BLK, (b + 1) * BLK)
                    k = own_kv[r, 0, rows, at]
                    parts.append(lax.dot_general(q_buf[r, rows, at], k, NT, preferred_element_type=F32))
                s = jnp.concatenate(parts, axis=0)
                s_buf[LISTED // 2, h, :, 0:128] = s
                m_buf[h] = s
        else:
            score(0, True)
        start = 0 if own else 1

        def more_scores(j, carry):
            score(j, False)
            return carry

        lax.fori_loop(start, pairs, more_scores, 0)
        tops = jnp.zeros((TOK, 128), F32)
        for h, at in heads:
            m = jnp.broadcast_to(jnp.max(m_buf[h], axis=1, keepdims=True) * TO_LOG2, (TOK, 128))
            m_buf[h] = m
            tops = jnp.where(lane == h, m, tops)
        if own:
            for h, at in heads:
                p = jnp.exp2(s_buf[LISTED // 2, h, :, 0:128] * TO_LOG2 - m_buf[h]).astype(BF)
                parts = []
                for b in range(2):
                    rows = slice(b * BLK, (b + 1) * BLK)
                    v = with_ones(own_kv[r, 1, rows, at])
                    parts.append(jnp.dot(p[rows], v, preferred_element_type=F32))
                a_buf[h] = jnp.concatenate(parts, axis=0)
        else:
            weigh(0, True)

        def more_weights(j, carry):
            weigh(j, False)
            return carry

        lax.fori_loop(start, pairs, more_weights, 0)
        totals = jnp.ones((TOK, 128), F32)
        for h, at in heads:
            total = a_buf[h, :, 128:]
            out_ref[slot, 0:TOK, at] = (a_buf[h, :, :128] / total).astype(BF)
            totals = jnp.where(lane == h, total, totals)
        sizes = tops + jnp.log2(totals)
        if not own:
            sizes = jnp.where(jnp.logical_and(count == 0, lane < HALF_HEADS), NEG, sizes)
        high = sizes.astype(BF).astype(F32)
        middle = (sizes - high).astype(BF).astype(F32)
        low = sizes - high - middle
        packed = high + pltpu.roll(middle, HALF_HEADS, 1) + pltpu.roll(low, 2 * HALF_HEADS, 1)
        out_ref[slot, TOK:QROWS, :] = jnp.zeros((QROWS - TOK, HALF), BF)
        out_ref[slot, TOK:QROWS, 0:TOK] = packed.T[0 : QROWS - TOK].astype(BF)

    own_kv = kv_in[0]
    fetch(0, 0)
    for g, out_ref in enumerate(outs):

        def one(i, carry, g=g, out_ref=out_ref):
            r = 2 * g + i

            @pl.when(r + 1 < readers)
            def _():
                fetch(r + 1, 1 - i)

            arrived(r, i)
            reader(r, i, out_ref)
            return carry

        lax.fori_loop(0, 2, one, 0)


def join_kernel(*refs):
    parts, outs = refs[:4], refs[4:]
    for r in range(2):
        sizes = []
        for p in parts:
            packed = p[r, TOK:QROWS, 0:TOK].astype(F32)
            packed = jnp.concatenate([packed, jnp.zeros((128 - (QROWS - TOK), TOK), F32)], axis=0).T
            sizes.append(packed + pltpu.roll(packed, 128 - HALF_HEADS, 1) + pltpu.roll(packed, 128 - 2 * HALF_HEADS, 1))
        top = functools.reduce(jnp.maximum, sizes)
        shares = [jnp.exp2(s - top) for s in sizes]
        total = functools.reduce(jnp.add, shares)
        shares = [s / total for s in shares]
        for h in range(HALF_HEADS):
            at = slice(h * 128, (h + 1) * 128)
            o = sum(s[:, h : h + 1] * p[r, 0:TOK, at].astype(F32) for s, p in zip(shares, parts, strict=True))
            outs[r][:, at] = o.astype(BF)


def place_kernel(me_ref, kept_ref, other_ref, out_ref, sems):
    core = me_ref[0] & 1
    copies = [
        pltpu.make_async_copy(half, to, sems.at[i])
        for i, (half, to) in enumerate(zip((kept_ref, other_ref), halves(core, (out_ref,)) + halves(1 - core, (out_ref,)), strict=True))
    ]
    for c in copies:
        c.start()
    for c in copies:
        c.wait()


def shape(*dims, dtype=BF):
    return jax.ShapeDtypeStruct(dims, dtype)


SMEM = pl.BlockSpec(memory_space=pltpu.SMEM)
VMEM = pl.BlockSpec(memory_space=pltpu.VMEM)
ANY = pl.BlockSpec(memory_space=pl.ANY)
HBM = pl.BlockSpec(memory_space=pltpu.HBM)


def room(mib):
    return pltpu.CompilerParams(vmem_limit_bytes=mib * 1024 * 1024)


def cost(flops, moved):
    return pl.CostEstimate(flops=int(flops), bytes_accessed=int(moved), transcendentals=0)


def in_hbm(*arrays):
    return tuple(pltpu.with_memory_space_constraint(a, pltpu.HBM) for a in arrays)


def hbm_shape(*dims, dtype=BF):
    return pltpu.HBM(dims, dtype)


def whole(*dims):
    return pl.BlockSpec(dims, lambda g: (0,) * len(dims))


def attend(name, me, queries, blocks):
    own = name == "attend_own"
    groups = len(queries)
    readers = 2 * groups
    first = VMEM if own else ANY
    return pl.pallas_call(
        functools.partial(attend_kernel, own, readers),
        out_shape=[shape(2, QROWS, HALF)] * groups,
        in_specs=[SMEM] + [ANY] * groups + [first] + [ANY] * (SIDE - 1),
        out_specs=[VMEM] * groups,
        scratch_shapes=[
            pltpu.VMEM((readers, QROWS, HALF), BF),
            pltpu.VMEM((2, LISTED, 2, BLK, HALF), BF),
            pltpu.VMEM((LISTED // 2 + 1, HALF_HEADS, TOK, 256), F32),
            pltpu.VMEM((HALF_HEADS, TOK, 128), F32),
            pltpu.VMEM((HALF_HEADS, TOK, 256), F32),
            pltpu.VMEM((8, 128), jnp.int32),
            pltpu.SMEM((8, 128), jnp.int32),
            pltpu.SMEM((readers, LISTED), jnp.int32),
            pltpu.SMEM((readers,), jnp.int32),
            pltpu.SemaphoreType.DMA((groups,)),
            pltpu.SemaphoreType.DMA,
            pltpu.SemaphoreType.DMA((2, LISTED)),
        ],
        compiler_params=room(24),
        cost_estimate=cost(readers * 4e8, 8e6),
    )(me, *queries, *blocks)


def layers(q_lin, k_lin, v_lin, q_soft, k_soft, v_soft, import_ids, import_counts):
    by_row, by_lane, tall, wide = (jnp.asarray(t) for t in feature_tables())
    me = lax.axis_index("files").astype(jnp.int32).reshape(1)
    place = lax.axis_index("seq").astype(jnp.int32).reshape(1)
    shards = lax.axis_size("seq")
    mine = (me, import_ids[0, 0], import_counts[0]) + in_hbm(k_soft[0], v_soft[0], q_soft[0])
    steps = (HEADS // GROUP,)
    lanes = GROUP * 128

    sent = pl.pallas_call(
        pack_kernel,
        name="pack",
        out_shape=shape(2 * TOK + QROWS, HALF),
        in_specs=[SMEM] * 3 + [HBM] * 3,
        out_specs=VMEM,
        scratch_shapes=[pltpu.SemaphoreType.DMA((3,))],
        compiler_params=room(4),
        cost_estimate=cost(0, 2e6),
    )(*mine)
    mate = swap_cores(sent)

    state, phi_k = pl.pallas_call(
        state_kernel,
        name="state",
        grid=steps,
        out_shape=[hbm_shape(HEADS, FROWS, 128), hbm_shape(HEADS, FROWS, TOK)],
        in_specs=[
            pl.BlockSpec((GROUP * FEAT, TOK), lambda g: (g, 0)),
            pl.BlockSpec((TOK, lanes), lambda g: (0, g)),
            whole(*by_row.shape),
            whole(*tall.shape),
        ],
        out_specs=[
            pl.BlockSpec((GROUP, FROWS, 128), lambda g: (g, 0, 0)),
            pl.BlockSpec((GROUP, FROWS, TOK), lambda g: (g, 0, 0)),
        ],
        compiler_params=room(12),
        cost_estimate=cost(1e9, 4e6),
    )(*in_hbm(k_lin[0].T, v_lin[0], by_row, tall))
    mate, state, phi_k = lax.optimization_barrier((mate, state, phi_k))

    kv, q = pl.pallas_call(
        pair_kernel,
        name="pair",
        out_shape=[shape(2, 2, TOK, HALF), shape(2, QROWS, HALF)],
        in_specs=[SMEM] * 3 + [HBM] * 3 + [VMEM],
        out_specs=[VMEM] * 2,
        scratch_shapes=[pltpu.SemaphoreType.DMA((3,))],
        compiler_params=room(8),
        cost_estimate=cost(0, 4e6),
    )(*mine, mate)
    kv_right = move(kv, "kv", -1)
    kv_left = move(kv, "kv", 1)
    q_left = move(q, "q", 1)
    q_right = move(q, "q", -1)
    kv_far = move(kv_right, "kv", -1)
    q_far = move(q_left, "q", 1)

    slices = lax.all_to_all(state.reshape(shards, HEADS * FROWS // shards, 128), "seq", 0, 0, tiled=True)

    num, den, phi = pl.pallas_call(
        local_kernel,
        name="local",
        grid=steps,
        out_shape=[hbm_shape(TOK, D, dtype=F32), hbm_shape(TOK, HEADS // GROUP * 128, dtype=F32), hbm_shape(HEADS, TOK, FPAD)],
        in_specs=[
            pl.BlockSpec((GROUP * FEAT, TOK), lambda g: (g, 0)),
            pl.BlockSpec((GROUP, FROWS, TOK), lambda g: (g, 0, 0)),
            pl.BlockSpec((TOK, lanes), lambda g: (0, g)),
            whole(*by_lane.shape),
            whole(*wide.shape),
        ],
        out_specs=[
            pl.BlockSpec((TOK, lanes), lambda g: (0, g)),
            pl.BlockSpec((TOK, 128), lambda g: (0, g)),
            pl.BlockSpec((GROUP, TOK, FPAD), lambda g: (g, 0, 0)),
        ],
        compiler_params=room(16),
        cost_estimate=cost(4e9, 8e6),
    )(*in_hbm(q_lin[0].T, phi_k, v_lin[0], by_lane, wide))
    slices, num, den, phi = lax.optimization_barrier((slices, num, den, phi))

    prefix = pl.pallas_call(
        prefix_kernel,
        name="prefix",
        out_shape=shape(*slices.shape),
        in_specs=[SMEM, VMEM],
        out_specs=VMEM,
        compiler_params=room(8),
        cost_estimate=cost(0, 2e6),
    )(place, slices)
    before = lax.all_to_all(prefix, "seq", 0, 0, tiled=True).reshape(HEADS, FROWS, 128)

    blocks = (kv, kv_right, kv_far, kv_left)
    (to_far,) = attend("attend_far", me, (q_far,), blocks)
    to_far, q_left, q_right = lax.optimization_barrier((to_far, q_left, q_right))
    from_far = move(to_far, "q", 2)
    to_left, to_right = attend("attend_sides", me, (q_left, q_right), blocks)
    from_right = move(to_left, "q", -1)
    from_left = move(to_right, "q", 1)
    (here,) = attend("attend_own", me, (q,), blocks)
    kept, send = pl.pallas_call(
        join_kernel,
        name="join",
        out_shape=[shape(TOK, HALF)] * 2,
        in_specs=[VMEM] * 4,
        out_specs=[VMEM] * 2,
        compiler_params=room(8),
        cost_estimate=cost(0, 4e6),
    )(here, from_right, from_left, from_far)
    other = swap_cores(send)
    soft_out = pl.pallas_call(
        place_kernel,
        name="place",
        out_shape=shape(TOK, SM_W),
        in_specs=[SMEM, VMEM, VMEM],
        out_specs=HBM,
        scratch_shapes=[pltpu.SemaphoreType.DMA((2,))],
        compiler_params=room(4),
        cost_estimate=cost(0, 1e6),
    )(me, kept, other)

    lin_out = pl.pallas_call(
        finish_kernel,
        name="finish",
        grid=steps,
        out_shape=shape(TOK, D),
        in_specs=[
            pl.BlockSpec((TOK, lanes), lambda g: (0, g)),
            pl.BlockSpec((TOK, 128), lambda g: (0, g)),
            pl.BlockSpec((GROUP, TOK, FPAD), lambda g: (g, 0, 0)),
            pl.BlockSpec((GROUP, FROWS, 128), lambda g: (g, 0, 0)),
        ],
        out_specs=pl.BlockSpec((TOK, lanes), lambda g: (0, g)),
        compiler_params=room(16),
        cost_estimate=cost(4e8, 8e6),
    )(*in_hbm(num, den, phi), before)
    return lin_out[None], soft_out[None]


def solution(mesh):
    wide = P("files", "seq", None)
    return jax.shard_map(
        layers,
        mesh=mesh,
        in_specs=(wide,) * 7 + (P("files", "seq"),),
        out_specs=(wide, wide),
        check_vma=False,
    )
```

```python
import functools
import math

import jax
import jax.numpy as jnp
import numpy as np
from jax import lax
from jax.experimental import pallas as pl
from jax.experimental.pallas import tpu as pltpu
from jax.sharding import PartitionSpec as P

D = 2560
HEADS = 20
FEAT = 16
FEATS = 153
FROWS = 160
FPAD = 256
SM_HD = 128
SM_W = 1280
BLK = 128
TOK = 256
LISTED = 8
GROUP = 4
HALF = 640
HALF_HEADS = 5
QROWS = 272
SIDE = 4
CORES = 2

inv_root_two = 0.7071067811865476
TO_LOG2 = math.log2(math.e) / math.sqrt(SM_HD)
NEG = -1e30
BF = jnp.bfloat16
F32 = jnp.float32
NT = (((1,), (1,)), ((), ()))


def along(what, step):
    pairs = []
    for x in range(SIDE):
        for y in range(SIDE):
            for c in range(CORES):
                on_x = (c == 0) == (what == "kv")
                x2 = (x + step) % SIDE if on_x else x
                y2 = y if on_x else (y + step) % SIDE
                pairs.append(((x * SIDE + y) * CORES + c, (x2 * SIDE + y2) * CORES + c))
    return pairs


def move(a, what, step):
    return lax.ppermute(a, "files", along(what, step))


def swap_cores(a):
    return lax.ppermute(a, "files", [(i, i ^ 1) for i in range(SIDE * SIDE * CORES)])


def feature_tables():
    rows, cols = np.triu_indices(FEAT)
    select = np.zeros((GROUP, 2, FROWS, GROUP * FEAT), np.float32)
    for j in range(GROUP):
        for f in range(FEAT):
            select[j, 0, 1 + f, j * FEAT + f] = 0.5
        for n in range(len(rows)):
            select[j, 0, 1 + FEAT + n, j * FEAT + rows[n]] = 0.5
            select[j, 1, 1 + FEAT + n, j * FEAT + cols[n]] = 0.5
    vectors = np.zeros((3, FROWS), np.float32)
    vectors[0, 0] = 1.0
    vectors[1, : 1 + FEAT] = 1.0
    vectors[2, :FEATS] = 1.0
    vectors[2, 1 + FEAT : FEATS] = np.where(rows == cols, inv_root_two, 1.0).astype(np.float32)
    vectors = np.ascontiguousarray(np.broadcast_to(vectors[:, :, None], (3, FROWS, 128)))
    return select.reshape(GROUP, 2 * FROWS, GROUP * FEAT).astype(jnp.bfloat16), vectors


def column(j):
    return slice(j * 128, (j + 1) * 128)


def features(select, x, vectors):
    first, second, factor = (jnp.concatenate([vectors[i], vectors[i]], axis=1) for i in range(3))
    ab = jnp.dot(select, x, preferred_element_type=F32)
    return ((ab[:FROWS] + first) * (ab[FROWS:] + second) * factor).astype(BF)


def taller(phi):
    return jnp.concatenate([phi, jnp.zeros((FPAD - FROWS, phi.shape[1]), BF)], axis=0)


def with_ones(values):
    return jnp.concatenate([values, jnp.ones(values.shape, BF)], axis=1)


def state_kernel(k_ref, v_ref, select_ref, vector_ref, out_ref):
    row = lax.broadcasted_iota(jnp.int32, (16, 128), 0)
    lane = lax.broadcasted_iota(jnp.int32, (FROWS, 128), 1)
    norms = jnp.zeros((FROWS, 128), F32)
    for j in range(GROUP):
        phi = features(select_ref[j], k_ref[...], vector_ref)
        both = jnp.dot(phi, with_ones(v_ref[:, column(j)]), preferred_element_type=F32)
        norms = jnp.where(lane == j, both[:, 128:], norms)
        out_ref[j] = both[:, :128].astype(BF)
    flat = jnp.concatenate([norms, jnp.zeros((FPAD - FROWS, 128), F32)], axis=0).T
    high = flat.astype(BF).astype(F32)
    low = flat - high
    at = row + (FROWS - 16 - FEATS)
    for j in range(GROUP):
        tail = out_ref[j, FROWS - 16 :].astype(F32)
        pieces = (high[j : j + 1, :128], high[j : j + 1, 128:], low[j : j + 1, :128], low[j : j + 1, 128:])
        for i, piece in enumerate(pieces):
            tail = jnp.where(at == i, piece, tail)
        out_ref[j, FROWS - 16 :] = tail.astype(BF)


def prefix_kernel(place_ref, in_ref, out_ref):
    rows = in_ref.shape[1]
    row = lax.broadcasted_iota(jnp.int32, (rows, 128), 0) + (place_ref[0] & 1) * (FROWS // 2)
    row = jnp.where(row >= FROWS, row - FROWS, row)
    row = jnp.where(row >= FROWS, row - FROWS, row)
    high = (row == FEATS) | (row == FEATS + 1)
    low = (row == FEATS + 2) | (row == FEATS + 3)
    total = jnp.zeros((rows, 128), F32)
    for z in range(in_ref.shape[0]):
        both = total + pltpu.roll(total, rows - 2, 0)
        top = both.astype(BF).astype(F32)
        rest = pltpu.roll(both - top, 2, 0)
        out_ref[z] = jnp.where(high, top, jnp.where(low, rest, total)).astype(BF)
        total = total + in_ref[z].astype(F32)


def local_kernel(q_ref, k_ref, v_ref, select_ref, vector_ref, num_ref, den_ref, phi_ref):
    causal = lax.broadcasted_iota(jnp.int32, (TOK, TOK), 0) >= lax.broadcasted_iota(jnp.int32, (TOK, TOK), 1)
    lane = lax.broadcasted_iota(jnp.int32, (TOK, 128), 1)
    group = pl.program_id(0)

    @pl.when(group == 0)
    def _():
        den_ref[...] = jnp.zeros((TOK, 128), F32)

    den = den_ref[...]
    for j in range(GROUP):
        phi_q = features(select_ref[j], q_ref[...], vector_ref)
        phi_ref[j] = phi_q
        phi_k = features(select_ref[j], k_ref[...], vector_ref)
        weight = jnp.dot(taller(phi_q).T, taller(phi_k), preferred_element_type=F32)
        weight = jnp.where(causal, weight, 0.0).astype(BF)
        both = jnp.dot(weight, with_ones(v_ref[:, column(j)]), preferred_element_type=F32)
        num_ref[:, column(j)] = both[:, :128].astype(BF)
        den = jnp.where(lane == group * GROUP + j, both[:, 128:], den)
    den_ref[...] = den


def finish_kernel(num_ref, den_ref, phi_ref, state_ref, out_ref):
    lane = lax.broadcasted_iota(jnp.int32, (TOK, 128), 1)
    group = pl.program_id(0)
    at = FEATS - (FROWS - 16)
    for j in range(GROUP):
        phi = taller(phi_ref[j]).T
        state = state_ref[j]
        carried = jnp.dot(phi, taller(state), preferred_element_type=F32)
        tail = state[FROWS - 16 : FROWS].astype(F32)
        n0 = tail[at : at + 1] + tail[at + 2 : at + 3]
        n1 = tail[at + 1 : at + 2] + tail[at + 3 : at + 4]
        phi32 = phi.astype(F32)
        den = jnp.where(lane == group * GROUP + j, den_ref[...], 0.0) + phi32[:, :128] * n0 + phi32[:, 128:] * n1
        den = jnp.sum(den, axis=1, keepdims=True)
        out_ref[:, column(j)] = ((num_ref[:, column(j)].astype(F32) + carried) / den).astype(BF)


def halves(core, refs):
    at = pl.ds(pl.multiple_of(core * HALF, 128), HALF)
    return [r.at[:, at] for r in refs]


def listed_rows(ids_ref, count_ref):
    lane = lax.broadcasted_iota(jnp.int32, (QROWS - TOK, HALF), 1)
    listed = jnp.full((QROWS - TOK, HALF), -1.0, F32)
    for i in range(LISTED):
        entry = jnp.where(i < count_ref[0], ids_ref[i], -1).astype(F32)
        listed = jnp.where(lane == i, entry, listed)
    return listed.astype(BF)


def pack_kernel(me_ref, ids_ref, count_ref, k_ref, v_ref, q_ref, out_ref, sems):
    copies = [
        pltpu.make_async_copy(half, out_ref.at[pl.ds(i * TOK, TOK)], sems.at[i])
        for i, half in enumerate(halves(1 - (me_ref[0] & 1), (k_ref, v_ref, q_ref)))
    ]
    for c in copies:
        c.start()
    out_ref[3 * TOK :] = listed_rows(ids_ref, count_ref)
    for c in copies:
        c.wait()


def pair_kernel(me_ref, ids_ref, count_ref, k_ref, v_ref, q_ref, mate_ref, kv_ref, both_ref, sems):
    targets = (kv_ref.at[0, 0], kv_ref.at[0, 1], both_ref.at[0, pl.ds(0, TOK)])
    copies = [
        pltpu.make_async_copy(half, to, sems.at[i])
        for i, (half, to) in enumerate(zip(halves(me_ref[0] & 1, (k_ref, v_ref, q_ref)), targets, strict=True))
    ]
    for c in copies:
        c.start()
    both_ref[0, TOK:QROWS] = listed_rows(ids_ref, count_ref)
    kv_ref[1, 0] = mate_ref[0:TOK]
    kv_ref[1, 1] = mate_ref[TOK : 2 * TOK]
    both_ref[1] = mate_ref[2 * TOK :]
    for c in copies:
        c.wait()


def search_kernel(me_ref, *refs):
    q_in, (found_ref, count_ref, wanted, ids, sems) = refs[:SIDE], refs[SIDE:]
    me = me_ref[0]
    core, y, x = me & 1, (me >> 1) & (SIDE - 1), me >> 3
    rows = pl.ds(TOK, QROWS - TOK)
    copies = [
        pltpu.make_async_copy(q_in[i].at[:, rows, pl.ds(0, 128)], ids.at[pl.ds(2 * i, 2)], sems.at[i]) for i in range(SIDE)
    ]
    for c in copies:
        c.start()
    for c in copies:
        c.wait()
    for r in range(2 * SIDE):
        wanted[r : r + 1] = ids[r].astype(F32).astype(jnp.int32)[0:1]
    pltpu.async_copy(wanted, found_ref, sems.at[SIDE]).wait()

    def search(r, carry):
        count = jnp.int32(0)
        for i in range(LISTED):
            entry = found_ref[r, i]
            xo, yo, co = entry >> 4, (entry >> 2) & (SIDE - 1), (entry >> 1) & 1
            mine = (entry >= 0) & jnp.where(core == 0, yo == y, xo == x)
            away = jnp.where(core == 0, xo - x, yo - y) & (SIDE - 1)
            found_ref[r, count] = (away * 2 + (co ^ core)) * 2 + (entry & 1)
            count = count + mine.astype(jnp.int32)
        count_ref[r] = count
        return carry

    lax.fori_loop(0, 2 * SIDE, search, 0)


def attend_kernel(own, base, readers, found, counts, *refs):
    groups = readers // 2
    q_in, kv_in, outs = refs[:groups], refs[groups : groups + SIDE], refs[groups + SIDE : readers + SIDE]
    q_buf, g_buf, s_buf, m_buf, a_buf, q_sems, g_sems = refs[readers + SIDE :]
    copies = [pltpu.make_async_copy(q_in[i], q_buf.at[pl.ds(2 * i, 2)], q_sems.at[i]) for i in range(groups)]
    for c in copies:
        c.start()
    lane = lax.broadcasted_iota(jnp.int32, (TOK, 128), 1)
    heads = [(h, slice(h * 128, (h + 1) * 128)) for h in range(HALF_HEADS)]

    def fetch(r, slot):
        def one(i, carry):
            code = found[base + r, i]
            rows = pl.ds(pl.multiple_of((code & 1) * BLK, BLK), BLK)
            for away in range(SIDE):

                @pl.when((code >> 2) == away)
                def _():
                    source = kv_in[away].at[(code >> 1) & 1, :, rows, :]
                    pltpu.make_async_copy(source, g_buf.at[slot, i], g_sems.at[slot, i]).start()

            return carry

        lax.fori_loop(0, counts[base + r], one, 0)

    def arrived(r, slot):
        def one(i, carry):
            source = kv_in[0].at[0, :, pl.ds(0, BLK), :]
            pltpu.make_async_copy(source, g_buf.at[slot, i], g_sems.at[slot, i]).wait()
            return carry

        lax.fori_loop(0, counts[base + r], one, 0)

    def blank(slot, i):
        g_buf[slot, i, 1] = jnp.zeros((BLK, HALF), BF)

    def reader(r, slot, out_ref):
        count = counts[base + r]
        pairs = (count + 1) >> 1

        @pl.when((count & 1) == 1)
        def _():
            blank(slot, count)

        if not own:

            @pl.when(count == 0)
            def _():
                blank(slot, 0)
                blank(slot, 1)

        def blocks(j, kind, at):
            return jnp.concatenate([g_buf[slot, 2 * j, kind, :, at], g_buf[slot, 2 * j + 1, kind, :, at]], axis=0)

        def score(j, fresh):
            for h, at in heads:
                s = lax.dot_general(q_buf[r, 0:TOK, at], blocks(j, 0, at), NT, preferred_element_type=F32)
                s0, s1 = s[:, :128], jnp.where(2 * j + 1 < count, s[:, 128:], NEG)
                if fresh:
                    s0 = jnp.where(count > 0, s0, NEG)
                s_buf[j, h, :, 0:128] = s0
                s_buf[j, h, :, 128:256] = s1
                m = jnp.maximum(s0, s1)
                m_buf[h] = m if fresh else jnp.maximum(m_buf[h], m)

        def weigh(j, fresh):
            for h, at in heads:
                m = m_buf[h]
                p = jnp.exp2(s_buf[j, h] * TO_LOG2 - jnp.concatenate([m, m], axis=1)).astype(BF)
                a = jnp.dot(p, with_ones(blocks(j, 1, at)), preferred_element_type=F32)
                a_buf[h] = a if fresh else a_buf[h] + a

        if own:
            for h, at in heads:
                parts = []
                for b in range(2):
                    rows = slice(b * BLK, (b + 1) * BLK)
                    k = own_kv[r, 0, rows, at]
                    parts.append(lax.dot_general(q_buf[r, rows, at], k, NT, preferred_element_type=F32))
                s = jnp.concatenate(parts, axis=0)
                s_buf[LISTED // 2, h, :, 0:128] = s
                m_buf[h] = s
        else:
            score(0, True)
        start = 0 if own else 1

        def more_scores(j, carry):
            score(j, False)
            return carry

        lax.fori_loop(start, pairs, more_scores, 0)
        tops = jnp.zeros((TOK, 128), F32)
        for h, at in heads:
            m = jnp.broadcast_to(jnp.max(m_buf[h], axis=1, keepdims=True) * TO_LOG2, (TOK, 128))
            m_buf[h] = m
            tops = jnp.where(lane == h, m, tops)
        if own:
            for h, at in heads:
                p = jnp.exp2(s_buf[LISTED // 2, h, :, 0:128] * TO_LOG2 - m_buf[h]).astype(BF)
                parts = []
                for b in range(2):
                    rows = slice(b * BLK, (b + 1) * BLK)
                    v = with_ones(own_kv[r, 1, rows, at])
                    parts.append(jnp.dot(p[rows], v, preferred_element_type=F32))
                a_buf[h] = jnp.concatenate(parts, axis=0)
        else:
            weigh(0, True)

        def more_weights(j, carry):
            weigh(j, False)
            return carry

        lax.fori_loop(start, pairs, more_weights, 0)
        totals = jnp.ones((TOK, 128), F32)
        for h, at in heads:
            total = a_buf[h, :, 128:]
            out_ref[slot, 0:TOK, at] = (a_buf[h, :, :128] / total).astype(BF)
            totals = jnp.where(lane == h, total, totals)
        sizes = tops + jnp.log2(totals)
        if not own:
            sizes = jnp.where(jnp.logical_and(count == 0, lane < HALF_HEADS), NEG, sizes)
        high = sizes.astype(BF).astype(F32)
        middle = (sizes - high).astype(BF).astype(F32)
        low = sizes - high - middle
        packed = high + pltpu.roll(middle, HALF_HEADS, 1) + pltpu.roll(low, 2 * HALF_HEADS, 1)
        out_ref[slot, TOK:QROWS, :] = jnp.zeros((QROWS - TOK, HALF), BF)
        out_ref[slot, TOK:QROWS, 0:TOK] = packed.T[0 : QROWS - TOK].astype(BF)

    own_kv = kv_in[0]
    fetch(0, 0)
    for c in copies:
        c.wait()
    for g, out_ref in enumerate(outs):

        def one(i, carry, g=g, out_ref=out_ref):
            r = 2 * g + i

            @pl.when(r + 1 < readers)
            def _():
                fetch(r + 1, 1 - i)

            arrived(r, i)
            reader(r, i, out_ref)
            return carry

        lax.fori_loop(0, 2, one, 0)


def join_kernel(*refs):
    parts, outs = refs[:4], refs[4:]
    for r in range(2):
        sizes = []
        for p in parts:
            packed = p[r, TOK:QROWS, 0:TOK].astype(F32)
            packed = jnp.concatenate([packed, jnp.zeros((128 - (QROWS - TOK), TOK), F32)], axis=0).T
            sizes.append(packed + pltpu.roll(packed, 128 - HALF_HEADS, 1) + pltpu.roll(packed, 128 - 2 * HALF_HEADS, 1))
        top = functools.reduce(jnp.maximum, sizes)
        shares = [jnp.exp2(s - top) for s in sizes]
        total = functools.reduce(jnp.add, shares)
        shares = [s / total for s in shares]
        for h in range(HALF_HEADS):
            at = slice(h * 128, (h + 1) * 128)
            o = sum(s[:, h : h + 1] * p[r, 0:TOK, at].astype(F32) for s, p in zip(shares, parts, strict=True))
            outs[r][:, at] = o.astype(BF)


def place_kernel(me_ref, kept_ref, other_ref, out_ref, sems):
    core = me_ref[0] & 1
    copies = [
        pltpu.make_async_copy(half, to, sems.at[i])
        for i, (half, to) in enumerate(zip((kept_ref, other_ref), halves(core, (out_ref,)) + halves(1 - core, (out_ref,)), strict=True))
    ]
    for c in copies:
        c.start()
    for c in copies:
        c.wait()


def shape(*dims, dtype=BF):
    return jax.ShapeDtypeStruct(dims, dtype)


SMEM = pl.BlockSpec(memory_space=pltpu.SMEM)
VMEM = pl.BlockSpec(memory_space=pltpu.VMEM)
ANY = pl.BlockSpec(memory_space=pl.ANY)
HBM = pl.BlockSpec(memory_space=pltpu.HBM)


def room(mib):
    return pltpu.CompilerParams(vmem_limit_bytes=mib * 1024 * 1024)


def cost(flops, moved):
    return pl.CostEstimate(flops=int(flops), bytes_accessed=int(moved), transcendentals=0)


def in_hbm(*arrays):
    return tuple(pltpu.with_memory_space_constraint(a, pltpu.HBM) for a in arrays)


def hbm_shape(*dims, dtype=BF):
    return pltpu.HBM(dims, dtype)


def whole(*dims):
    return pl.BlockSpec(dims, lambda g: (0,) * len(dims))


def attend(name, base, lists, queries, blocks):
    own = name == "attend_own"
    groups = len(queries)
    readers = 2 * groups
    first = VMEM if own else ANY
    return pl.pallas_call(
        functools.partial(attend_kernel, own, base, readers),
        out_shape=[shape(2, QROWS, HALF)] * groups,
        in_specs=[SMEM, SMEM] + [ANY] * groups + [first] + [ANY] * (SIDE - 1),
        out_specs=[VMEM] * groups,
        scratch_shapes=[
            pltpu.VMEM((readers, QROWS, HALF), BF),
            pltpu.VMEM((2, LISTED, 2, BLK, HALF), BF),
            pltpu.VMEM((LISTED // 2 + 1, HALF_HEADS, TOK, 256), F32),
            pltpu.VMEM((HALF_HEADS, TOK, 128), F32),
            pltpu.VMEM((HALF_HEADS, TOK, 256), F32),
            pltpu.SemaphoreType.DMA((groups,)),
            pltpu.SemaphoreType.DMA((2, LISTED)),
        ],
        compiler_params=room(20),
        cost_estimate=cost(readers * 4e8, 8e6),
    )(*lists, *queries, *blocks)


def layers(q_lin, k_lin, v_lin, q_soft, k_soft, v_soft, import_ids, import_counts):
    select, vectors = (jnp.asarray(t) for t in feature_tables())
    me = lax.axis_index("files").astype(jnp.int32).reshape(1)
    place = lax.axis_index("seq").astype(jnp.int32).reshape(1)
    shards = lax.axis_size("seq")
    steps = (HEADS // GROUP,)
    heads16 = pl.BlockSpec((GROUP * FEAT, TOK), lambda g: (g, 0))
    heads128 = pl.BlockSpec((TOK, GROUP * 128), lambda g: (0, g))
    mine = (me, import_ids[0, 0], import_counts[0]) + in_hbm(k_soft[0], v_soft[0], q_soft[0])

    sent = pl.pallas_call(
        pack_kernel,
        name="pack",
        out_shape=shape(2 * TOK + QROWS, HALF),
        in_specs=[SMEM] * 3 + [HBM] * 3,
        out_specs=VMEM,
        scratch_shapes=[pltpu.SemaphoreType.DMA((3,))],
        compiler_params=room(4),
        cost_estimate=cost(0, 2e6),
    )(*mine)
    mate = swap_cores(sent)

    state = pl.pallas_call(
        state_kernel,
        name="state",
        grid=steps,
        out_shape=hbm_shape(HEADS, FROWS, 128),
        in_specs=[heads16, heads128, whole(*select.shape), whole(*vectors.shape)],
        out_specs=pl.BlockSpec((GROUP, FROWS, 128), lambda g: (g, 0, 0)),
        compiler_params=room(12),
        cost_estimate=cost(1e9, 4e6),
    )(*in_hbm(k_lin[0].T, v_lin[0], select, vectors))
    mate, state = lax.optimization_barrier((mate, state))

    kv, q = pl.pallas_call(
        pair_kernel,
        name="pair",
        out_shape=[shape(2, 2, TOK, HALF), shape(2, QROWS, HALF)],
        in_specs=[SMEM] * 3 + [HBM] * 3 + [VMEM],
        out_specs=[VMEM] * 2,
        scratch_shapes=[pltpu.SemaphoreType.DMA((3,))],
        compiler_params=room(8),
        cost_estimate=cost(0, 4e6),
    )(*mine, mate)
    kv_right = move(kv, "kv", -1)
    kv_left = move(kv, "kv", 1)
    q_left = move(q, "q", 1)
    q_right = move(q, "q", -1)
    kv_far = move(kv_right, "kv", -1)
    q_far = move(q_left, "q", 1)

    slices = lax.all_to_all(state.reshape(shards, HEADS * FROWS // shards, 128), "seq", 0, 0, tiled=True)

    num, den, phi = pl.pallas_call(
        local_kernel,
        name="local",
        grid=steps,
        out_shape=[hbm_shape(TOK, D), hbm_shape(TOK, 128, dtype=F32), hbm_shape(HEADS, FROWS, TOK)],
        in_specs=[heads16, heads16, heads128, whole(*select.shape), whole(*vectors.shape)],
        out_specs=[heads128, whole(TOK, 128), pl.BlockSpec((GROUP, FROWS, TOK), lambda g: (g, 0, 0))],
        compiler_params=room(16),
        cost_estimate=cost(4e9, 8e6),
    )(*in_hbm(q_lin[0].T, k_lin[0].T, v_lin[0], select, vectors))
    slices, num, den, phi = lax.optimization_barrier((slices, num, den, phi))

    prefix = pl.pallas_call(
        prefix_kernel,
        name="prefix",
        out_shape=hbm_shape(*slices.shape),
        in_specs=[SMEM, VMEM],
        out_specs=VMEM,
        compiler_params=room(8),
        cost_estimate=cost(0, 2e6),
    )(place, slices)
    before = lax.all_to_all(prefix, "seq", 0, 0, tiled=True).reshape(HEADS, FROWS, 128)

    blocks = (kv, kv_right, kv_far, kv_left)
    lists = pl.pallas_call(
        search_kernel,
        name="search",
        out_shape=[shape(2 * SIDE, 128, dtype=jnp.int32), shape(2 * SIDE, dtype=jnp.int32)],
        in_specs=[SMEM] + [ANY] * SIDE,
        out_specs=[SMEM] * 2,
        scratch_shapes=[
            pltpu.VMEM((2 * SIDE, 128), jnp.int32),
            pltpu.VMEM((2 * SIDE, QROWS - TOK, 128), BF),
            pltpu.SemaphoreType.DMA((SIDE + 1,)),
        ],
        compiler_params=room(2),
        cost_estimate=cost(0, 1e5),
    )(me, q_far, q_left, q_right, q)
    (to_far,) = attend("attend_far", 0, lists, (q_far,), blocks)
    to_far, q_left, q_right = lax.optimization_barrier((to_far, q_left, q_right))
    from_far = move(to_far, "q", 2)
    to_left, to_right = attend("attend_sides", 2, lists, (q_left, q_right), blocks)
    from_right = move(to_left, "q", -1)
    from_left = move(to_right, "q", 1)
    (here,) = attend("attend_own", 6, lists, (q,), blocks)
    kept, send = pl.pallas_call(
        join_kernel,
        name="join",
        out_shape=[shape(TOK, HALF)] * 2,
        in_specs=[VMEM] * 4,
        out_specs=[VMEM] * 2,
        compiler_params=room(8),
        cost_estimate=cost(0, 4e6),
    )(here, from_right, from_left, from_far)
    other = swap_cores(send)
    soft_out = pl.pallas_call(
        place_kernel,
        name="place",
        out_shape=shape(TOK, SM_W),
        in_specs=[SMEM, VMEM, VMEM],
        out_specs=HBM,
        scratch_shapes=[pltpu.SemaphoreType.DMA((2,))],
        compiler_params=room(4),
        cost_estimate=cost(0, 1e6),
    )(me, kept, other)

    lin_out = pl.pallas_call(
        finish_kernel,
        name="finish",
        grid=steps,
        out_shape=shape(TOK, D),
        in_specs=[
            heads128,
            whole(TOK, 128),
            pl.BlockSpec((GROUP, FROWS, TOK), lambda g: (g, 0, 0)),
            pl.BlockSpec((GROUP, FROWS, 128), lambda g: (g, 0, 0)),
        ],
        out_specs=heads128,
        compiler_params=room(16),
        cost_estimate=cost(4e8, 8e6),
    )(*in_hbm(num, den, phi), before)
    return lin_out[None], soft_out[None]


def solution(mesh):
    wide = P("files", "seq", None)
    return jax.shard_map(
        layers,
        mesh=mesh,
        in_specs=(wide,) * 7 + (P("files", "seq"),),
        out_specs=(wide, wide),
        check_vma=False,
    )
```

```python
import functools
import math

import jax
import jax.numpy as jnp
import numpy as np
from jax import lax
from jax.experimental import pallas as pl
from jax.experimental.pallas import tpu as pltpu
from jax.sharding import PartitionSpec as P

D = 2560
HEADS = 20
FEAT = 16
FEATS = 153
FROWS = 160
FPAD = 256
SM_HD = 128
SM_W = 1280
BLK = 128
TOK = 256
LISTED = 8
GROUP = 4
HALF = 640
HALF_HEADS = 5
QROWS = 272
SIDE = 4
CORES = 2

inv_root_two = 0.7071067811865476
TO_LOG2 = math.log2(math.e) / math.sqrt(SM_HD)
NEG = -1e30
BF = jnp.bfloat16
F32 = jnp.float32
NT = (((1,), (1,)), ((), ()))


def along(what, step):
    pairs = []
    for x in range(SIDE):
        for y in range(SIDE):
            for c in range(CORES):
                on_x = (c == 0) == (what == "kv")
                x2 = (x + step) % SIDE if on_x else x
                y2 = y if on_x else (y + step) % SIDE
                pairs.append(((x * SIDE + y) * CORES + c, (x2 * SIDE + y2) * CORES + c))
    return pairs


def move(a, what, step):
    return lax.ppermute(a, "files", along(what, step))


def swap_cores(a):
    return lax.ppermute(a, "files", [(i, i ^ 1) for i in range(SIDE * SIDE * CORES)])


def feature_tables():
    rows, cols = np.triu_indices(FEAT)
    select = np.zeros((GROUP, 2, FROWS, GROUP * FEAT), np.float32)
    for j in range(GROUP):
        for f in range(FEAT):
            select[j, 0, 1 + f, j * FEAT + f] = 0.5
        for n in range(len(rows)):
            select[j, 0, 1 + FEAT + n, j * FEAT + rows[n]] = 0.5
            select[j, 1, 1 + FEAT + n, j * FEAT + cols[n]] = 0.5
    vectors = np.zeros((3, FROWS), np.float32)
    vectors[0, 0] = 1.0
    vectors[1, : 1 + FEAT] = 1.0
    vectors[2, :FEATS] = 1.0
    vectors[2, 1 + FEAT : FEATS] = np.where(rows == cols, inv_root_two, 1.0).astype(np.float32)
    vectors = np.ascontiguousarray(np.broadcast_to(vectors[:, :, None], (3, FROWS, 128)))
    return select.reshape(GROUP, 2 * FROWS, GROUP * FEAT).astype(jnp.bfloat16), vectors


def column(j):
    return slice(j * 128, (j + 1) * 128)


def features(select, x, vectors):
    first, second, factor = (jnp.concatenate([vectors[i], vectors[i]], axis=1) for i in range(3))
    ab = jnp.dot(select, x, preferred_element_type=F32)
    return ((ab[:FROWS] + first) * (ab[FROWS:] + second) * factor).astype(BF)


def taller(phi):
    return jnp.concatenate([phi, jnp.zeros((FPAD - FROWS, phi.shape[1]), BF)], axis=0)


def with_ones(values):
    return jnp.concatenate([values, jnp.ones(values.shape, BF)], axis=1)


def state_kernel(k_ref, v_ref, select_ref, vector_ref, out_ref):
    row = lax.broadcasted_iota(jnp.int32, (16, 128), 0)
    lane = lax.broadcasted_iota(jnp.int32, (FROWS, 128), 1)
    norms = jnp.zeros((FROWS, 128), F32)
    for j in range(GROUP):
        phi = features(select_ref[j], k_ref[...], vector_ref)
        both = jnp.dot(phi, with_ones(v_ref[:, column(j)]), preferred_element_type=F32)
        norms = jnp.where(lane == j, both[:, 128:], norms)
        out_ref[j] = both[:, :128].astype(BF)
    flat = jnp.concatenate([norms, jnp.zeros((FPAD - FROWS, 128), F32)], axis=0).T
    high = flat.astype(BF).astype(F32)
    low = flat - high
    at = row + (FROWS - 16 - FEATS)
    for j in range(GROUP):
        tail = out_ref[j, FROWS - 16 :].astype(F32)
        pieces = (high[j : j + 1, :128], high[j : j + 1, 128:], low[j : j + 1, :128], low[j : j + 1, 128:])
        for i, piece in enumerate(pieces):
            tail = jnp.where(at == i, piece, tail)
        out_ref[j, FROWS - 16 :] = tail.astype(BF)


def prefix_kernel(place_ref, in_ref, out_ref):
    rows = in_ref.shape[1]
    row = lax.broadcasted_iota(jnp.int32, (rows, 128), 0) + (place_ref[0] & 1) * (FROWS // 2)
    row = jnp.where(row >= FROWS, row - FROWS, row)
    row = jnp.where(row >= FROWS, row - FROWS, row)
    high = (row == FEATS) | (row == FEATS + 1)
    low = (row == FEATS + 2) | (row == FEATS + 3)
    total = jnp.zeros((rows, 128), F32)
    for z in range(in_ref.shape[0]):
        both = total + pltpu.roll(total, rows - 2, 0)
        top = both.astype(BF).astype(F32)
        rest = pltpu.roll(both - top, 2, 0)
        out_ref[z] = jnp.where(high, top, jnp.where(low, rest, total)).astype(BF)
        total = total + in_ref[z].astype(F32)


def local_kernel(q_ref, k_ref, v_ref, select_ref, vector_ref, num_ref, den_ref, phi_ref):
    causal = lax.broadcasted_iota(jnp.int32, (TOK, TOK), 0) >= lax.broadcasted_iota(jnp.int32, (TOK, TOK), 1)
    lane = lax.broadcasted_iota(jnp.int32, (TOK, 128), 1)
    group = pl.program_id(0)

    @pl.when(group == 0)
    def _():
        den_ref[...] = jnp.zeros((TOK, 128), F32)

    den = den_ref[...]
    for j in range(GROUP):
        phi_q = features(select_ref[j], q_ref[...], vector_ref)
        phi_ref[j] = phi_q
        phi_k = features(select_ref[j], k_ref[...], vector_ref)
        weight = jnp.dot(taller(phi_q).T, taller(phi_k), preferred_element_type=F32)
        weight = jnp.where(causal, weight, 0.0).astype(BF)
        both = jnp.dot(weight, with_ones(v_ref[:, column(j)]), preferred_element_type=F32)
        num_ref[:, column(j)] = both[:, :128].astype(BF)
        den = jnp.where(lane == group * GROUP + j, both[:, 128:], den)
    den_ref[...] = den


def finish_kernel(num_ref, den_ref, phi_ref, state_ref, out_ref):
    lane = lax.broadcasted_iota(jnp.int32, (TOK, 128), 1)
    group = pl.program_id(0)
    at = FEATS - (FROWS - 16)
    for j in range(GROUP):
        phi = taller(phi_ref[j]).T
        state = state_ref[j]
        carried = jnp.dot(phi, taller(state), preferred_element_type=F32)
        tail = state[FROWS - 16 : FROWS].astype(F32)
        n0 = tail[at : at + 1] + tail[at + 2 : at + 3]
        n1 = tail[at + 1 : at + 2] + tail[at + 3 : at + 4]
        phi32 = phi.astype(F32)
        den = jnp.where(lane == group * GROUP + j, den_ref[...], 0.0) + phi32[:, :128] * n0 + phi32[:, 128:] * n1
        den = jnp.sum(den, axis=1, keepdims=True)
        out_ref[:, column(j)] = ((num_ref[:, column(j)].astype(F32) + carried) / den).astype(BF)


def halves(core, refs):
    at = pl.ds(pl.multiple_of(core * HALF, 128), HALF)
    return [r.at[:, at] for r in refs]


def listed_rows(ids_ref, count_ref):
    lane = lax.broadcasted_iota(jnp.int32, (QROWS - TOK, HALF), 1)
    listed = jnp.full((QROWS - TOK, HALF), -1.0, F32)
    for i in range(LISTED):
        entry = jnp.where(i < count_ref[0], ids_ref[i], -1).astype(F32)
        listed = jnp.where(lane == i, entry, listed)
    return listed.astype(BF)


def pack_kernel(me_ref, ids_ref, count_ref, k_ref, v_ref, q_ref, out_ref, sems):
    copies = [
        pltpu.make_async_copy(half, out_ref.at[pl.ds(i * TOK, TOK)], sems.at[i])
        for i, half in enumerate(halves(1 - (me_ref[0] & 1), (k_ref, v_ref, q_ref)))
    ]
    for c in copies:
        c.start()
    out_ref[3 * TOK :] = listed_rows(ids_ref, count_ref)
    for c in copies:
        c.wait()


def own_kernel(me_ref, ids_ref, count_ref, k_ref, v_ref, q_ref, kv_ref, both_ref, sems):
    targets = (kv_ref.at[0, 0], kv_ref.at[0, 1], both_ref.at[0, pl.ds(0, TOK)])
    copies = [
        pltpu.make_async_copy(half, to, sems.at[i])
        for i, (half, to) in enumerate(zip(halves(me_ref[0] & 1, (k_ref, v_ref, q_ref)), targets, strict=True))
    ]
    for c in copies:
        c.start()
    both_ref[0, TOK:QROWS] = listed_rows(ids_ref, count_ref)
    for c in copies:
        c.wait()


def merge_kernel(mate_ref, kv_in, both_in, kv_ref, both_ref, sems):
    del kv_in, both_in
    pieces = ((pl.ds(0, TOK), kv_ref.at[1, 0]), (pl.ds(TOK, TOK), kv_ref.at[1, 1]), (pl.ds(2 * TOK, QROWS), both_ref.at[1]))
    copies = [pltpu.make_async_copy(mate_ref.at[at], to, sems.at[i]) for i, (at, to) in enumerate(pieces)]
    for c in copies:
        c.start()
    for c in copies:
        c.wait()


def search_kernel(me_ref, *refs):
    q_in, (found_ref, count_ref, wanted, ids, sems) = refs[:SIDE], refs[SIDE:]
    me = me_ref[0]
    core, y, x = me & 1, (me >> 1) & (SIDE - 1), me >> 3
    rows = pl.ds(TOK, QROWS - TOK)
    copies = [
        pltpu.make_async_copy(q_in[i].at[:, rows, pl.ds(0, 128)], ids.at[pl.ds(2 * i, 2)], sems.at[i]) for i in range(SIDE)
    ]
    for c in copies:
        c.start()
    for c in copies:
        c.wait()
    for r in range(2 * SIDE):
        wanted[r : r + 1] = ids[r].astype(F32).astype(jnp.int32)[0:1]
    pltpu.async_copy(wanted, found_ref, sems.at[SIDE]).wait()

    def search(r, carry):
        count = jnp.int32(0)
        for i in range(LISTED):
            entry = found_ref[r, i]
            xo, yo, co = entry >> 4, (entry >> 2) & (SIDE - 1), (entry >> 1) & 1
            mine = (entry >= 0) & jnp.where(core == 0, yo == y, xo == x)
            away = jnp.where(core == 0, xo - x, yo - y) & (SIDE - 1)
            found_ref[r, count] = (away * 2 + (co ^ core)) * 2 + (entry & 1)
            count = count + mine.astype(jnp.int32)
        count_ref[r] = count
        return carry

    lax.fori_loop(0, 2 * SIDE, search, 0)


def attend_kernel(own, base, readers, found, counts, *refs):
    groups = readers // 2
    q_in, kv_in, outs = refs[:groups], refs[groups : groups + SIDE], refs[groups + SIDE : readers + SIDE]
    q_buf, g_buf, s_buf, m_buf, a_buf, q_sems, g_sems = refs[readers + SIDE :]
    copies = [pltpu.make_async_copy(q_in[i], q_buf.at[pl.ds(2 * i, 2)], q_sems.at[i]) for i in range(groups)]
    for c in copies:
        c.start()
    lane = lax.broadcasted_iota(jnp.int32, (TOK, 128), 1)
    heads = [(h, slice(h * 128, (h + 1) * 128)) for h in range(HALF_HEADS)]

    def fetch(r, slot):
        def one(i, carry):
            code = found[base + r, i]
            rows = pl.ds(pl.multiple_of((code & 1) * BLK, BLK), BLK)
            for away in range(SIDE):

                @pl.when((code >> 2) == away)
                def _():
                    source = kv_in[away].at[(code >> 1) & 1, :, rows, :]
                    pltpu.make_async_copy(source, g_buf.at[slot, i], g_sems.at[slot, i]).start()

            return carry

        lax.fori_loop(0, counts[base + r], one, 0)

    def arrived(r, slot):
        def one(i, carry):
            source = kv_in[0].at[0, :, pl.ds(0, BLK), :]
            pltpu.make_async_copy(source, g_buf.at[slot, i], g_sems.at[slot, i]).wait()
            return carry

        lax.fori_loop(0, counts[base + r], one, 0)

    def blank(slot, i):
        g_buf[slot, i, 1] = jnp.zeros((BLK, HALF), BF)

    def reader(r, slot, out_ref):
        count = counts[base + r]
        pairs = (count + 1) >> 1

        @pl.when((count & 1) == 1)
        def _():
            blank(slot, count)

        if not own:

            @pl.when(count == 0)
            def _():
                blank(slot, 0)
                blank(slot, 1)

        def blocks(j, kind, at):
            return jnp.concatenate([g_buf[slot, 2 * j, kind, :, at], g_buf[slot, 2 * j + 1, kind, :, at]], axis=0)

        def score(j, fresh):
            for h, at in heads:
                s = lax.dot_general(q_buf[r, 0:TOK, at], blocks(j, 0, at), NT, preferred_element_type=F32)
                s0, s1 = s[:, :128], jnp.where(2 * j + 1 < count, s[:, 128:], NEG)
                if fresh:
                    s0 = jnp.where(count > 0, s0, NEG)
                s_buf[j, h, :, 0:128] = s0
                s_buf[j, h, :, 128:256] = s1
                m = jnp.maximum(s0, s1)
                m_buf[h] = m if fresh else jnp.maximum(m_buf[h], m)

        def weigh(j, fresh):
            for h, at in heads:
                m = m_buf[h]
                p = jnp.exp2(s_buf[j, h] * TO_LOG2 - jnp.concatenate([m, m], axis=1)).astype(BF)
                a = jnp.dot(p, with_ones(blocks(j, 1, at)), preferred_element_type=F32)
                a_buf[h] = a if fresh else a_buf[h] + a

        if own:
            for h, at in heads:
                parts = []
                for b in range(2):
                    rows = slice(b * BLK, (b + 1) * BLK)
                    k = own_kv[r, 0, rows, at]
                    parts.append(lax.dot_general(q_buf[r, rows, at], k, NT, preferred_element_type=F32))
                s = jnp.concatenate(parts, axis=0)
                s_buf[LISTED // 2, h, :, 0:128] = s
                m_buf[h] = s
        else:
            score(0, True)
        start = 0 if own else 1

        def more_scores(j, carry):
            score(j, False)
            return carry

        lax.fori_loop(start, pairs, more_scores, 0)
        tops = jnp.zeros((TOK, 128), F32)
        for h, at in heads:
            m = jnp.broadcast_to(jnp.max(m_buf[h], axis=1, keepdims=True) * TO_LOG2, (TOK, 128))
            m_buf[h] = m
            tops = jnp.where(lane == h, m, tops)
        if own:
            for h, at in heads:
                p = jnp.exp2(s_buf[LISTED // 2, h, :, 0:128] * TO_LOG2 - m_buf[h]).astype(BF)
                parts = []
                for b in range(2):
                    rows = slice(b * BLK, (b + 1) * BLK)
                    v = with_ones(own_kv[r, 1, rows, at])
                    parts.append(jnp.dot(p[rows], v, preferred_element_type=F32))
                a_buf[h] = jnp.concatenate(parts, axis=0)
        else:
            weigh(0, True)

        def more_weights(j, carry):
            weigh(j, False)
            return carry

        lax.fori_loop(start, pairs, more_weights, 0)
        totals = jnp.ones((TOK, 128), F32)
        for h, at in heads:
            total = a_buf[h, :, 128:]
            out_ref[slot, 0:TOK, at] = (a_buf[h, :, :128] / total).astype(BF)
            totals = jnp.where(lane == h, total, totals)
        sizes = tops + jnp.log2(totals)
        if not own:
            sizes = jnp.where(jnp.logical_and(count == 0, lane < HALF_HEADS), NEG, sizes)
        high = sizes.astype(BF).astype(F32)
        middle = (sizes - high).astype(BF).astype(F32)
        low = sizes - high - middle
        packed = high + pltpu.roll(middle, HALF_HEADS, 1) + pltpu.roll(low, 2 * HALF_HEADS, 1)
        out_ref[slot, TOK:QROWS, :] = jnp.zeros((QROWS - TOK, HALF), BF)
        out_ref[slot, TOK:QROWS, 0:TOK] = packed.T[0 : QROWS - TOK].astype(BF)

    own_kv = kv_in[0]
    fetch(0, 0)
    for c in copies:
        c.wait()
    for g, out_ref in enumerate(outs):

        def one(i, carry, g=g, out_ref=out_ref):
            r = 2 * g + i

            @pl.when(r + 1 < readers)
            def _():
                fetch(r + 1, 1 - i)

            arrived(r, i)
            reader(r, i, out_ref)
            return carry

        lax.fori_loop(0, 2, one, 0)


def join_kernel(*refs):
    parts, outs = refs[:4], refs[4:]
    for r in range(2):
        sizes = []
        for p in parts:
            packed = p[r, TOK:QROWS, 0:TOK].astype(F32)
            packed = jnp.concatenate([packed, jnp.zeros((128 - (QROWS - TOK), TOK), F32)], axis=0).T
            sizes.append(packed + pltpu.roll(packed, 128 - HALF_HEADS, 1) + pltpu.roll(packed, 128 - 2 * HALF_HEADS, 1))
        top = functools.reduce(jnp.maximum, sizes)
        shares = [jnp.exp2(s - top) for s in sizes]
        total = functools.reduce(jnp.add, shares)
        shares = [s / total for s in shares]
        for h in range(HALF_HEADS):
            at = slice(h * 128, (h + 1) * 128)
            o = sum(s[:, h : h + 1] * p[r, 0:TOK, at].astype(F32) for s, p in zip(shares, parts, strict=True))
            outs[r][:, at] = o.astype(BF)


def place_kernel(me_ref, kept_ref, other_ref, out_ref, sems):
    core = me_ref[0] & 1
    copies = [
        pltpu.make_async_copy(half, to, sems.at[i])
        for i, (half, to) in enumerate(zip((kept_ref, other_ref), halves(core, (out_ref,)) + halves(1 - core, (out_ref,)), strict=True))
    ]
    for c in copies:
        c.start()
    for c in copies:
        c.wait()


def shape(*dims, dtype=BF):
    return jax.ShapeDtypeStruct(dims, dtype)


SMEM = pl.BlockSpec(memory_space=pltpu.SMEM)
VMEM = pl.BlockSpec(memory_space=pltpu.VMEM)
ANY = pl.BlockSpec(memory_space=pl.ANY)
HBM = pl.BlockSpec(memory_space=pltpu.HBM)


def room(mib):
    return pltpu.CompilerParams(vmem_limit_bytes=mib * 1024 * 1024)


def cost(flops, moved):
    return pl.CostEstimate(flops=int(flops), bytes_accessed=int(moved), transcendentals=0)


def in_hbm(*arrays):
    return tuple(pltpu.with_memory_space_constraint(a, pltpu.HBM) for a in arrays)


def hbm_shape(*dims, dtype=BF):
    return pltpu.HBM(dims, dtype)


def whole(*dims):
    return pl.BlockSpec(dims, lambda g: (0,) * len(dims))


def attend(name, base, lists, queries, blocks):
    own = name == "attend_own"
    groups = len(queries)
    readers = 2 * groups
    first = VMEM if own else ANY
    return pl.pallas_call(
        functools.partial(attend_kernel, own, base, readers),
        out_shape=[shape(2, QROWS, HALF)] * groups,
        in_specs=[SMEM, SMEM] + [ANY] * groups + [first] + [ANY] * (SIDE - 1),
        out_specs=[VMEM] * groups,
        scratch_shapes=[
            pltpu.VMEM((readers, QROWS, HALF), BF),
            pltpu.VMEM((2, LISTED, 2, BLK, HALF), BF),
            pltpu.VMEM((LISTED // 2 + 1, HALF_HEADS, TOK, 256), F32),
            pltpu.VMEM((HALF_HEADS, TOK, 128), F32),
            pltpu.VMEM((HALF_HEADS, TOK, 256), F32),
            pltpu.SemaphoreType.DMA((groups,)),
            pltpu.SemaphoreType.DMA((2, LISTED)),
        ],
        compiler_params=room(20),
        cost_estimate=cost(readers * 4e8, 8e6),
    )(*lists, *queries, *blocks)


def layers(q_lin, k_lin, v_lin, q_soft, k_soft, v_soft, import_ids, import_counts):
    select, vectors = (jnp.asarray(t) for t in feature_tables())
    me = lax.axis_index("files").astype(jnp.int32).reshape(1)
    place = lax.axis_index("seq").astype(jnp.int32).reshape(1)
    shards = lax.axis_size("seq")
    steps = (HEADS // GROUP,)
    heads16 = pl.BlockSpec((GROUP * FEAT, TOK), lambda g: (g, 0))
    heads128 = pl.BlockSpec((TOK, GROUP * 128), lambda g: (0, g))
    mine = (me, import_ids[0, 0], import_counts[0]) + in_hbm(k_soft[0], v_soft[0], q_soft[0])

    sent = pl.pallas_call(
        pack_kernel,
        name="pack",
        out_shape=shape(2 * TOK + QROWS, HALF),
        in_specs=[SMEM] * 3 + [HBM] * 3,
        out_specs=VMEM,
        scratch_shapes=[pltpu.SemaphoreType.DMA((3,))],
        compiler_params=room(4),
        cost_estimate=cost(0, 2e6),
    )(*mine)
    mate = swap_cores(sent)
    pair = [shape(2, 2, TOK, HALF), shape(2, QROWS, HALF)]
    kv, q = pl.pallas_call(
        own_kernel,
        name="own",
        out_shape=pair,
        in_specs=[SMEM] * 3 + [HBM] * 3,
        out_specs=[VMEM] * 2,
        scratch_shapes=[pltpu.SemaphoreType.DMA((3,))],
        compiler_params=room(6),
        cost_estimate=cost(0, 2e6),
    )(*mine)

    kv, q = pl.pallas_call(
        merge_kernel,
        name="merge",
        out_shape=pair,
        in_specs=[VMEM, ANY, ANY],
        out_specs=[ANY] * 2,
        scratch_shapes=[pltpu.SemaphoreType.DMA((3,))],
        input_output_aliases={1: 0, 2: 1},
        compiler_params=room(4),
        cost_estimate=cost(0, 2e6),
    )(mate, kv, q)
    kv_right = move(kv, "kv", -1)
    kv_left = move(kv, "kv", 1)
    q_left = move(q, "q", 1)
    q_right = move(q, "q", -1)
    kv_far = move(kv_right, "kv", -1)
    q_far = move(q_left, "q", 1)

    state = pl.pallas_call(
        state_kernel,
        name="state",
        grid=steps,
        out_shape=hbm_shape(HEADS, FROWS, 128),
        in_specs=[heads16, heads128, whole(*select.shape), whole(*vectors.shape)],
        out_specs=pl.BlockSpec((GROUP, FROWS, 128), lambda g: (g, 0, 0)),
        compiler_params=room(12),
        cost_estimate=cost(1e9, 4e6),
    )(*in_hbm(k_lin[0].T, v_lin[0], select, vectors))
    slices = lax.all_to_all(state.reshape(shards, HEADS * FROWS // shards, 128), "seq", 0, 0, tiled=True)

    num, den, phi = pl.pallas_call(
        local_kernel,
        name="local",
        grid=steps,
        out_shape=[hbm_shape(TOK, D), hbm_shape(TOK, 128, dtype=F32), hbm_shape(HEADS, FROWS, TOK)],
        in_specs=[heads16, heads16, heads128, whole(*select.shape), whole(*vectors.shape)],
        out_specs=[heads128, whole(TOK, 128), pl.BlockSpec((GROUP, FROWS, TOK), lambda g: (g, 0, 0))],
        compiler_params=room(16),
        cost_estimate=cost(4e9, 8e6),
    )(*in_hbm(q_lin[0].T, k_lin[0].T, v_lin[0], select, vectors))

    blocks = (kv, kv_right, kv_far, kv_left)
    lists = pl.pallas_call(
        search_kernel,
        name="search",
        out_shape=[shape(2 * SIDE, 128, dtype=jnp.int32), shape(2 * SIDE, dtype=jnp.int32)],
        in_specs=[SMEM] + [ANY] * SIDE,
        out_specs=[SMEM] * 2,
        scratch_shapes=[
            pltpu.VMEM((2 * SIDE, 128), jnp.int32),
            pltpu.VMEM((2 * SIDE, QROWS - TOK, 128), BF),
            pltpu.SemaphoreType.DMA((SIDE + 1,)),
        ],
        compiler_params=room(2),
        cost_estimate=cost(0, 1e5),
    )(me, q_far, q_left, q_right, q)
    (to_far,) = attend("attend_far", 0, lists, (q_far,), blocks)
    to_far, q_left, q_right = lax.optimization_barrier((to_far, q_left, q_right))
    _, slices, num, den, phi = lax.optimization_barrier((to_far, slices, num, den, phi))
    prefix = pl.pallas_call(
        prefix_kernel,
        name="prefix",
        out_shape=hbm_shape(*slices.shape),
        in_specs=[SMEM, VMEM],
        out_specs=VMEM,
        compiler_params=room(8),
        cost_estimate=cost(0, 2e6),
    )(place, slices)
    before = lax.all_to_all(prefix, "seq", 0, 0, tiled=True).reshape(HEADS, FROWS, 128)
    from_far = move(to_far, "q", 2)
    to_left, to_right = attend("attend_sides", 2, lists, (q_left, q_right), blocks)
    from_right = move(to_left, "q", -1)
    from_left = move(to_right, "q", 1)
    (here,) = attend("attend_own", 6, lists, (q,), blocks)
    kept, send = pl.pallas_call(
        join_kernel,
        name="join",
        out_shape=[shape(TOK, HALF)] * 2,
        in_specs=[VMEM] * 4,
        out_specs=[VMEM] * 2,
        compiler_params=room(8),
        cost_estimate=cost(0, 4e6),
    )(here, from_right, from_left, from_far)
    other = swap_cores(send)
    soft_out = pl.pallas_call(
        place_kernel,
        name="place",
        out_shape=shape(TOK, SM_W),
        in_specs=[SMEM, VMEM, VMEM],
        out_specs=HBM,
        scratch_shapes=[pltpu.SemaphoreType.DMA((2,))],
        compiler_params=room(4),
        cost_estimate=cost(0, 1e6),
    )(me, kept, other)

    lin_out = pl.pallas_call(
        finish_kernel,
        name="finish",
        grid=steps,
        out_shape=shape(TOK, D),
        in_specs=[
            heads128,
            whole(TOK, 128),
            pl.BlockSpec((GROUP, FROWS, TOK), lambda g: (g, 0, 0)),
            pl.BlockSpec((GROUP, FROWS, 128), lambda g: (g, 0, 0)),
        ],
        out_specs=heads128,
        compiler_params=room(16),
        cost_estimate=cost(4e8, 8e6),
    )(*in_hbm(num, den, phi), before)
    return lin_out[None], soft_out[None]


def solution(mesh):
    wide = P("files", "seq", None)
    return jax.shard_map(
        layers,
        mesh=mesh,
        in_specs=(wide,) * 7 + (P("files", "seq"),),
        out_specs=(wide, wide),
        check_vma=False,
    )
```

```python
import functools
import math

import jax
import jax.numpy as jnp
import numpy as np
from jax import lax
from jax.experimental import pallas as pl
from jax.experimental.pallas import tpu as pltpu
from jax.sharding import PartitionSpec as P

D = 2560
HEADS = 20
FEAT = 16
FEATS = 153
FROWS = 160
FPAD = 256
SM_HD = 128
SM_W = 1280
BLK = 128
TOK = 256
LISTED = 8
GROUP = 4
HALF = 640
HALF_HEADS = 5
QROWS = 272
SIDE = 4
CORES = 2

inv_root_two = 0.7071067811865476
TO_LOG2 = math.log2(math.e) / math.sqrt(SM_HD)
NEG = -1e30
BF = jnp.bfloat16
F32 = jnp.float32
NT = (((1,), (1,)), ((), ()))


def along(what, step):
    pairs = []
    for x in range(SIDE):
        for y in range(SIDE):
            for c in range(CORES):
                on_x = (c == 0) == (what == "kv")
                x2 = (x + step) % SIDE if on_x else x
                y2 = y if on_x else (y + step) % SIDE
                pairs.append(((x * SIDE + y) * CORES + c, (x2 * SIDE + y2) * CORES + c))
    return pairs


def move(a, what, step):
    return lax.ppermute(a, "files", along(what, step))


def swap_cores(a):
    return lax.ppermute(a, "files", [(i, i ^ 1) for i in range(SIDE * SIDE * CORES)])


def feature_tables():
    rows, cols = np.triu_indices(FEAT)
    select = np.zeros((GROUP, 2, FROWS, GROUP * FEAT), np.float32)
    for j in range(GROUP):
        for f in range(FEAT):
            select[j, 0, 1 + f, j * FEAT + f] = 0.5
        for n in range(len(rows)):
            select[j, 0, 1 + FEAT + n, j * FEAT + rows[n]] = 0.5
            select[j, 1, 1 + FEAT + n, j * FEAT + cols[n]] = 0.5
    vectors = np.zeros((3, FROWS), np.float32)
    vectors[0, 0] = 1.0
    vectors[1, : 1 + FEAT] = 1.0
    vectors[2, :FEATS] = 1.0
    vectors[2, 1 + FEAT : FEATS] = np.where(rows == cols, inv_root_two, 1.0).astype(np.float32)
    vectors = np.ascontiguousarray(np.broadcast_to(vectors[:, :, None], (3, FROWS, 128)))
    return select.reshape(GROUP, 2 * FROWS, GROUP * FEAT).astype(jnp.bfloat16), vectors


def column(j):
    return slice(j * 128, (j + 1) * 128)


def features(select, x, vectors):
    first, second, factor = (jnp.concatenate([vectors[i], vectors[i]], axis=1) for i in range(3))
    ab = jnp.dot(select, x, preferred_element_type=F32)
    return ((ab[:FROWS] + first) * (ab[FROWS:] + second) * factor).astype(BF)


def taller(phi):
    return jnp.concatenate([phi, jnp.zeros((FPAD - FROWS, phi.shape[1]), BF)], axis=0)


def with_ones(values):
    return jnp.concatenate([values, jnp.ones(values.shape, BF)], axis=1)


def state_kernel(k_ref, v_ref, select_ref, vector_ref, out_ref):
    row = lax.broadcasted_iota(jnp.int32, (16, 128), 0)
    lane = lax.broadcasted_iota(jnp.int32, (FROWS, 128), 1)
    norms = jnp.zeros((FROWS, 128), F32)
    phis = [features(select_ref[j], k_ref[...], vector_ref) for j in range(GROUP)]
    boths = [jnp.dot(phis[j], with_ones(v_ref[:, column(j)]), preferred_element_type=F32) for j in range(GROUP)]
    for j in range(GROUP):
        norms = jnp.where(lane == j, boths[j][:, 128:], norms)
        out_ref[j] = boths[j][:, :128].astype(BF)
    flat = jnp.concatenate([norms, jnp.zeros((FPAD - FROWS, 128), F32)], axis=0).T
    high = flat.astype(BF).astype(F32)
    low = flat - high
    at = row + (FROWS - 16 - FEATS)
    for j in range(GROUP):
        tail = out_ref[j, FROWS - 16 :].astype(F32)
        pieces = (high[j : j + 1, :128], high[j : j + 1, 128:], low[j : j + 1, :128], low[j : j + 1, 128:])
        for i, piece in enumerate(pieces):
            tail = jnp.where(at == i, piece, tail)
        out_ref[j, FROWS - 16 :] = tail.astype(BF)


def prefix_kernel(place_ref, in_ref, out_ref):
    rows = in_ref.shape[1]
    row = lax.broadcasted_iota(jnp.int32, (rows, 128), 0) + (place_ref[0] & 1) * (FROWS // 2)
    row = jnp.where(row >= FROWS, row - FROWS, row)
    row = jnp.where(row >= FROWS, row - FROWS, row)
    high = (row == FEATS) | (row == FEATS + 1)
    low = (row == FEATS + 2) | (row == FEATS + 3)
    total = jnp.zeros((rows, 128), F32)
    for z in range(in_ref.shape[0]):
        both = total + pltpu.roll(total, rows - 2, 0)
        top = both.astype(BF).astype(F32)
        rest = pltpu.roll(both - top, 2, 0)
        out_ref[z] = jnp.where(high, top, jnp.where(low, rest, total)).astype(BF)
        total = total + in_ref[z].astype(F32)


def local_kernel(q_ref, k_ref, v_ref, select_ref, vector_ref, num_ref, den_ref, phi_ref):
    causal = lax.broadcasted_iota(jnp.int32, (TOK, TOK), 0) >= lax.broadcasted_iota(jnp.int32, (TOK, TOK), 1)
    lane = lax.broadcasted_iota(jnp.int32, (TOK, 128), 1)
    group = pl.program_id(0)

    @pl.when(group == 0)
    def _():
        den_ref[...] = jnp.zeros((TOK, 128), F32)

    den = den_ref[...]
    phis_q = [features(select_ref[j], q_ref[...], vector_ref) for j in range(GROUP)]
    phis_k = [features(select_ref[j], k_ref[...], vector_ref) for j in range(GROUP)]
    for j in range(GROUP):
        phi_ref[j] = phis_q[j]
    turned = [taller(p).T for p in phis_q]
    weights = [jnp.dot(turned[j], taller(phis_k[j]), preferred_element_type=F32) for j in range(GROUP)]
    weights = [jnp.where(causal, w, 0.0).astype(BF) for w in weights]
    boths = [jnp.dot(weights[j], with_ones(v_ref[:, column(j)]), preferred_element_type=F32) for j in range(GROUP)]
    for j in range(GROUP):
        num_ref[:, column(j)] = boths[j][:, :128].astype(BF)
        den = jnp.where(lane == group * GROUP + j, boths[j][:, 128:], den)
    den_ref[...] = den


def finish_kernel(num_ref, den_ref, phi_ref, state_ref, out_ref):
    lane = lax.broadcasted_iota(jnp.int32, (TOK, 128), 1)
    group = pl.program_id(0)
    at = FEATS - (FROWS - 16)
    phis = [taller(phi_ref[j]).T for j in range(GROUP)]
    carried = [jnp.dot(phis[j], taller(state_ref[j]), preferred_element_type=F32) for j in range(GROUP)]
    dens = []
    for j in range(GROUP):
        tail = state_ref[j, FROWS - 16 :].astype(F32)
        n0 = tail[at : at + 1] + tail[at + 2 : at + 3]
        n1 = tail[at + 1 : at + 2] + tail[at + 3 : at + 4]
        phi32 = phis[j].astype(F32)
        den = jnp.where(lane == group * GROUP + j, den_ref[...], 0.0) + phi32[:, :128] * n0 + phi32[:, 128:] * n1
        dens.append(jnp.sum(den, axis=1, keepdims=True))
    for j in range(GROUP):
        out_ref[:, column(j)] = ((num_ref[:, column(j)].astype(F32) + carried[j]) / dens[j]).astype(BF)


def halves(core, refs):
    at = pl.ds(pl.multiple_of(core * HALF, 128), HALF)
    return [r.at[:, at] for r in refs]


def listed_rows(ids_ref, count_ref):
    lane = lax.broadcasted_iota(jnp.int32, (QROWS - TOK, HALF), 1)
    listed = jnp.full((QROWS - TOK, HALF), -1.0, F32)
    for i in range(LISTED):
        entry = jnp.where(i < count_ref[0], ids_ref[i], -1).astype(F32)
        listed = jnp.where(lane == i, entry, listed)
    return listed.astype(BF)


def pack_kernel(me_ref, ids_ref, count_ref, k_ref, v_ref, q_ref, out_ref, sems):
    copies = [
        pltpu.make_async_copy(half, out_ref.at[pl.ds(i * TOK, TOK)], sems.at[i])
        for i, half in enumerate(halves(1 - (me_ref[0] & 1), (k_ref, v_ref, q_ref)))
    ]
    for c in copies:
        c.start()
    out_ref[3 * TOK :] = listed_rows(ids_ref, count_ref)
    for c in copies:
        c.wait()


def own_kernel(me_ref, ids_ref, count_ref, k_ref, v_ref, q_ref, kv_ref, both_ref, sems):
    targets = (kv_ref.at[0, 0], kv_ref.at[0, 1], both_ref.at[0, pl.ds(0, TOK)])
    copies = [
        pltpu.make_async_copy(half, to, sems.at[i])
        for i, (half, to) in enumerate(zip(halves(me_ref[0] & 1, (k_ref, v_ref, q_ref)), targets, strict=True))
    ]
    for c in copies:
        c.start()
    both_ref[0, TOK:QROWS] = listed_rows(ids_ref, count_ref)
    for c in copies:
        c.wait()


def merge_kernel(mate_ref, kv_in, both_in, kv_ref, both_ref, sems):
    del kv_in, both_in
    pieces = ((pl.ds(0, TOK), kv_ref.at[1, 0]), (pl.ds(TOK, TOK), kv_ref.at[1, 1]), (pl.ds(2 * TOK, QROWS), both_ref.at[1]))
    copies = [pltpu.make_async_copy(mate_ref.at[at], to, sems.at[i]) for i, (at, to) in enumerate(pieces)]
    for c in copies:
        c.start()
    for c in copies:
        c.wait()


def search_kernel(me_ref, *refs):
    q_in, (found_ref, count_ref, wanted, ids, sems) = refs[:SIDE], refs[SIDE:]
    me = me_ref[0]
    core, y, x = me & 1, (me >> 1) & (SIDE - 1), me >> 3
    rows = pl.ds(TOK, QROWS - TOK)
    copies = [
        pltpu.make_async_copy(q_in[i].at[:, rows, pl.ds(0, 128)], ids.at[pl.ds(2 * i, 2)], sems.at[i]) for i in range(SIDE)
    ]
    for c in copies:
        c.start()
    for c in copies:
        c.wait()
    for r in range(2 * SIDE):
        wanted[r : r + 1] = ids[r].astype(F32).astype(jnp.int32)[0:1]
    pltpu.async_copy(wanted, found_ref, sems.at[SIDE]).wait()

    def search(r, carry):
        count = jnp.int32(0)
        for i in range(LISTED):
            entry = found_ref[r, i]
            xo, yo, co = entry >> 4, (entry >> 2) & (SIDE - 1), (entry >> 1) & 1
            mine = (entry >= 0) & jnp.where(core == 0, yo == y, xo == x)
            away = jnp.where(core == 0, xo - x, yo - y) & (SIDE - 1)
            found_ref[r, count] = (away * 2 + (co ^ core)) * 2 + (entry & 1)
            count = count + mine.astype(jnp.int32)
        count_ref[r] = count
        return carry

    lax.fori_loop(0, 2 * SIDE, search, 0)


def attend_kernel(own, base, readers, found, counts, *refs):
    groups = readers // 2
    q_in, kv_in, outs = refs[:groups], refs[groups : groups + SIDE], refs[groups + SIDE : readers + SIDE]
    q_buf, g_buf, s_buf, m_buf, a_buf, q_sems, g_sems = refs[readers + SIDE :]
    copies = [pltpu.make_async_copy(q_in[i], q_buf.at[pl.ds(2 * i, 2)], q_sems.at[i]) for i in range(groups)]
    for c in copies:
        c.start()
    lane = lax.broadcasted_iota(jnp.int32, (TOK, 128), 1)
    heads = [(h, slice(h * 128, (h + 1) * 128)) for h in range(HALF_HEADS)]

    def fetch(r, slot):
        def one(i, carry):
            code = found[base + r, i]
            rows = pl.ds(pl.multiple_of((code & 1) * BLK, BLK), BLK)
            for away in range(SIDE):

                @pl.when((code >> 2) == away)
                def _():
                    source = kv_in[away].at[(code >> 1) & 1, :, rows, :]
                    pltpu.make_async_copy(source, g_buf.at[slot, i], g_sems.at[slot, i]).start()

            return carry

        lax.fori_loop(0, counts[base + r], one, 0)

    def arrived(r, slot):
        def one(i, carry):
            source = kv_in[0].at[0, :, pl.ds(0, BLK), :]
            pltpu.make_async_copy(source, g_buf.at[slot, i], g_sems.at[slot, i]).wait()
            return carry

        lax.fori_loop(0, counts[base + r], one, 0)

    def blank(slot, i):
        g_buf[slot, i, 1] = jnp.zeros((BLK, HALF), BF)

    def reader(r, slot, out_ref):
        count = counts[base + r]
        pairs = (count + 1) >> 1

        @pl.when((count & 1) == 1)
        def _():
            blank(slot, count)

        if not own:

            @pl.when(count == 0)
            def _():
                blank(slot, 0)
                blank(slot, 1)

        def blocks(j, kind, at):
            return jnp.concatenate([g_buf[slot, 2 * j, kind, :, at], g_buf[slot, 2 * j + 1, kind, :, at]], axis=0)

        def score(j, fresh):
            for h, at in heads:
                s = lax.dot_general(q_buf[r, 0:TOK, at], blocks(j, 0, at), NT, preferred_element_type=F32)
                s0, s1 = s[:, :128], jnp.where(2 * j + 1 < count, s[:, 128:], NEG)
                if fresh:
                    s0 = jnp.where(count > 0, s0, NEG)
                s_buf[j, h, :, 0:128] = s0
                s_buf[j, h, :, 128:256] = s1
                m = jnp.maximum(s0, s1)
                m_buf[h] = m if fresh else jnp.maximum(m_buf[h], m)

        def weigh(j, fresh):
            for h, at in heads:
                m = m_buf[h]
                p = jnp.exp2(s_buf[j, h] * TO_LOG2 - jnp.concatenate([m, m], axis=1)).astype(BF)
                a = jnp.dot(p, with_ones(blocks(j, 1, at)), preferred_element_type=F32)
                a_buf[h] = a if fresh else a_buf[h] + a

        if own:
            for h, at in heads:
                parts = []
                for b in range(2):
                    rows = slice(b * BLK, (b + 1) * BLK)
                    k = own_kv[r, 0, rows, at]
                    parts.append(lax.dot_general(q_buf[r, rows, at], k, NT, preferred_element_type=F32))
                s = jnp.concatenate(parts, axis=0)
                s_buf[LISTED // 2, h, :, 0:128] = s
                m_buf[h] = s
        else:
            score(0, True)
        start = 0 if own else 1

        def more_scores(j, carry):
            score(j, False)
            return carry

        lax.fori_loop(start, pairs, more_scores, 0)
        tops = jnp.zeros((TOK, 128), F32)
        for h, at in heads:
            m = jnp.broadcast_to(jnp.max(m_buf[h], axis=1, keepdims=True) * TO_LOG2, (TOK, 128))
            m_buf[h] = m
            tops = jnp.where(lane == h, m, tops)
        if own:
            for h, at in heads:
                p = jnp.exp2(s_buf[LISTED // 2, h, :, 0:128] * TO_LOG2 - m_buf[h]).astype(BF)
                parts = []
                for b in range(2):
                    rows = slice(b * BLK, (b + 1) * BLK)
                    v = with_ones(own_kv[r, 1, rows, at])
                    parts.append(jnp.dot(p[rows], v, preferred_element_type=F32))
                a_buf[h] = jnp.concatenate(parts, axis=0)
        else:
            weigh(0, True)

        def more_weights(j, carry):
            weigh(j, False)
            return carry

        lax.fori_loop(start, pairs, more_weights, 0)
        totals = jnp.ones((TOK, 128), F32)
        for h, at in heads:
            total = a_buf[h, :, 128:]
            out_ref[slot, 0:TOK, at] = (a_buf[h, :, :128] / total).astype(BF)
            totals = jnp.where(lane == h, total, totals)
        sizes = tops + jnp.log2(totals)
        if not own:
            sizes = jnp.where(jnp.logical_and(count == 0, lane < HALF_HEADS), NEG, sizes)
        high = sizes.astype(BF).astype(F32)
        middle = (sizes - high).astype(BF).astype(F32)
        low = sizes - high - middle
        packed = high + pltpu.roll(middle, HALF_HEADS, 1) + pltpu.roll(low, 2 * HALF_HEADS, 1)
        out_ref[slot, TOK:QROWS, :] = jnp.zeros((QROWS - TOK, HALF), BF)
        out_ref[slot, TOK:QROWS, 0:TOK] = packed.T[0 : QROWS - TOK].astype(BF)

    own_kv = kv_in[0]
    fetch(0, 0)
    for c in copies:
        c.wait()
    for g, out_ref in enumerate(outs):

        def one(i, carry, g=g, out_ref=out_ref):
            r = 2 * g + i

            @pl.when(r + 1 < readers)
            def _():
                fetch(r + 1, 1 - i)

            arrived(r, i)
            reader(r, i, out_ref)
            return carry

        lax.fori_loop(0, 2, one, 0)


def join_kernel(*refs):
    parts, outs = refs[:4], refs[4:]
    for r in range(2):
        sizes = []
        for p in parts:
            packed = p[r, TOK:QROWS, 0:TOK].astype(F32)
            packed = jnp.concatenate([packed, jnp.zeros((128 - (QROWS - TOK), TOK), F32)], axis=0).T
            sizes.append(packed + pltpu.roll(packed, 128 - HALF_HEADS, 1) + pltpu.roll(packed, 128 - 2 * HALF_HEADS, 1))
        top = functools.reduce(jnp.maximum, sizes)
        shares = [jnp.exp2(s - top) for s in sizes]
        total = functools.reduce(jnp.add, shares)
        shares = [s / total for s in shares]
        for h in range(HALF_HEADS):
            at = slice(h * 128, (h + 1) * 128)
            o = sum(s[:, h : h + 1] * p[r, 0:TOK, at].astype(F32) for s, p in zip(shares, parts, strict=True))
            outs[r][:, at] = o.astype(BF)


def place_kernel(me_ref, kept_ref, other_ref, out_ref, sems):
    core = me_ref[0] & 1
    copies = [
        pltpu.make_async_copy(half, to, sems.at[i])
        for i, (half, to) in enumerate(zip((kept_ref, other_ref), halves(core, (out_ref,)) + halves(1 - core, (out_ref,)), strict=True))
    ]
    for c in copies:
        c.start()
    for c in copies:
        c.wait()


def shape(*dims, dtype=BF):
    return jax.ShapeDtypeStruct(dims, dtype)


SMEM = pl.BlockSpec(memory_space=pltpu.SMEM)
VMEM = pl.BlockSpec(memory_space=pltpu.VMEM)
ANY = pl.BlockSpec(memory_space=pl.ANY)
HBM = pl.BlockSpec(memory_space=pltpu.HBM)


def room(mib):
    return pltpu.CompilerParams(vmem_limit_bytes=mib * 1024 * 1024)


def cost(flops, moved):
    return pl.CostEstimate(flops=int(flops), bytes_accessed=int(moved), transcendentals=0)


def in_hbm(*arrays):
    return tuple(pltpu.with_memory_space_constraint(a, pltpu.HBM) for a in arrays)


def hbm_shape(*dims, dtype=BF):
    return pltpu.HBM(dims, dtype)


def whole(*dims):
    return pl.BlockSpec(dims, lambda g: (0,) * len(dims))


def attend(name, base, lists, queries, blocks):
    own = name == "attend_own"
    groups = len(queries)
    readers = 2 * groups
    first = VMEM if own else ANY
    return pl.pallas_call(
        functools.partial(attend_kernel, own, base, readers),
        out_shape=[shape(2, QROWS, HALF)] * groups,
        in_specs=[SMEM, SMEM] + [ANY] * groups + [first] + [ANY] * (SIDE - 1),
        out_specs=[VMEM] * groups,
        scratch_shapes=[
            pltpu.VMEM((readers, QROWS, HALF), BF),
            pltpu.VMEM((2, LISTED, 2, BLK, HALF), BF),
            pltpu.VMEM((LISTED // 2 + 1, HALF_HEADS, TOK, 256), F32),
            pltpu.VMEM((HALF_HEADS, TOK, 128), F32),
            pltpu.VMEM((HALF_HEADS, TOK, 256), F32),
            pltpu.SemaphoreType.DMA((groups,)),
            pltpu.SemaphoreType.DMA((2, LISTED)),
        ],
        compiler_params=room(18),
        cost_estimate=cost(readers * 4e8, 8e6),
    )(*lists, *queries, *blocks)


def layers(q_lin, k_lin, v_lin, q_soft, k_soft, v_soft, import_ids, import_counts):
    select, vectors = (jnp.asarray(t) for t in feature_tables())
    me = lax.axis_index("files").astype(jnp.int32).reshape(1)
    place = lax.axis_index("seq").astype(jnp.int32).reshape(1)
    shards = lax.axis_size("seq")
    steps = (HEADS // GROUP,)
    heads16 = pl.BlockSpec((GROUP * FEAT, TOK), lambda g: (g, 0))
    heads128 = pl.BlockSpec((TOK, GROUP * 128), lambda g: (0, g))
    mine = (me, import_ids[0, 0], import_counts[0]) + in_hbm(k_soft[0], v_soft[0], q_soft[0])

    sent = pl.pallas_call(
        pack_kernel,
        name="pack",
        out_shape=shape(2 * TOK + QROWS, HALF),
        in_specs=[SMEM] * 3 + [HBM] * 3,
        out_specs=VMEM,
        scratch_shapes=[pltpu.SemaphoreType.DMA((3,))],
        compiler_params=room(4),
        cost_estimate=cost(0, 2e6),
    )(*mine)
    mate = swap_cores(sent)
    pair = [shape(2, 2, TOK, HALF), shape(2, QROWS, HALF)]
    kv, q = pl.pallas_call(
        own_kernel,
        name="own",
        out_shape=pair,
        in_specs=[SMEM] * 3 + [HBM] * 3,
        out_specs=[VMEM] * 2,
        scratch_shapes=[pltpu.SemaphoreType.DMA((3,))],
        compiler_params=room(6),
        cost_estimate=cost(0, 2e6),
    )(*mine)

    kv, q = pl.pallas_call(
        merge_kernel,
        name="merge",
        out_shape=pair,
        in_specs=[VMEM, ANY, ANY],
        out_specs=[ANY] * 2,
        scratch_shapes=[pltpu.SemaphoreType.DMA((3,))],
        input_output_aliases={1: 0, 2: 1},
        compiler_params=room(4),
        cost_estimate=cost(0, 2e6),
    )(mate, kv, q)
    kv_right = move(kv, "kv", -1)
    kv_left = move(kv, "kv", 1)
    q_left = move(q, "q", 1)
    q_right = move(q, "q", -1)
    kv_far = move(kv_right, "kv", -1)
    q_far = move(q_left, "q", 1)

    state = pl.pallas_call(
        state_kernel,
        name="state",
        grid=steps,
        out_shape=hbm_shape(HEADS, FROWS, 128),
        in_specs=[heads16, heads128, whole(*select.shape), whole(*vectors.shape)],
        out_specs=pl.BlockSpec((GROUP, FROWS, 128), lambda g: (g, 0, 0)),
        compiler_params=room(8),
        cost_estimate=cost(1e9, 4e6),
    )(*in_hbm(k_lin[0].T, v_lin[0], select, vectors))
    slices = lax.all_to_all(state.reshape(shards, HEADS * FROWS // shards, 128), "seq", 0, 0, tiled=True)

    num, den, phi = pl.pallas_call(
        local_kernel,
        name="local",
        grid=steps,
        out_shape=[hbm_shape(TOK, D), hbm_shape(TOK, 128, dtype=F32), hbm_shape(HEADS, FROWS, TOK)],
        in_specs=[heads16, heads16, heads128, whole(*select.shape), whole(*vectors.shape)],
        out_specs=[heads128, whole(TOK, 128), pl.BlockSpec((GROUP, FROWS, TOK), lambda g: (g, 0, 0))],
        compiler_params=room(10),
        cost_estimate=cost(4e9, 8e6),
    )(*in_hbm(q_lin[0].T, k_lin[0].T, v_lin[0], select, vectors))

    blocks = (kv, kv_right, kv_far, kv_left)
    lists = pl.pallas_call(
        search_kernel,
        name="search",
        out_shape=[shape(2 * SIDE, 128, dtype=jnp.int32), shape(2 * SIDE, dtype=jnp.int32)],
        in_specs=[SMEM] + [ANY] * SIDE,
        out_specs=[SMEM] * 2,
        scratch_shapes=[
            pltpu.VMEM((2 * SIDE, 128), jnp.int32),
            pltpu.VMEM((2 * SIDE, QROWS - TOK, 128), BF),
            pltpu.SemaphoreType.DMA((SIDE + 1,)),
        ],
        compiler_params=room(2),
        cost_estimate=cost(0, 1e5),
    )(me, q_far, q_left, q_right, q)
    slices, num, den, phi, *lists = lax.optimization_barrier((slices, num, den, phi, *lists))
    prefix = pl.pallas_call(
        prefix_kernel,
        name="prefix",
        out_shape=hbm_shape(*slices.shape),
        in_specs=[SMEM, VMEM],
        out_specs=VMEM,
        compiler_params=room(6),
        cost_estimate=cost(0, 2e6),
    )(place, slices)
    before = lax.all_to_all(prefix, "seq", 0, 0, tiled=True).reshape(HEADS, FROWS, 128)
    (to_far,) = attend("attend_far", 0, lists, (q_far,), blocks)
    to_far, q_left, q_right = lax.optimization_barrier((to_far, q_left, q_right))
    from_far = move(to_far, "q", 2)
    to_left, to_right = attend("attend_sides", 2, lists, (q_left, q_right), blocks)
    from_right = move(to_left, "q", -1)
    from_left = move(to_right, "q", 1)
    (here,) = attend("attend_own", 6, lists, (q,), blocks)
    kept, send = pl.pallas_call(
        join_kernel,
        name="join",
        out_shape=[shape(TOK, HALF)] * 2,
        in_specs=[VMEM] * 4,
        out_specs=[VMEM] * 2,
        compiler_params=room(8),
        cost_estimate=cost(0, 4e6),
    )(here, from_right, from_left, from_far)
    other = swap_cores(send)
    soft_out = pl.pallas_call(
        place_kernel,
        name="place",
        out_shape=shape(TOK, SM_W),
        in_specs=[SMEM, VMEM, VMEM],
        out_specs=HBM,
        scratch_shapes=[pltpu.SemaphoreType.DMA((2,))],
        compiler_params=room(4),
        cost_estimate=cost(0, 1e6),
    )(me, kept, other)

    lin_out = pl.pallas_call(
        finish_kernel,
        name="finish",
        grid=steps,
        out_shape=shape(TOK, D),
        in_specs=[
            heads128,
            whole(TOK, 128),
            pl.BlockSpec((GROUP, FROWS, TOK), lambda g: (g, 0, 0)),
            pl.BlockSpec((GROUP, FROWS, 128), lambda g: (g, 0, 0)),
        ],
        out_specs=heads128,
        compiler_params=room(8),
        cost_estimate=cost(4e8, 8e6),
    )(*in_hbm(num, den, phi), before)
    return lin_out[None], soft_out[None]


def solution(mesh):
    wide = P("files", "seq", None)
    return jax.shard_map(
        layers,
        mesh=mesh,
        in_specs=(wide,) * 7 + (P("files", "seq"),),
        out_specs=(wide, wide),
        check_vma=False,
    )
```

```python
import functools
import math

import jax
import jax.numpy as jnp
import numpy as np
from jax import lax
from jax.experimental import pallas as pl
from jax.experimental.pallas import tpu as pltpu
from jax.sharding import PartitionSpec as P

D = 2560
HEADS = 20
FEAT = 16
FEATS = 153
FROWS = 160
FPAD = 256
SM_HD = 128
SM_W = 1280
BLK = 128
TOK = 256
LISTED = 8
GROUP = 4
HALF = 640
HALF_HEADS = 5
QROWS = 272
SIDE = 4
CORES = 2
JOIN_ROWS = 64

inv_root_two = 0.7071067811865476
TO_LOG2 = math.log2(math.e) / math.sqrt(SM_HD)
NEG = -1e30
BF = jnp.bfloat16
F32 = jnp.float32
NT = (((1,), (1,)), ((), ()))


def along(what, step):
    pairs = []
    for x in range(SIDE):
        for y in range(SIDE):
            for c in range(CORES):
                on_x = (c == 0) == (what == "kv")
                x2 = (x + step) % SIDE if on_x else x
                y2 = y if on_x else (y + step) % SIDE
                pairs.append(((x * SIDE + y) * CORES + c, (x2 * SIDE + y2) * CORES + c))
    return pairs


def move(a, what, step):
    return lax.ppermute(a, "files", along(what, step))


def swap_cores(a):
    return lax.ppermute(a, "files", [(i, i ^ 1) for i in range(SIDE * SIDE * CORES)])


def feature_tables():
    rows, cols = np.triu_indices(FEAT)
    select = np.zeros((GROUP, 2, FROWS, GROUP * FEAT), np.float32)
    for j in range(GROUP):
        for f in range(FEAT):
            select[j, 0, 1 + f, j * FEAT + f] = 0.5
        for n in range(len(rows)):
            select[j, 0, 1 + FEAT + n, j * FEAT + rows[n]] = 0.5
            select[j, 1, 1 + FEAT + n, j * FEAT + cols[n]] = 0.5
    vectors = np.zeros((3, FROWS), np.float32)
    vectors[0, 0] = 1.0
    vectors[1, : 1 + FEAT] = 1.0
    vectors[2, :FEATS] = 1.0
    vectors[2, 1 + FEAT : FEATS] = np.where(rows == cols, inv_root_two, 1.0).astype(np.float32)
    vectors = np.ascontiguousarray(np.broadcast_to(vectors[:, :, None], (3, FROWS, 128)))
    return select.reshape(GROUP, 2 * FROWS, GROUP * FEAT).astype(jnp.bfloat16), vectors


def column(j):
    return slice(j * 128, (j + 1) * 128)


def features(select, x, vectors):
    first, second, factor = (jnp.concatenate([vectors[i], vectors[i]], axis=1) for i in range(3))
    ab = jnp.dot(select, x, preferred_element_type=F32)
    return ((ab[:FROWS] + first) * (ab[FROWS:] + second) * factor).astype(BF)


def taller(phi):
    return jnp.concatenate([phi, jnp.zeros((FPAD - FROWS, phi.shape[1]), BF)], axis=0)


def with_ones(values):
    return jnp.concatenate([values, jnp.ones(values.shape, BF)], axis=1)


def state_kernel(k_ref, v_ref, select_ref, vector_ref, out_ref):
    row = lax.broadcasted_iota(jnp.int32, (16, 128), 0)
    lane = lax.broadcasted_iota(jnp.int32, (FROWS, 128), 1)
    norms = jnp.zeros((FROWS, 128), F32)
    phis = [features(select_ref[j], k_ref[...], vector_ref) for j in range(GROUP)]
    boths = [jnp.dot(phis[j], with_ones(v_ref[:, column(j)]), preferred_element_type=F32) for j in range(GROUP)]
    for j in range(GROUP):
        norms = jnp.where(lane == j, boths[j][:, 128:], norms)
        out_ref[j] = boths[j][:, :128].astype(BF)
    flat = jnp.concatenate([norms, jnp.zeros((FPAD - FROWS, 128), F32)], axis=0).T
    high = flat.astype(BF).astype(F32)
    low = flat - high
    at = row + (FROWS - 16 - FEATS)
    for j in range(GROUP):
        tail = out_ref[j, FROWS - 16 :].astype(F32)
        pieces = (high[j : j + 1, :128], high[j : j + 1, 128:], low[j : j + 1, :128], low[j : j + 1, 128:])
        for i, piece in enumerate(pieces):
            tail = jnp.where(at == i, piece, tail)
        out_ref[j, FROWS - 16 :] = tail.astype(BF)


def prefix_kernel(place_ref, in_ref, out_ref):
    rows = in_ref.shape[1]
    row = lax.broadcasted_iota(jnp.int32, (rows, 128), 0) + (place_ref[0] & 1) * (FROWS // 2)
    row = jnp.where(row >= FROWS, row - FROWS, row)
    row = jnp.where(row >= FROWS, row - FROWS, row)
    high = (row == FEATS) | (row == FEATS + 1)
    low = (row == FEATS + 2) | (row == FEATS + 3)
    total = jnp.zeros((rows, 128), F32)
    for z in range(in_ref.shape[0]):
        both = total + pltpu.roll(total, rows - 2, 0)
        top = both.astype(BF).astype(F32)
        rest = pltpu.roll(both - top, 2, 0)
        out_ref[z] = jnp.where(high, top, jnp.where(low, rest, total)).astype(BF)
        total = total + in_ref[z].astype(F32)


def local_kernel(q_ref, k_ref, v_ref, select_ref, vector_ref, num_ref, den_ref):
    causal = lax.broadcasted_iota(jnp.int32, (TOK, TOK), 0) >= lax.broadcasted_iota(jnp.int32, (TOK, TOK), 1)
    lane = lax.broadcasted_iota(jnp.int32, (TOK, 128), 1)
    group = pl.program_id(0)

    @pl.when(group == 0)
    def _():
        den_ref[...] = jnp.zeros((TOK, 128), F32)

    den = den_ref[...]
    phis_q = [features(select_ref[j], q_ref[...], vector_ref) for j in range(GROUP)]
    phis_k = [features(select_ref[j], k_ref[...], vector_ref) for j in range(GROUP)]
    turned = [taller(p).T for p in phis_q]
    weights = [jnp.dot(turned[j], taller(phis_k[j]), preferred_element_type=F32) for j in range(GROUP)]
    weights = [jnp.where(causal, w, 0.0).astype(BF) for w in weights]
    boths = [jnp.dot(weights[j], with_ones(v_ref[:, column(j)]), preferred_element_type=F32) for j in range(GROUP)]
    for j in range(GROUP):
        num_ref[:, column(j)] = boths[j][:, :128].astype(BF)
        den = jnp.where(lane == group * GROUP + j, boths[j][:, 128:], den)
    den_ref[...] = den


def finish_kernel(num_ref, den_ref, q_ref, select_ref, vector_ref, state_ref, out_ref):
    lane = lax.broadcasted_iota(jnp.int32, (TOK, 128), 1)
    group = pl.program_id(0)
    at = FEATS - (FROWS - 16)
    phis = [features(select_ref[j], q_ref[...], vector_ref) for j in range(GROUP)]
    phis = [taller(p).T for p in phis]
    carried = [jnp.dot(phis[j], taller(state_ref[j]), preferred_element_type=F32) for j in range(GROUP)]
    dens = []
    for j in range(GROUP):
        tail = state_ref[j, FROWS - 16 :].astype(F32)
        n0 = tail[at : at + 1] + tail[at + 2 : at + 3]
        n1 = tail[at + 1 : at + 2] + tail[at + 3 : at + 4]
        phi32 = phis[j].astype(F32)
        den = jnp.where(lane == group * GROUP + j, den_ref[...], 0.0) + phi32[:, :128] * n0 + phi32[:, 128:] * n1
        dens.append(jnp.sum(den, axis=1, keepdims=True))
    for j in range(GROUP):
        out_ref[:, column(j)] = ((num_ref[:, column(j)].astype(F32) + carried[j]) / dens[j]).astype(BF)


def halves(core, refs):
    at = pl.ds(pl.multiple_of(core * HALF, 128), HALF)
    return [r.at[:, at] for r in refs]


def listed_rows(ids_ref, count_ref):
    lane = lax.broadcasted_iota(jnp.int32, (QROWS - TOK, HALF), 1)
    listed = jnp.full((QROWS - TOK, HALF), -1.0, F32)
    for i in range(LISTED):
        entry = jnp.where(i < count_ref[0], ids_ref[i], -1).astype(F32)
        listed = jnp.where(lane == i, entry, listed)
    return listed.astype(BF)


def pack_kernel(me_ref, ids_ref, count_ref, k_ref, v_ref, q_ref, out_ref, sems):
    copies = [
        pltpu.make_async_copy(half, out_ref.at[pl.ds(i * TOK, TOK)], sems.at[i])
        for i, half in enumerate(halves(1 - (me_ref[0] & 1), (k_ref, v_ref, q_ref)))
    ]
    for c in copies:
        c.start()
    out_ref[3 * TOK :] = listed_rows(ids_ref, count_ref)
    for c in copies:
        c.wait()


def own_kernel(me_ref, ids_ref, count_ref, k_ref, v_ref, q_ref, kv_ref, both_ref, sems):
    targets = (kv_ref.at[0, 0], kv_ref.at[0, 1], both_ref.at[0, pl.ds(0, TOK)])
    copies = [
        pltpu.make_async_copy(half, to, sems.at[i])
        for i, (half, to) in enumerate(zip(halves(me_ref[0] & 1, (k_ref, v_ref, q_ref)), targets, strict=True))
    ]
    for c in copies:
        c.start()
    both_ref[0, TOK:QROWS] = listed_rows(ids_ref, count_ref)
    for c in copies:
        c.wait()


def merge_kernel(mate_ref, kv_in, both_in, kv_ref, both_ref, sems):
    del kv_in, both_in
    pieces = ((pl.ds(0, TOK), kv_ref.at[1, 0]), (pl.ds(TOK, TOK), kv_ref.at[1, 1]), (pl.ds(2 * TOK, QROWS), both_ref.at[1]))
    copies = [pltpu.make_async_copy(mate_ref.at[at], to, sems.at[i]) for i, (at, to) in enumerate(pieces)]
    for c in copies:
        c.start()
    for c in copies:
        c.wait()


def search_kernel(me_ref, *refs):
    q_in, (found_ref, count_ref, wanted, ids, sems) = refs[:SIDE], refs[SIDE:]
    me = me_ref[0]
    core, y, x = me & 1, (me >> 1) & (SIDE - 1), me >> 3
    rows = pl.ds(TOK, QROWS - TOK)
    copies = [
        pltpu.make_async_copy(q_in[i].at[:, rows, pl.ds(0, 128)], ids.at[pl.ds(2 * i, 2)], sems.at[i]) for i in range(SIDE)
    ]
    for c in copies:
        c.start()
    for c in copies:
        c.wait()
    for r in range(2 * SIDE):
        wanted[r : r + 1] = ids[r].astype(F32).astype(jnp.int32)[0:1]
    pltpu.async_copy(wanted, found_ref, sems.at[SIDE]).wait()

    def search(r, carry):
        count = jnp.int32(0)
        for i in range(LISTED):
            entry = found_ref[r, i]
            xo, yo, co = entry >> 4, (entry >> 2) & (SIDE - 1), (entry >> 1) & 1
            mine = (entry >= 0) & jnp.where(core == 0, yo == y, xo == x)
            away = jnp.where(core == 0, xo - x, yo - y) & (SIDE - 1)
            found_ref[r, count] = (away * 2 + (co ^ core)) * 2 + (entry & 1)
            count = count + mine.astype(jnp.int32)
        count_ref[r] = count
        return carry

    lax.fori_loop(0, 2 * SIDE, search, 0)


def attend_kernel(own, base, readers, found, counts, *refs):
    groups = readers // 2
    q_in, kv_in, outs = refs[:groups], refs[groups : groups + SIDE], refs[groups + SIDE : readers + SIDE]
    q_buf, g_buf, s_buf, m_buf, a_buf, q_sems, g_sems = refs[readers + SIDE :]
    copies = [pltpu.make_async_copy(q_in[i], q_buf.at[pl.ds(2 * i, 2)], q_sems.at[i]) for i in range(groups)]
    for c in copies:
        c.start()
    lane = lax.broadcasted_iota(jnp.int32, (TOK, 128), 1)
    heads = [(h, slice(h * 128, (h + 1) * 128)) for h in range(HALF_HEADS)]

    def fetch(r, slot):
        def one(i, carry):
            code = found[base + r, i]
            rows = pl.ds(pl.multiple_of((code & 1) * BLK, BLK), BLK)
            for away in range(SIDE):

                @pl.when((code >> 2) == away)
                def _():
                    source = kv_in[away].at[(code >> 1) & 1, :, rows, :]
                    pltpu.make_async_copy(source, g_buf.at[slot, i], g_sems.at[slot, i]).start()

            return carry

        lax.fori_loop(0, counts[base + r], one, 0)

    def arrived(r, slot):
        def one(i, carry):
            source = kv_in[0].at[0, :, pl.ds(0, BLK), :]
            pltpu.make_async_copy(source, g_buf.at[slot, i], g_sems.at[slot, i]).wait()
            return carry

        lax.fori_loop(0, counts[base + r], one, 0)

    def blank(slot, i):
        g_buf[slot, i, 1] = jnp.zeros((BLK, HALF), BF)

    def reader(r, slot, out_ref):
        count = counts[base + r]
        pairs = (count + 1) >> 1

        @pl.when((count & 1) == 1)
        def _():
            blank(slot, count)

        if not own:

            @pl.when(count == 0)
            def _():
                blank(slot, 0)
                blank(slot, 1)

        def blocks(j, kind, at):
            return jnp.concatenate([g_buf[slot, 2 * j, kind, :, at], g_buf[slot, 2 * j + 1, kind, :, at]], axis=0)

        def score(j, fresh):
            for h, at in heads:
                s = lax.dot_general(q_buf[r, 0:TOK, at], blocks(j, 0, at), NT, preferred_element_type=F32)
                s0, s1 = s[:, :128], jnp.where(2 * j + 1 < count, s[:, 128:], NEG)
                if fresh:
                    s0 = jnp.where(count > 0, s0, NEG)
                s_buf[j, h, :, 0:128] = s0
                s_buf[j, h, :, 128:256] = s1
                m = jnp.maximum(s0, s1)
                m_buf[h] = m if fresh else jnp.maximum(m_buf[h], m)

        def weigh(j, fresh):
            for h, at in heads:
                m = m_buf[h]
                p = jnp.exp2(s_buf[j, h] * TO_LOG2 - jnp.concatenate([m, m], axis=1)).astype(BF)
                a = jnp.dot(p, with_ones(blocks(j, 1, at)), preferred_element_type=F32)
                a_buf[h] = a if fresh else a_buf[h] + a

        if own:
            for h, at in heads:
                parts = []
                for b in range(2):
                    rows = slice(b * BLK, (b + 1) * BLK)
                    k = own_kv[r, 0, rows, at]
                    parts.append(lax.dot_general(q_buf[r, rows, at], k, NT, preferred_element_type=F32))
                s = jnp.concatenate(parts, axis=0)
                s_buf[LISTED // 2, h, :, 0:128] = s
                m_buf[h] = s
        else:
            score(0, True)
        start = 0 if own else 1

        def more_scores(j, carry):
            score(j, False)
            return carry

        lax.fori_loop(start, pairs, more_scores, 0)
        tops = jnp.zeros((TOK, 128), F32)
        for h, at in heads:
            m = jnp.broadcast_to(jnp.max(m_buf[h], axis=1, keepdims=True) * TO_LOG2, (TOK, 128))
            m_buf[h] = m
            tops = jnp.where(lane == h, m, tops)
        if own:
            for h, at in heads:
                p = jnp.exp2(s_buf[LISTED // 2, h, :, 0:128] * TO_LOG2 - m_buf[h]).astype(BF)
                parts = []
                for b in range(2):
                    rows = slice(b * BLK, (b + 1) * BLK)
                    v = with_ones(own_kv[r, 1, rows, at])
                    parts.append(jnp.dot(p[rows], v, preferred_element_type=F32))
                a_buf[h] = jnp.concatenate(parts, axis=0)
        else:
            weigh(0, True)

        def more_weights(j, carry):
            weigh(j, False)
            return carry

        lax.fori_loop(start, pairs, more_weights, 0)
        totals = jnp.ones((TOK, 128), F32)
        for h, at in heads:
            total = a_buf[h, :, 128:]
            out_ref[slot, 0:TOK, at] = (a_buf[h, :, :128] / total).astype(BF)
            totals = jnp.where(lane == h, total, totals)
        sizes = tops + jnp.log2(totals)
        if not own:
            sizes = jnp.where(jnp.logical_and(count == 0, lane < HALF_HEADS), NEG, sizes)
        high = sizes.astype(BF).astype(F32)
        middle = (sizes - high).astype(BF).astype(F32)
        low = sizes - high - middle
        packed = high + pltpu.roll(middle, HALF_HEADS, 1) + pltpu.roll(low, 2 * HALF_HEADS, 1)
        out_ref[slot, TOK:QROWS, :] = jnp.zeros((QROWS - TOK, HALF), BF)
        out_ref[slot, TOK:QROWS, 0:TOK] = packed.T[0 : QROWS - TOK].astype(BF)

    own_kv = kv_in[0]
    fetch(0, 0)
    for c in copies:
        c.wait()
    for g, out_ref in enumerate(outs):

        def one(i, carry, g=g, out_ref=out_ref):
            r = 2 * g + i

            @pl.when(r + 1 < readers)
            def _():
                fetch(r + 1, 1 - i)

            arrived(r, i)
            reader(r, i, out_ref)
            return carry

        lax.fori_loop(0, 2, one, 0)


def join_kernel(*refs):
    parts, outs, size_ref = refs[:4], refs[4:6], refs[6]
    for r in range(2):
        for i, p in enumerate(parts):
            packed = p[r, TOK:QROWS, 0:TOK].astype(F32)
            packed = jnp.concatenate([packed, jnp.zeros((128 - (QROWS - TOK), TOK), F32)], axis=0).T
            size_ref[r, i] = packed + pltpu.roll(packed, 128 - HALF_HEADS, 1) + pltpu.roll(packed, 128 - 2 * HALF_HEADS, 1)
    for r in range(2):
        for t in range(TOK // JOIN_ROWS):
            rows = slice(t * JOIN_ROWS, (t + 1) * JOIN_ROWS)
            sizes = [size_ref[r, i, rows] for i in range(4)]
            top = functools.reduce(jnp.maximum, sizes)
            shares = [jnp.exp2(s - top) for s in sizes]
            total = functools.reduce(jnp.add, shares)
            shares = [s / total for s in shares]
            for h in range(HALF_HEADS):
                at = slice(h * 128, (h + 1) * 128)
                o = sum(s[:, h : h + 1] * p[r, rows, at].astype(F32) for s, p in zip(shares, parts, strict=True))
                outs[r][rows, at] = o.astype(BF)


def place_kernel(me_ref, kept_ref, other_ref, out_ref, sems):
    core = me_ref[0] & 1
    copies = [
        pltpu.make_async_copy(half, to, sems.at[i])
        for i, (half, to) in enumerate(zip((kept_ref, other_ref), halves(core, (out_ref,)) + halves(1 - core, (out_ref,)), strict=True))
    ]
    for c in copies:
        c.start()
    for c in copies:
        c.wait()


def shape(*dims, dtype=BF):
    return jax.ShapeDtypeStruct(dims, dtype)


SMEM = pl.BlockSpec(memory_space=pltpu.SMEM)
VMEM = pl.BlockSpec(memory_space=pltpu.VMEM)
ANY = pl.BlockSpec(memory_space=pl.ANY)
HBM = pl.BlockSpec(memory_space=pltpu.HBM)


def room(mib):
    return pltpu.CompilerParams(vmem_limit_bytes=mib * 1024 * 1024)


def cost(flops, moved):
    return pl.CostEstimate(flops=int(flops), bytes_accessed=int(moved), transcendentals=0)


def in_hbm(*arrays):
    return tuple(pltpu.with_memory_space_constraint(a, pltpu.HBM) for a in arrays)


def hbm_shape(*dims, dtype=BF):
    return pltpu.HBM(dims, dtype)


def whole(*dims):
    return pl.BlockSpec(dims, lambda g: (0,) * len(dims))


def attend(name, base, lists, queries, blocks):
    own = name == "attend_own"
    groups = len(queries)
    readers = 2 * groups
    first = VMEM if own else ANY
    return pl.pallas_call(
        functools.partial(attend_kernel, own, base, readers),
        out_shape=[shape(2, QROWS, HALF)] * groups,
        in_specs=[SMEM, SMEM] + [ANY] * groups + [first] + [ANY] * (SIDE - 1),
        out_specs=[VMEM] * groups,
        scratch_shapes=[
            pltpu.VMEM((readers, QROWS, HALF), BF),
            pltpu.VMEM((2, LISTED, 2, BLK, HALF), BF),
            pltpu.VMEM((LISTED // 2 + 1, HALF_HEADS, TOK, 256), F32),
            pltpu.VMEM((HALF_HEADS, TOK, 128), F32),
            pltpu.VMEM((HALF_HEADS, TOK, 256), F32),
            pltpu.SemaphoreType.DMA((groups,)),
            pltpu.SemaphoreType.DMA((2, LISTED)),
        ],
        compiler_params=room(18),
        cost_estimate=cost(readers * 4e8, 8e6),
    )(*lists, *queries, *blocks)


def layers(q_lin, k_lin, v_lin, q_soft, k_soft, v_soft, import_ids, import_counts):
    select, vectors = (jnp.asarray(t) for t in feature_tables())
    me = lax.axis_index("files").astype(jnp.int32).reshape(1)
    place = lax.axis_index("seq").astype(jnp.int32).reshape(1)
    shards = lax.axis_size("seq")
    steps = (HEADS // GROUP,)
    heads16 = pl.BlockSpec((GROUP * FEAT, TOK), lambda g: (g, 0))
    heads128 = pl.BlockSpec((TOK, GROUP * 128), lambda g: (0, g))
    mine = (me, import_ids[0, 0], import_counts[0]) + in_hbm(k_soft[0], v_soft[0], q_soft[0])

    sent = pl.pallas_call(
        pack_kernel,
        name="pack",
        out_shape=shape(2 * TOK + QROWS, HALF),
        in_specs=[SMEM] * 3 + [HBM] * 3,
        out_specs=VMEM,
        scratch_shapes=[pltpu.SemaphoreType.DMA((3,))],
        compiler_params=room(4),
        cost_estimate=cost(0, 2e6),
    )(*mine)
    mate = swap_cores(sent)
    pair = [shape(2, 2, TOK, HALF), shape(2, QROWS, HALF)]
    kv, q = pl.pallas_call(
        own_kernel,
        name="own",
        out_shape=pair,
        in_specs=[SMEM] * 3 + [HBM] * 3,
        out_specs=[VMEM] * 2,
        scratch_shapes=[pltpu.SemaphoreType.DMA((3,))],
        compiler_params=room(6),
        cost_estimate=cost(0, 2e6),
    )(*mine)

    kv, q = pl.pallas_call(
        merge_kernel,
        name="merge",
        out_shape=pair,
        in_specs=[VMEM, ANY, ANY],
        out_specs=[ANY] * 2,
        scratch_shapes=[pltpu.SemaphoreType.DMA((3,))],
        input_output_aliases={1: 0, 2: 1},
        compiler_params=room(4),
        cost_estimate=cost(0, 2e6),
    )(mate, kv, q)
    kv_right = move(kv, "kv", -1)
    kv_left = move(kv, "kv", 1)
    q_left = move(q, "q", 1)
    q_right = move(q, "q", -1)
    kv_far = move(kv_right, "kv", -1)
    q_far = move(q_left, "q", 1)

    state = pl.pallas_call(
        state_kernel,
        name="state",
        grid=steps,
        out_shape=hbm_shape(HEADS, FROWS, 128),
        in_specs=[heads16, heads128, whole(*select.shape), whole(*vectors.shape)],
        out_specs=pl.BlockSpec((GROUP, FROWS, 128), lambda g: (g, 0, 0)),
        compiler_params=room(8),
        cost_estimate=cost(1e9, 4e6),
    )(*in_hbm(k_lin[0].T, v_lin[0], select, vectors))
    slices = lax.all_to_all(state.reshape(shards, HEADS * FROWS // shards, 128), "seq", 0, 0, tiled=True)

    num, den = pl.pallas_call(
        local_kernel,
        name="local",
        grid=steps,
        out_shape=[hbm_shape(TOK, D), hbm_shape(TOK, 128, dtype=F32)],
        in_specs=[heads16, heads16, heads128, whole(*select.shape), whole(*vectors.shape)],
        out_specs=[heads128, whole(TOK, 128)],
        compiler_params=room(10),
        cost_estimate=cost(4e9, 8e6),
    )(*in_hbm(q_lin[0].T, k_lin[0].T, v_lin[0], select, vectors))

    blocks = (kv, kv_right, kv_far, kv_left)
    lists = pl.pallas_call(
        search_kernel,
        name="search",
        out_shape=[shape(2 * SIDE, 128, dtype=jnp.int32), shape(2 * SIDE, dtype=jnp.int32)],
        in_specs=[SMEM] + [ANY] * SIDE,
        out_specs=[SMEM] * 2,
        scratch_shapes=[
            pltpu.VMEM((2 * SIDE, 128), jnp.int32),
            pltpu.VMEM((2 * SIDE, QROWS - TOK, 128), BF),
            pltpu.SemaphoreType.DMA((SIDE + 1,)),
        ],
        compiler_params=room(2),
        cost_estimate=cost(0, 1e5),
    )(me, q_far, q_left, q_right, q)
    slices, num, den, *lists = lax.optimization_barrier((slices, num, den, *lists))
    prefix = pl.pallas_call(
        prefix_kernel,
        name="prefix",
        out_shape=hbm_shape(*slices.shape),
        in_specs=[SMEM, VMEM],
        out_specs=VMEM,
        compiler_params=room(6),
        cost_estimate=cost(0, 2e6),
    )(place, slices)
    before = lax.all_to_all(prefix, "seq", 0, 0, tiled=True).reshape(HEADS, FROWS, 128)
    (to_far,) = attend("attend_far", 0, lists, (q_far,), blocks)
    to_far, q_left, q_right = lax.optimization_barrier((to_far, q_left, q_right))
    from_far = move(to_far, "q", 2)
    to_left, to_right = attend("attend_sides", 2, lists, (q_left, q_right), blocks)
    from_right = move(to_left, "q", -1)
    from_left = move(to_right, "q", 1)
    (here,) = attend("attend_own", 6, lists, (q,), blocks)
    kept, send = pl.pallas_call(
        join_kernel,
        name="join",
        out_shape=[shape(TOK, HALF)] * 2,
        in_specs=[VMEM] * 4,
        out_specs=[VMEM] * 2,
        scratch_shapes=[pltpu.VMEM((2, 4, TOK, 128), F32)],
        compiler_params=room(8),
        cost_estimate=cost(0, 4e6),
    )(here, from_right, from_left, from_far)
    other = swap_cores(send)
    soft_out = pl.pallas_call(
        place_kernel,
        name="place",
        out_shape=shape(TOK, SM_W),
        in_specs=[SMEM, VMEM, VMEM],
        out_specs=HBM,
        scratch_shapes=[pltpu.SemaphoreType.DMA((2,))],
        compiler_params=room(4),
        cost_estimate=cost(0, 1e6),
    )(me, kept, other)

    lin_out = pl.pallas_call(
        finish_kernel,
        name="finish",
        grid=steps,
        out_shape=shape(TOK, D),
        in_specs=[
            heads128,
            whole(TOK, 128),
            heads16,
            whole(*select.shape),
            whole(*vectors.shape),
            pl.BlockSpec((GROUP, FROWS, 128), lambda g: (g, 0, 0)),
        ],
        out_specs=heads128,
        compiler_params=room(8),
        cost_estimate=cost(4e8, 8e6),
    )(*in_hbm(num, den, q_lin[0].T, select, vectors), before)
    return lin_out[None], soft_out[None]


def solution(mesh):
    wide = P("files", "seq", None)
    return jax.shard_map(
        layers,
        mesh=mesh,
        in_specs=(wide,) * 7 + (P("files", "seq"),),
        out_specs=(wide, wide),
        check_vma=False,
    )
```

```python
import functools
import math

import jax
import jax.numpy as jnp
import numpy as np
from jax import lax
from jax.experimental import pallas as pl
from jax.experimental.pallas import tpu as pltpu
from jax.sharding import PartitionSpec as P

D = 2560
HEADS = 20
FEAT = 16
FEATS = 153
FROWS = 160
FPAD = 256
SM_HD = 128
SM_W = 1280
BLK = 128
TOK = 256
LISTED = 8
GROUP = 4
HALF = 640
HALF_HEADS = 5
QROWS = 272
SIDE = 4
CORES = 2
JOIN_ROWS = 64

inv_root_two = 0.7071067811865476
TO_LOG2 = math.log2(math.e) / math.sqrt(SM_HD)
NEG = -1e30
BF = jnp.bfloat16
F32 = jnp.float32
NT = (((1,), (1,)), ((), ()))


def along(what, step):
    pairs = []
    for x in range(SIDE):
        for y in range(SIDE):
            for c in range(CORES):
                on_x = (c == 0) == (what == "kv")
                x2 = (x + step) % SIDE if on_x else x
                y2 = y if on_x else (y + step) % SIDE
                pairs.append(((x * SIDE + y) * CORES + c, (x2 * SIDE + y2) * CORES + c))
    return pairs


def move(a, what, step):
    return lax.ppermute(a, "files", along(what, step))


def swap_cores(a):
    return lax.ppermute(a, "files", [(i, i ^ 1) for i in range(SIDE * SIDE * CORES)])


def feature_tables():
    rows, cols = np.triu_indices(FEAT)
    select = np.zeros((GROUP, 2, FROWS, GROUP * FEAT), np.float32)
    for j in range(GROUP):
        for f in range(FEAT):
            select[j, 0, 1 + f, j * FEAT + f] = 0.5
        for n in range(len(rows)):
            select[j, 0, 1 + FEAT + n, j * FEAT + rows[n]] = 0.5
            select[j, 1, 1 + FEAT + n, j * FEAT + cols[n]] = 0.5
    vectors = np.zeros((3, FROWS), np.float32)
    vectors[0, 0] = 1.0
    vectors[1, : 1 + FEAT] = 1.0
    vectors[2, :FEATS] = 1.0
    vectors[2, 1 + FEAT : FEATS] = np.where(rows == cols, inv_root_two, 1.0).astype(np.float32)
    vectors = np.ascontiguousarray(np.broadcast_to(vectors[:, :, None], (3, FROWS, 128)))
    return select.reshape(GROUP, 2 * FROWS, GROUP * FEAT).astype(jnp.bfloat16), vectors


def column(j):
    return slice(j * 128, (j + 1) * 128)


def features(select, x, vectors):
    first, second, factor = (jnp.concatenate([vectors[i], vectors[i]], axis=1) for i in range(3))
    ab = jnp.dot(select, x, preferred_element_type=F32)
    return ((ab[:FROWS] + first) * (ab[FROWS:] + second) * factor).astype(BF)


def taller(phi):
    return jnp.concatenate([phi, jnp.zeros((FPAD - FROWS, phi.shape[1]), BF)], axis=0)


def with_ones(values):
    return jnp.concatenate([values, jnp.ones(values.shape, BF)], axis=1)


def state_kernel(k_ref, v_ref, select_ref, vector_ref, out_ref):
    row = lax.broadcasted_iota(jnp.int32, (16, 128), 0)
    lane = lax.broadcasted_iota(jnp.int32, (FROWS, 128), 1)
    norms = jnp.zeros((FROWS, 128), F32)
    phis = [features(select_ref[j], k_ref[...], vector_ref) for j in range(GROUP)]
    boths = [jnp.dot(phis[j], with_ones(v_ref[:, column(j)]), preferred_element_type=F32) for j in range(GROUP)]
    for j in range(GROUP):
        norms = jnp.where(lane == j, boths[j][:, 128:], norms)
        out_ref[j] = boths[j][:, :128].astype(BF)
    flat = jnp.concatenate([norms, jnp.zeros((FPAD - FROWS, 128), F32)], axis=0).T
    high = flat.astype(BF).astype(F32)
    low = flat - high
    at = row + (FROWS - 16 - FEATS)
    for j in range(GROUP):
        tail = out_ref[j, FROWS - 16 :].astype(F32)
        pieces = (high[j : j + 1, :128], high[j : j + 1, 128:], low[j : j + 1, :128], low[j : j + 1, 128:])
        for i, piece in enumerate(pieces):
            tail = jnp.where(at == i, piece, tail)
        out_ref[j, FROWS - 16 :] = tail.astype(BF)


def prefix_kernel(place_ref, in_ref, out_ref):
    rows = in_ref.shape[1]
    row = lax.broadcasted_iota(jnp.int32, (rows, 128), 0) + ((place_ref[0] + pl.program_id(0)) & 1) * rows
    high = (row == FEATS) | (row == FEATS + 1)
    low = (row == FEATS + 2) | (row == FEATS + 3)
    total = jnp.zeros((rows, 128), F32)
    for z in range(in_ref.shape[0]):
        both = total + pltpu.roll(total, rows - 2, 0)
        top = both.astype(BF).astype(F32)
        rest = pltpu.roll(both - top, 2, 0)
        out_ref[z] = jnp.where(high, top, jnp.where(low, rest, total)).astype(BF)
        total = total + in_ref[z].astype(F32)


def local_kernel(q_ref, k_ref, v_ref, select_ref, vector_ref, num_ref, den_ref, phi_ref):
    causal = lax.broadcasted_iota(jnp.int32, (TOK, TOK), 0) >= lax.broadcasted_iota(jnp.int32, (TOK, TOK), 1)
    lane = lax.broadcasted_iota(jnp.int32, (TOK, 128), 1)
    group = pl.program_id(0)

    @pl.when(group == 0)
    def _():
        den_ref[...] = jnp.zeros((TOK, 128), F32)

    den = den_ref[...]
    phis_q = [features(select_ref[j], q_ref[...], vector_ref) for j in range(GROUP)]
    phis_k = [features(select_ref[j], k_ref[...], vector_ref) for j in range(GROUP)]
    for j in range(GROUP):
        phi_ref[j] = phis_q[j]
    turned = [taller(p).T for p in phis_q]
    weights = [jnp.dot(turned[j], taller(phis_k[j]), preferred_element_type=F32) for j in range(GROUP)]
    weights = [jnp.where(causal, w, 0.0).astype(BF) for w in weights]
    boths = [jnp.dot(weights[j], with_ones(v_ref[:, column(j)]), preferred_element_type=F32) for j in range(GROUP)]
    for j in range(GROUP):
        num_ref[:, column(j)] = boths[j][:, :128].astype(BF)
        den = jnp.where(lane == group * GROUP + j, boths[j][:, 128:], den)
    den_ref[...] = den


def finish_kernel(num_ref, den_ref, phi_ref, state_ref, out_ref):
    lane = lax.broadcasted_iota(jnp.int32, (TOK, 128), 1)
    group = pl.program_id(0)
    at = FEATS - (FROWS - 16)
    phis = [taller(phi_ref[j]).T for j in range(GROUP)]
    carried = [jnp.dot(phis[j], taller(state_ref[j]), preferred_element_type=F32) for j in range(GROUP)]
    dens = []
    for j in range(GROUP):
        tail = state_ref[j, FROWS - 16 :].astype(F32)
        n0 = tail[at : at + 1] + tail[at + 2 : at + 3]
        n1 = tail[at + 1 : at + 2] + tail[at + 3 : at + 4]
        phi32 = phis[j].astype(F32)
        den = jnp.where(lane == group * GROUP + j, den_ref[...], 0.0) + phi32[:, :128] * n0 + phi32[:, 128:] * n1
        dens.append(jnp.sum(den, axis=1, keepdims=True))
    for j in range(GROUP):
        out_ref[:, column(j)] = ((num_ref[:, column(j)].astype(F32) + carried[j]) / dens[j]).astype(BF)


def halves(core, refs):
    at = pl.ds(pl.multiple_of(core * HALF, 128), HALF)
    return [r.at[:, at] for r in refs]


def listed_rows(ids_ref, count_ref):
    lane = lax.broadcasted_iota(jnp.int32, (QROWS - TOK, HALF), 1)
    listed = jnp.full((QROWS - TOK, HALF), -1.0, F32)
    for i in range(LISTED):
        entry = jnp.where(i < count_ref[0], ids_ref[i], -1).astype(F32)
        listed = jnp.where(lane == i, entry, listed)
    return listed.astype(BF)


def pack_kernel(me_ref, ids_ref, count_ref, k_ref, v_ref, q_ref, out_ref, sems):
    copies = [
        pltpu.make_async_copy(half, out_ref.at[pl.ds(i * TOK, TOK)], sems.at[i])
        for i, half in enumerate(halves(1 - (me_ref[0] & 1), (k_ref, v_ref, q_ref)))
    ]
    for c in copies:
        c.start()
    out_ref[3 * TOK :] = listed_rows(ids_ref, count_ref)
    for c in copies:
        c.wait()


def own_kernel(me_ref, ids_ref, count_ref, k_ref, v_ref, q_ref, kv_ref, both_ref, sems):
    targets = (kv_ref.at[0, 0], kv_ref.at[0, 1], both_ref.at[0, pl.ds(0, TOK)])
    copies = [
        pltpu.make_async_copy(half, to, sems.at[i])
        for i, (half, to) in enumerate(zip(halves(me_ref[0] & 1, (k_ref, v_ref, q_ref)), targets, strict=True))
    ]
    for c in copies:
        c.start()
    both_ref[0, TOK:QROWS] = listed_rows(ids_ref, count_ref)
    for c in copies:
        c.wait()


def merge_kernel(mate_ref, kv_in, both_in, kv_ref, both_ref, sems):
    del kv_in, both_in
    pieces = ((pl.ds(0, TOK), kv_ref.at[1, 0]), (pl.ds(TOK, TOK), kv_ref.at[1, 1]), (pl.ds(2 * TOK, QROWS), both_ref.at[1]))
    copies = [pltpu.make_async_copy(mate_ref.at[at], to, sems.at[i]) for i, (at, to) in enumerate(pieces)]
    for c in copies:
        c.start()
    for c in copies:
        c.wait()


def search_kernel(me_ref, *refs):
    q_in, (found_ref, count_ref, wanted, ids, sems) = refs[:SIDE], refs[SIDE:]
    me = me_ref[0]
    core, y, x = me & 1, (me >> 1) & (SIDE - 1), me >> 3
    rows = pl.ds(TOK, QROWS - TOK)
    copies = [
        pltpu.make_async_copy(q_in[i].at[:, rows, pl.ds(0, 128)], ids.at[pl.ds(2 * i, 2)], sems.at[i]) for i in range(SIDE)
    ]
    for c in copies:
        c.start()
    for c in copies:
        c.wait()
    for r in range(2 * SIDE):
        wanted[r : r + 1] = ids[r].astype(F32).astype(jnp.int32)[0:1]
    pltpu.async_copy(wanted, found_ref, sems.at[SIDE]).wait()

    def search(r, carry):
        count = jnp.int32(0)
        for i in range(LISTED):
            entry = found_ref[r, i]
            xo, yo, co = entry >> 4, (entry >> 2) & (SIDE - 1), (entry >> 1) & 1
            mine = (entry >= 0) & jnp.where(core == 0, yo == y, xo == x)
            away = jnp.where(core == 0, xo - x, yo - y) & (SIDE - 1)
            found_ref[r, count] = (away * 2 + (co ^ core)) * 2 + (entry & 1)
            count = count + mine.astype(jnp.int32)
        count_ref[r] = count
        return carry

    lax.fori_loop(0, 2 * SIDE, search, 0)


def attend_kernel(own, base, readers, found, counts, *refs):
    groups = readers // 2
    q_in, kv_in, outs = refs[:groups], refs[groups : groups + SIDE], refs[groups + SIDE : readers + SIDE]
    q_buf, g_buf, s_buf, m_buf, a_buf, q_sems, g_sems = refs[readers + SIDE :]
    copies = [pltpu.make_async_copy(q_in[i], q_buf.at[pl.ds(2 * i, 2)], q_sems.at[i]) for i in range(groups)]
    for c in copies:
        c.start()
    lane = lax.broadcasted_iota(jnp.int32, (TOK, 128), 1)
    heads = [(h, slice(h * 128, (h + 1) * 128)) for h in range(HALF_HEADS)]

    def fetch(r, slot):
        def one(i, carry):
            code = found[base + r, i]
            rows = pl.ds(pl.multiple_of((code & 1) * BLK, BLK), BLK)
            for away in range(SIDE):

                @pl.when((code >> 2) == away)
                def _():
                    source = kv_in[away].at[(code >> 1) & 1, :, rows, :]
                    pltpu.make_async_copy(source, g_buf.at[slot, i], g_sems.at[slot, i]).start()

            return carry

        lax.fori_loop(0, counts[base + r], one, 0)

    def arrived(r, slot):
        def one(i, carry):
            source = kv_in[0].at[0, :, pl.ds(0, BLK), :]
            pltpu.make_async_copy(source, g_buf.at[slot, i], g_sems.at[slot, i]).wait()
            return carry

        lax.fori_loop(0, counts[base + r], one, 0)

    def blank(slot, i):
        g_buf[slot, i, 1] = jnp.zeros((BLK, HALF), BF)

    def reader(r, slot, out_ref):
        count = counts[base + r]
        pairs = (count + 1) >> 1

        @pl.when((count & 1) == 1)
        def _():
            blank(slot, count)

        if not own:

            @pl.when(count == 0)
            def _():
                blank(slot, 0)
                blank(slot, 1)

        def blocks(j, kind, at):
            return jnp.concatenate([g_buf[slot, 2 * j, kind, :, at], g_buf[slot, 2 * j + 1, kind, :, at]], axis=0)

        def score(j, fresh):
            for h, at in heads:
                s = lax.dot_general(q_buf[r, 0:TOK, at], blocks(j, 0, at), NT, preferred_element_type=F32)
                s0, s1 = s[:, :128], jnp.where(2 * j + 1 < count, s[:, 128:], NEG)
                if fresh:
                    s0 = jnp.where(count > 0, s0, NEG)
                s_buf[j, h, :, 0:128] = s0
                s_buf[j, h, :, 128:256] = s1
                m = jnp.maximum(s0, s1)
                m_buf[h] = m if fresh else jnp.maximum(m_buf[h], m)

        def weigh(j, fresh):
            for h, at in heads:
                m = m_buf[h]
                p = jnp.exp2(s_buf[j, h] * TO_LOG2 - jnp.concatenate([m, m], axis=1)).astype(BF)
                a = jnp.dot(p, with_ones(blocks(j, 1, at)), preferred_element_type=F32)
                a_buf[h] = a if fresh else a_buf[h] + a

        if own:
            for h, at in heads:
                parts = []
                for b in range(2):
                    rows = slice(b * BLK, (b + 1) * BLK)
                    k = own_kv[r, 0, rows, at]
                    parts.append(lax.dot_general(q_buf[r, rows, at], k, NT, preferred_element_type=F32))
                s = jnp.concatenate(parts, axis=0)
                s_buf[LISTED // 2, h, :, 0:128] = s
                m_buf[h] = s
        else:
            score(0, True)
        start = 0 if own else 1

        def more_scores(j, carry):
            score(j, False)
            return carry

        lax.fori_loop(start, pairs, more_scores, 0)
        tops = jnp.zeros((TOK, 128), F32)
        for h, at in heads:
            m = jnp.broadcast_to(jnp.max(m_buf[h], axis=1, keepdims=True) * TO_LOG2, (TOK, 128))
            m_buf[h] = m
            tops = jnp.where(lane == h, m, tops)
        if own:
            for h, at in heads:
                p = jnp.exp2(s_buf[LISTED // 2, h, :, 0:128] * TO_LOG2 - m_buf[h]).astype(BF)
                parts = []
                for b in range(2):
                    rows = slice(b * BLK, (b + 1) * BLK)
                    v = with_ones(own_kv[r, 1, rows, at])
                    parts.append(jnp.dot(p[rows], v, preferred_element_type=F32))
                a_buf[h] = jnp.concatenate(parts, axis=0)
        else:
            weigh(0, True)

        def more_weights(j, carry):
            weigh(j, False)
            return carry

        lax.fori_loop(start, pairs, more_weights, 0)
        totals = jnp.ones((TOK, 128), F32)
        for h, at in heads:
            total = a_buf[h, :, 128:]
            out_ref[slot, 0:TOK, at] = (a_buf[h, :, :128] / total).astype(BF)
            totals = jnp.where(lane == h, total, totals)
        sizes = tops + jnp.log2(totals)
        if not own:
            sizes = jnp.where(jnp.logical_and(count == 0, lane < HALF_HEADS), NEG, sizes)
        high = sizes.astype(BF).astype(F32)
        middle = (sizes - high).astype(BF).astype(F32)
        low = sizes - high - middle
        packed = high + pltpu.roll(middle, HALF_HEADS, 1) + pltpu.roll(low, 2 * HALF_HEADS, 1)
        out_ref[slot, TOK:QROWS, :] = jnp.zeros((QROWS - TOK, HALF), BF)
        out_ref[slot, TOK:QROWS, 0:TOK] = packed.T[0 : QROWS - TOK].astype(BF)

    own_kv = kv_in[0]
    fetch(0, 0)
    for c in copies:
        c.wait()
    for g, out_ref in enumerate(outs):

        def one(i, carry, g=g, out_ref=out_ref):
            r = 2 * g + i

            @pl.when(r + 1 < readers)
            def _():
                fetch(r + 1, 1 - i)

            arrived(r, i)
            reader(r, i, out_ref)
            return carry

        lax.fori_loop(0, 2, one, 0)


def join_kernel(*refs):
    parts, outs, size_ref = refs[:4], refs[4:6], refs[6]
    for r in range(2):
        for i, p in enumerate(parts):
            packed = p[r, TOK:QROWS, 0:TOK].astype(F32)
            packed = jnp.concatenate([packed, jnp.zeros((128 - (QROWS - TOK), TOK), F32)], axis=0).T
            size_ref[r, i] = packed + pltpu.roll(packed, 128 - HALF_HEADS, 1) + pltpu.roll(packed, 128 - 2 * HALF_HEADS, 1)
    for r in range(2):
        for t in range(TOK // JOIN_ROWS):
            rows = slice(t * JOIN_ROWS, (t + 1) * JOIN_ROWS)
            sizes = [size_ref[r, i, rows] for i in range(4)]
            top = functools.reduce(jnp.maximum, sizes)
            shares = [jnp.exp2(s - top) for s in sizes]
            total = functools.reduce(jnp.add, shares)
            shares = [s / total for s in shares]
            for h in range(HALF_HEADS):
                at = slice(h * 128, (h + 1) * 128)
                o = sum(s[:, h : h + 1] * p[r, rows, at].astype(F32) for s, p in zip(shares, parts, strict=True))
                outs[r][rows, at] = o.astype(BF)


def place_kernel(me_ref, kept_ref, other_ref, out_ref, sems):
    core = me_ref[0] & 1
    copies = [
        pltpu.make_async_copy(half, to, sems.at[i])
        for i, (half, to) in enumerate(zip((kept_ref, other_ref), halves(core, (out_ref,)) + halves(1 - core, (out_ref,)), strict=True))
    ]
    for c in copies:
        c.start()
    for c in copies:
        c.wait()


def shape(*dims, dtype=BF):
    return jax.ShapeDtypeStruct(dims, dtype)


SMEM = pl.BlockSpec(memory_space=pltpu.SMEM)
VMEM = pl.BlockSpec(memory_space=pltpu.VMEM)
ANY = pl.BlockSpec(memory_space=pl.ANY)
HBM = pl.BlockSpec(memory_space=pltpu.HBM)


def room(mib):
    return pltpu.CompilerParams(vmem_limit_bytes=mib * 1024 * 1024)


def cost(flops, moved):
    return pl.CostEstimate(flops=int(flops), bytes_accessed=int(moved), transcendentals=0)


def in_hbm(*arrays):
    return tuple(pltpu.with_memory_space_constraint(a, pltpu.HBM) for a in arrays)


def hbm_shape(*dims, dtype=BF):
    return pltpu.HBM(dims, dtype)


def whole(*dims):
    return pl.BlockSpec(dims, lambda g: (0,) * len(dims))


def attend(name, base, lists, queries, blocks):
    own = name == "attend_own"
    groups = len(queries)
    readers = 2 * groups
    first = VMEM if own else ANY
    return pl.pallas_call(
        functools.partial(attend_kernel, own, base, readers),
        out_shape=[shape(2, QROWS, HALF)] * groups,
        in_specs=[SMEM, SMEM] + [ANY] * groups + [first] + [ANY] * (SIDE - 1),
        out_specs=[VMEM] * groups,
        scratch_shapes=[
            pltpu.VMEM((readers, QROWS, HALF), BF),
            pltpu.VMEM((2, LISTED, 2, BLK, HALF), BF),
            pltpu.VMEM((LISTED // 2 + 1, HALF_HEADS, TOK, 256), F32),
            pltpu.VMEM((HALF_HEADS, TOK, 128), F32),
            pltpu.VMEM((HALF_HEADS, TOK, 256), F32),
            pltpu.SemaphoreType.DMA((groups,)),
            pltpu.SemaphoreType.DMA((2, LISTED)),
        ],
        compiler_params=room(18),
        cost_estimate=cost(readers * 4e8, 8e6),
    )(*lists, *queries, *blocks)


def layers(q_lin, k_lin, v_lin, q_soft, k_soft, v_soft, import_ids, import_counts):
    select, vectors = (jnp.asarray(t) for t in feature_tables())
    me = lax.axis_index("files").astype(jnp.int32).reshape(1)
    place = lax.axis_index("seq").astype(jnp.int32).reshape(1)
    shards = lax.axis_size("seq")
    steps = (HEADS // GROUP,)
    heads16 = pl.BlockSpec((GROUP * FEAT, TOK), lambda g: (g, 0))
    heads128 = pl.BlockSpec((TOK, GROUP * 128), lambda g: (0, g))
    mine = (me, import_ids[0, 0], import_counts[0]) + in_hbm(k_soft[0], v_soft[0], q_soft[0])

    sent = pl.pallas_call(
        pack_kernel,
        name="pack",
        out_shape=shape(2 * TOK + QROWS, HALF),
        in_specs=[SMEM] * 3 + [HBM] * 3,
        out_specs=VMEM,
        scratch_shapes=[pltpu.SemaphoreType.DMA((3,))],
        compiler_params=room(4),
        cost_estimate=cost(0, 2e6),
    )(*mine)
    mate = swap_cores(sent)
    pair = [shape(2, 2, TOK, HALF), shape(2, QROWS, HALF)]
    kv, q = pl.pallas_call(
        own_kernel,
        name="own",
        out_shape=pair,
        in_specs=[SMEM] * 3 + [HBM] * 3,
        out_specs=[VMEM] * 2,
        scratch_shapes=[pltpu.SemaphoreType.DMA((3,))],
        compiler_params=room(6),
        cost_estimate=cost(0, 2e6),
    )(*mine)

    kv, q = pl.pallas_call(
        merge_kernel,
        name="merge",
        out_shape=pair,
        in_specs=[VMEM, ANY, ANY],
        out_specs=[ANY] * 2,
        scratch_shapes=[pltpu.SemaphoreType.DMA((3,))],
        input_output_aliases={1: 0, 2: 1},
        compiler_params=room(4),
        cost_estimate=cost(0, 2e6),
    )(mate, kv, q)
    kv_right = move(kv, "kv", -1)
    kv_left = move(kv, "kv", 1)
    q_left = move(q, "q", 1)
    q_right = move(q, "q", -1)
    kv_far = move(kv_right, "kv", -1)
    q_far = move(q_left, "q", 1)

    state = pl.pallas_call(
        state_kernel,
        name="state",
        grid=steps,
        out_shape=hbm_shape(HEADS, FROWS, 128),
        in_specs=[heads16, heads128, whole(*select.shape), whole(*vectors.shape)],
        out_specs=pl.BlockSpec((GROUP, FROWS, 128), lambda g: (g, 0, 0)),
        compiler_params=room(8),
        cost_estimate=cost(1e9, 4e6),
    )(*in_hbm(k_lin[0].T, v_lin[0], select, vectors))
    slices = lax.all_to_all(state.reshape(shards, HEADS * FROWS // shards, 128), "seq", 0, 0, tiled=True)

    num, den, phi = pl.pallas_call(
        local_kernel,
        name="local",
        grid=steps,
        out_shape=[hbm_shape(TOK, D), hbm_shape(TOK, 128, dtype=F32), hbm_shape(HEADS, FROWS, TOK)],
        in_specs=[heads16, heads16, heads128, whole(*select.shape), whole(*vectors.shape)],
        out_specs=[heads128, whole(TOK, 128), pl.BlockSpec((GROUP, FROWS, TOK), lambda g: (g, 0, 0))],
        compiler_params=room(10),
        cost_estimate=cost(4e9, 8e6),
    )(*in_hbm(q_lin[0].T, k_lin[0].T, v_lin[0], select, vectors))

    blocks = (kv, kv_right, kv_far, kv_left)
    slices, num, den, phi = lax.optimization_barrier((slices, num, den, phi))
    part = pl.BlockSpec((shards, FROWS // 2, 128), lambda g: (0, g, 0))
    prefix = pl.pallas_call(
        prefix_kernel,
        name="prefix",
        grid=(slices.shape[1] // (FROWS // 2),),
        out_shape=hbm_shape(*slices.shape),
        in_specs=[SMEM, part],
        out_specs=part,
        compiler_params=room(6),
        cost_estimate=cost(0, 2e6),
    )(place, slices)
    before = lax.all_to_all(prefix, "seq", 0, 0, tiled=True).reshape(HEADS, FROWS, 128)
    lists = pl.pallas_call(
        search_kernel,
        name="search",
        out_shape=[shape(2 * SIDE, 128, dtype=jnp.int32), shape(2 * SIDE, dtype=jnp.int32)],
        in_specs=[SMEM] + [ANY] * SIDE,
        out_specs=[SMEM] * 2,
        scratch_shapes=[
            pltpu.VMEM((2 * SIDE, 128), jnp.int32),
            pltpu.VMEM((2 * SIDE, QROWS - TOK, 128), BF),
            pltpu.SemaphoreType.DMA((SIDE + 1,)),
        ],
        compiler_params=room(2),
        cost_estimate=cost(0, 1e5),
    )(me, q_far, q_left, q_right, q)
    (to_far,) = attend("attend_far", 0, lists, (q_far,), blocks)
    to_far, q_left = lax.optimization_barrier((to_far, q_left))
    from_far = move(to_far, "q", 2)
    (to_left,) = attend("attend_left", 2, lists, (q_left,), blocks)
    to_left, q_right = lax.optimization_barrier((to_left, q_right))
    from_right = move(to_left, "q", -1)
    (to_right,) = attend("attend_right", 4, lists, (q_right,), blocks)
    to_right, q = lax.optimization_barrier((to_right, q))
    from_left = move(to_right, "q", 1)
    (here,) = attend("attend_own", 6, lists, (q,), blocks)
    kept, send = pl.pallas_call(
        join_kernel,
        name="join",
        out_shape=[shape(TOK, HALF)] * 2,
        in_specs=[VMEM] * 4,
        out_specs=[VMEM] * 2,
        scratch_shapes=[pltpu.VMEM((2, 4, TOK, 128), F32)],
        compiler_params=room(8),
        cost_estimate=cost(0, 4e6),
    )(here, from_right, from_left, from_far)
    other = swap_cores(send)
    soft_out = pl.pallas_call(
        place_kernel,
        name="place",
        out_shape=shape(TOK, SM_W),
        in_specs=[SMEM, VMEM, VMEM],
        out_specs=HBM,
        scratch_shapes=[pltpu.SemaphoreType.DMA((2,))],
        compiler_params=room(4),
        cost_estimate=cost(0, 1e6),
    )(me, kept, other)

    lin_out = pl.pallas_call(
        finish_kernel,
        name="finish",
        grid=steps,
        out_shape=shape(TOK, D),
        in_specs=[
            heads128,
            whole(TOK, 128),
            pl.BlockSpec((GROUP, FROWS, TOK), lambda g: (g, 0, 0)),
            pl.BlockSpec((GROUP, FROWS, 128), lambda g: (g, 0, 0)),
        ],
        out_specs=heads128,
        compiler_params=room(8),
        cost_estimate=cost(4e8, 8e6),
    )(*in_hbm(num, den, phi), before)
    return lin_out[None], soft_out[None]


def solution(mesh):
    wide = P("files", "seq", None)
    return jax.shard_map(
        layers,
        mesh=mesh,
        in_specs=(wide,) * 7 + (P("files", "seq"),),
        out_specs=(wide, wide),
        check_vma=False,
    )
```

```python
import functools
import math

import jax
import jax.numpy as jnp
import numpy as np
from jax import lax
from jax.experimental import pallas as pl
from jax.experimental.pallas import tpu as pltpu
from jax.sharding import PartitionSpec as P

D = 2560
HEADS = 20
FEAT = 16
FEATS = 153
FROWS = 160
FPAD = 256
SM_HD = 128
SM_W = 1280
BLK = 128
TOK = 256
LISTED = 8
GROUP = 4
HALF = 640
HALF_HEADS = 5
QROWS = 272
SIDE = 4
CORES = 2
JOIN_ROWS = 64

inv_root_two = 0.7071067811865476
TO_LOG2 = math.log2(math.e) / math.sqrt(SM_HD)
NEG = -1e30
BF = jnp.bfloat16
F32 = jnp.float32
NT = (((1,), (1,)), ((), ()))


def along(what, step):
    pairs = []
    for x in range(SIDE):
        for y in range(SIDE):
            for c in range(CORES):
                on_x = (c == 0) == (what == "kv")
                x2 = (x + step) % SIDE if on_x else x
                y2 = y if on_x else (y + step) % SIDE
                pairs.append(((x * SIDE + y) * CORES + c, (x2 * SIDE + y2) * CORES + c))
    return pairs


def move(a, what, step):
    return lax.ppermute(a, "files", along(what, step))


def swap_cores(a):
    return lax.ppermute(a, "files", [(i, i ^ 1) for i in range(SIDE * SIDE * CORES)])


def feature_tables():
    rows, cols = np.triu_indices(FEAT)
    select = np.zeros((GROUP, 2, FROWS, GROUP * FEAT), np.float32)
    for j in range(GROUP):
        for f in range(FEAT):
            select[j, 0, 1 + f, j * FEAT + f] = 0.5
        for n in range(len(rows)):
            select[j, 0, 1 + FEAT + n, j * FEAT + rows[n]] = 0.5
            select[j, 1, 1 + FEAT + n, j * FEAT + cols[n]] = 0.5
    vectors = np.zeros((3, FROWS), np.float32)
    vectors[0, 0] = 1.0
    vectors[1, : 1 + FEAT] = 1.0
    vectors[2, :FEATS] = 1.0
    vectors[2, 1 + FEAT : FEATS] = np.where(rows == cols, inv_root_two, 1.0).astype(np.float32)
    vectors = np.ascontiguousarray(np.broadcast_to(vectors[:, :, None], (3, FROWS, 128)))
    return select.reshape(GROUP, 2 * FROWS, GROUP * FEAT).astype(jnp.bfloat16), vectors


def column(j):
    return slice(j * 128, (j + 1) * 128)


def features(select, x, vectors):
    first, second, factor = (jnp.concatenate([vectors[i], vectors[i]], axis=1) for i in range(3))
    ab = jnp.dot(select, x, preferred_element_type=F32)
    return ((ab[:FROWS] + first) * (ab[FROWS:] + second) * factor).astype(BF)


def taller(phi):
    return jnp.concatenate([phi, jnp.zeros((FPAD - FROWS, phi.shape[1]), BF)], axis=0)


def with_ones(values):
    return jnp.concatenate([values, jnp.ones(values.shape, BF)], axis=1)


def state_kernel(k_ref, v_ref, select_ref, vector_ref, out_ref):
    row = lax.broadcasted_iota(jnp.int32, (16, 128), 0)
    lane = lax.broadcasted_iota(jnp.int32, (FROWS, 128), 1)
    norms = jnp.zeros((FROWS, 128), F32)
    phis = [features(select_ref[j], k_ref[...], vector_ref) for j in range(GROUP)]
    boths = [jnp.dot(phis[j], with_ones(v_ref[:, column(j)]), preferred_element_type=F32) for j in range(GROUP)]
    for j in range(GROUP):
        norms = jnp.where(lane == j, boths[j][:, 128:], norms)
        out_ref[j] = boths[j][:, :128].astype(BF)
    flat = jnp.concatenate([norms, jnp.zeros((FPAD - FROWS, 128), F32)], axis=0).T
    high = flat.astype(BF).astype(F32)
    low = flat - high
    at = row + (FROWS - 16 - FEATS)
    for j in range(GROUP):
        tail = out_ref[j, FROWS - 16 :].astype(F32)
        pieces = (high[j : j + 1, :128], high[j : j + 1, 128:], low[j : j + 1, :128], low[j : j + 1, 128:])
        for i, piece in enumerate(pieces):
            tail = jnp.where(at == i, piece, tail)
        out_ref[j, FROWS - 16 :] = tail.astype(BF)


def prefix_kernel(place_ref, in_ref, out_ref):
    rows = in_ref.shape[1]
    row = lax.broadcasted_iota(jnp.int32, (rows, 128), 0) + (place_ref[0] & 1) * (FROWS // 2)
    row = jnp.where(row >= FROWS, row - FROWS, row)
    row = jnp.where(row >= FROWS, row - FROWS, row)
    high = (row == FEATS) | (row == FEATS + 1)
    low = (row == FEATS + 2) | (row == FEATS + 3)
    total = jnp.zeros((rows, 128), F32)
    for z in range(in_ref.shape[0]):
        both = total + pltpu.roll(total, rows - 2, 0)
        top = both.astype(BF).astype(F32)
        rest = pltpu.roll(both - top, 2, 0)
        out_ref[z] = jnp.where(high, top, jnp.where(low, rest, total)).astype(BF)
        total = total + in_ref[z].astype(F32)


def local_kernel(q_ref, k_ref, v_ref, select_ref, vector_ref, num_ref, den_ref, phi_ref):
    causal = lax.broadcasted_iota(jnp.int32, (TOK, TOK), 0) >= lax.broadcasted_iota(jnp.int32, (TOK, TOK), 1)
    lane = lax.broadcasted_iota(jnp.int32, (TOK, 128), 1)
    group = pl.program_id(0)

    @pl.when(group == 0)
    def _():
        den_ref[...] = jnp.zeros((TOK, 128), F32)

    den = den_ref[...]
    phis_q = [features(select_ref[j], q_ref[...], vector_ref) for j in range(GROUP)]
    phis_k = [features(select_ref[j], k_ref[...], vector_ref) for j in range(GROUP)]
    for j in range(GROUP):
        phi_ref[j] = phis_q[j]
    turned = [taller(p).T for p in phis_q]
    weights = [jnp.dot(turned[j], taller(phis_k[j]), preferred_element_type=F32) for j in range(GROUP)]
    weights = [jnp.where(causal, w, 0.0).astype(BF) for w in weights]
    boths = [jnp.dot(weights[j], with_ones(v_ref[:, column(j)]), preferred_element_type=F32) for j in range(GROUP)]
    for j in range(GROUP):
        num_ref[:, column(j)] = boths[j][:, :128].astype(BF)
        den = jnp.where(lane == group * GROUP + j, boths[j][:, 128:], den)
    den_ref[...] = den


def finish_kernel(num_ref, den_ref, phi_ref, state_ref, out_ref):
    lane = lax.broadcasted_iota(jnp.int32, (TOK, 128), 1)
    group = pl.program_id(0)
    at = FEATS - (FROWS - 16)
    phis = [taller(phi_ref[j]).T for j in range(GROUP)]
    carried = [jnp.dot(phis[j], taller(state_ref[j]), preferred_element_type=F32) for j in range(GROUP)]
    dens = []
    for j in range(GROUP):
        tail = state_ref[j, FROWS - 16 :].astype(F32)
        n0 = tail[at : at + 1] + tail[at + 2 : at + 3]
        n1 = tail[at + 1 : at + 2] + tail[at + 3 : at + 4]
        phi32 = phis[j].astype(F32)
        den = jnp.where(lane == group * GROUP + j, den_ref[...], 0.0) + phi32[:, :128] * n0 + phi32[:, 128:] * n1
        dens.append(jnp.sum(den, axis=1, keepdims=True))
    for j in range(GROUP):
        out_ref[:, column(j)] = ((num_ref[:, column(j)].astype(F32) + carried[j]) / dens[j]).astype(BF)


def halves(core, refs):
    at = pl.ds(pl.multiple_of(core * HALF, 128), HALF)
    return [r.at[:, at] for r in refs]


def listed_rows(ids_ref, count_ref):
    lane = lax.broadcasted_iota(jnp.int32, (QROWS - TOK, HALF), 1)
    listed = jnp.full((QROWS - TOK, HALF), -1.0, F32)
    for i in range(LISTED):
        entry = jnp.where(i < count_ref[0], ids_ref[i], -1).astype(F32)
        listed = jnp.where(lane == i, entry, listed)
    return listed.astype(BF)


def pack_kernel(me_ref, ids_ref, count_ref, k_ref, v_ref, q_ref, out_ref, sems):
    copies = [
        pltpu.make_async_copy(half, out_ref.at[pl.ds(i * TOK, TOK)], sems.at[i])
        for i, half in enumerate(halves(1 - (me_ref[0] & 1), (k_ref, v_ref, q_ref)))
    ]
    for c in copies:
        c.start()
    out_ref[3 * TOK :] = listed_rows(ids_ref, count_ref)
    for c in copies:
        c.wait()


def own_kernel(me_ref, ids_ref, count_ref, k_ref, v_ref, q_ref, kv_ref, both_ref, sems):
    targets = (kv_ref.at[0, 0], kv_ref.at[0, 1], both_ref.at[0, pl.ds(0, TOK)])
    copies = [
        pltpu.make_async_copy(half, to, sems.at[i])
        for i, (half, to) in enumerate(zip(halves(me_ref[0] & 1, (k_ref, v_ref, q_ref)), targets, strict=True))
    ]
    for c in copies:
        c.start()
    both_ref[0, TOK:QROWS] = listed_rows(ids_ref, count_ref)
    for c in copies:
        c.wait()


def merge_kernel(mate_ref, kv_in, both_in, kv_ref, both_ref, sems):
    del kv_in, both_in
    pieces = ((pl.ds(0, TOK), kv_ref.at[1, 0]), (pl.ds(TOK, TOK), kv_ref.at[1, 1]), (pl.ds(2 * TOK, QROWS), both_ref.at[1]))
    copies = [pltpu.make_async_copy(mate_ref.at[at], to, sems.at[i]) for i, (at, to) in enumerate(pieces)]
    for c in copies:
        c.start()
    for c in copies:
        c.wait()


def search_kernel(me_ref, *refs):
    q_in, (found_ref, count_ref, wanted, ids, sems) = refs[:SIDE], refs[SIDE:]
    me = me_ref[0]
    core, y, x = me & 1, (me >> 1) & (SIDE - 1), me >> 3
    rows = pl.ds(TOK, QROWS - TOK)
    copies = [
        pltpu.make_async_copy(q_in[i].at[:, rows, pl.ds(0, 128)], ids.at[pl.ds(2 * i, 2)], sems.at[i]) for i in range(SIDE)
    ]
    for c in copies:
        c.start()
    for c in copies:
        c.wait()
    entry = jnp.concatenate([ids[r].astype(F32)[0:1] for r in range(2 * SIDE)], axis=0).astype(jnp.int32)
    xo, yo, co = entry >> 4, (entry >> 2) & (SIDE - 1), (entry >> 1) & 1
    on_x = core == 0
    line = jnp.where(on_x, yo, xo) == jnp.where(on_x, y, x)
    away = jnp.where(on_x, xo - x, yo - y) & (SIDE - 1)
    code = (away * 2 + (co ^ core)) * 2 + (entry & 1)
    wanted[...] = jnp.where((entry >= 0) & line, code, -1)
    pltpu.async_copy(wanted, found_ref, sems.at[SIDE]).wait()

    def search(r, carry):
        count = jnp.int32(0)
        for i in range(LISTED):
            entry = found_ref[r, i]
            found_ref[r, count] = entry
            count = count + (entry >= 0).astype(jnp.int32)
        count_ref[r] = count
        return carry

    lax.fori_loop(0, 2 * SIDE, search, 0)


def attend_kernel(own, base, readers, found, counts, *refs):
    groups = readers // 2
    q_in, kv_in, outs = refs[:groups], refs[groups : groups + SIDE], refs[groups + SIDE : readers + SIDE]
    q_buf, g_buf, s_buf, m_buf, a_buf, q_sems, g_sems = refs[readers + SIDE :]
    copies = [pltpu.make_async_copy(q_in[r // 2].at[r % 2], q_buf.at[r], q_sems.at[r]) for r in range(readers)]
    lane = lax.broadcasted_iota(jnp.int32, (TOK, 128), 1)
    heads = [(h, slice(h * 128, (h + 1) * 128)) for h in range(HALF_HEADS)]

    def fetch(r, slot):
        def one(i, carry):
            code = found[base + r, i]
            rows = pl.ds(pl.multiple_of((code & 1) * BLK, BLK), BLK)
            for away in range(SIDE):

                @pl.when((code >> 2) == away)
                def _():
                    for kind in range(2):
                        source = kv_in[away].at[(code >> 1) & 1, kind, rows, :]
                        pltpu.make_async_copy(source, g_buf.at[slot, i, kind], g_sems.at[slot, i, kind]).start()

            return carry

        lax.fori_loop(0, counts[base + r], one, 0)

    def arrived(r, slot, kind):
        def one(i, carry):
            source = kv_in[0].at[0, kind, pl.ds(0, BLK), :]
            pltpu.make_async_copy(source, g_buf.at[slot, i, kind], g_sems.at[slot, i, kind]).wait()
            return carry

        lax.fori_loop(0, counts[base + r], one, 0)

    def blank(slot, i):
        g_buf[slot, i, 1] = jnp.zeros((BLK, HALF), BF)

    def reader(r, slot, out_ref):
        count = counts[base + r]
        pairs = (count + 1) >> 1

        @pl.when((count & 1) == 1)
        def _():
            blank(slot, count)

        if not own:

            @pl.when(count == 0)
            def _():
                blank(slot, 0)
                blank(slot, 1)

        def blocks(j, kind, at):
            return jnp.concatenate([g_buf[slot, 2 * j, kind, :, at], g_buf[slot, 2 * j + 1, kind, :, at]], axis=0)

        def score(j, fresh):
            for h, at in heads:
                s = lax.dot_general(q_buf[r, 0:TOK, at], blocks(j, 0, at), NT, preferred_element_type=F32)
                s0, s1 = s[:, :128], jnp.where(2 * j + 1 < count, s[:, 128:], NEG)
                if fresh:
                    s0 = jnp.where(count > 0, s0, NEG)
                s_buf[j, h, :, 0:128] = s0
                s_buf[j, h, :, 128:256] = s1
                m = jnp.maximum(s0, s1)
                m_buf[h] = m if fresh else jnp.maximum(m_buf[h], m)

        def weigh(j, fresh):
            for h, at in heads:
                m = m_buf[h]
                p = jnp.exp2(s_buf[j, h] * TO_LOG2 - jnp.concatenate([m, m], axis=1)).astype(BF)
                a = jnp.dot(p, with_ones(blocks(j, 1, at)), preferred_element_type=F32)
                a_buf[h] = a if fresh else a_buf[h] + a

        if own:
            for h, at in heads:
                parts = []
                for b in range(2):
                    rows = slice(b * BLK, (b + 1) * BLK)
                    k = own_kv[r, 0, rows, at]
                    parts.append(lax.dot_general(q_buf[r, rows, at], k, NT, preferred_element_type=F32))
                s = jnp.concatenate(parts, axis=0)
                s_buf[LISTED // 2, h, :, 0:128] = s
                m_buf[h] = s
            arrived(r, slot, 0)
        else:
            arrived(r, slot, 0)
            score(0, True)
        start = 0 if own else 1

        def more_scores(j, carry):
            score(j, False)
            return carry

        lax.fori_loop(start, pairs, more_scores, 0)
        tops = jnp.zeros((TOK, 128), F32)
        for h, at in heads:
            m = jnp.broadcast_to(jnp.max(m_buf[h], axis=1, keepdims=True) * TO_LOG2, (TOK, 128))
            m_buf[h] = m
            tops = jnp.where(lane == h, m, tops)
        if own:
            for h, at in heads:
                p = jnp.exp2(s_buf[LISTED // 2, h, :, 0:128] * TO_LOG2 - m_buf[h]).astype(BF)
                parts = []
                for b in range(2):
                    rows = slice(b * BLK, (b + 1) * BLK)
                    v = with_ones(own_kv[r, 1, rows, at])
                    parts.append(jnp.dot(p[rows], v, preferred_element_type=F32))
                a_buf[h] = jnp.concatenate(parts, axis=0)
            arrived(r, slot, 1)
        else:
            arrived(r, slot, 1)
            weigh(0, True)

        def more_weights(j, carry):
            weigh(j, False)
            return carry

        lax.fori_loop(start, pairs, more_weights, 0)
        totals = jnp.ones((TOK, 128), F32)
        for h, at in heads:
            total = a_buf[h, :, 128:]
            out_ref[slot, 0:TOK, at] = (a_buf[h, :, :128] / total).astype(BF)
            totals = jnp.where(lane == h, total, totals)
        sizes = tops + jnp.log2(totals)
        if not own:
            sizes = jnp.where(jnp.logical_and(count == 0, lane < HALF_HEADS), NEG, sizes)
        high = sizes.astype(BF).astype(F32)
        middle = (sizes - high).astype(BF).astype(F32)
        low = sizes - high - middle
        packed = high + pltpu.roll(middle, HALF_HEADS, 1) + pltpu.roll(low, 2 * HALF_HEADS, 1)
        out_ref[slot, TOK:QROWS, :] = jnp.zeros((QROWS - TOK, HALF), BF)
        out_ref[slot, TOK:QROWS, 0:TOK] = packed.T[0 : QROWS - TOK].astype(BF)

    own_kv = kv_in[0]
    copies[0].start()
    fetch(0, 0)
    for c in copies[1:]:
        c.start()
    for g, out_ref in enumerate(outs):

        def one(i, carry, g=g, out_ref=out_ref):
            r = 2 * g + i

            @pl.when(r + 1 < readers)
            def _():
                fetch(r + 1, 1 - i)

            pltpu.make_async_copy(q_in[0].at[0], q_buf.at[r], q_sems.at[r]).wait()
            reader(r, i, out_ref)
            return carry

        lax.fori_loop(0, 2, one, 0)


def join_kernel(*refs):
    parts, outs, size_ref = refs[:4], refs[4:6], refs[6]
    for r in range(2):
        for i, p in enumerate(parts):
            packed = p[r, TOK:QROWS, 0:TOK].astype(F32)
            packed = jnp.concatenate([packed, jnp.zeros((128 - (QROWS - TOK), TOK), F32)], axis=0).T
            size_ref[r, i] = packed + pltpu.roll(packed, 128 - HALF_HEADS, 1) + pltpu.roll(packed, 128 - 2 * HALF_HEADS, 1)
    for r in range(2):
        for t in range(TOK // JOIN_ROWS):
            rows = slice(t * JOIN_ROWS, (t + 1) * JOIN_ROWS)
            sizes = [size_ref[r, i, rows] for i in range(4)]
            top = functools.reduce(jnp.maximum, sizes)
            shares = [jnp.exp2(s - top) for s in sizes]
            total = functools.reduce(jnp.add, shares)
            shares = [s / total for s in shares]
            for h in range(HALF_HEADS):
                at = slice(h * 128, (h + 1) * 128)
                o = sum(s[:, h : h + 1] * p[r, rows, at].astype(F32) for s, p in zip(shares, parts, strict=True))
                outs[r][rows, at] = o.astype(BF)


def place_kernel(me_ref, kept_ref, other_ref, out_ref, sems):
    core = me_ref[0] & 1
    copies = [
        pltpu.make_async_copy(half, to, sems.at[i])
        for i, (half, to) in enumerate(zip((kept_ref, other_ref), halves(core, (out_ref,)) + halves(1 - core, (out_ref,)), strict=True))
    ]
    for c in copies:
        c.start()
    for c in copies:
        c.wait()


def shape(*dims, dtype=BF):
    return jax.ShapeDtypeStruct(dims, dtype)


SMEM = pl.BlockSpec(memory_space=pltpu.SMEM)
VMEM = pl.BlockSpec(memory_space=pltpu.VMEM)
ANY = pl.BlockSpec(memory_space=pl.ANY)
HBM = pl.BlockSpec(memory_space=pltpu.HBM)


def room(mib):
    return pltpu.CompilerParams(vmem_limit_bytes=mib * 1024 * 1024)


def cost(flops, moved):
    return pl.CostEstimate(flops=int(flops), bytes_accessed=int(moved), transcendentals=0)


def in_hbm(*arrays):
    return tuple(pltpu.with_memory_space_constraint(a, pltpu.HBM) for a in arrays)


def hbm_shape(*dims, dtype=BF):
    return pltpu.HBM(dims, dtype)


def whole(*dims):
    return pl.BlockSpec(dims, lambda g: (0,) * len(dims))


def attend(name, base, lists, queries, blocks):
    own = name == "attend_own"
    groups = len(queries)
    readers = 2 * groups
    first = VMEM if own else ANY
    return pl.pallas_call(
        functools.partial(attend_kernel, own, base, readers),
        out_shape=[shape(2, QROWS, HALF)] * groups,
        in_specs=[SMEM, SMEM] + [ANY] * groups + [first] + [ANY] * (SIDE - 1),
        out_specs=[VMEM] * groups,
        scratch_shapes=[
            pltpu.VMEM((readers, QROWS, HALF), BF),
            pltpu.VMEM((2, LISTED, 2, BLK, HALF), BF),
            pltpu.VMEM((LISTED // 2 + 1, HALF_HEADS, TOK, 256), F32),
            pltpu.VMEM((HALF_HEADS, TOK, 128), F32),
            pltpu.VMEM((HALF_HEADS, TOK, 256), F32),
            pltpu.SemaphoreType.DMA((readers,)),
            pltpu.SemaphoreType.DMA((2, LISTED, 2)),
        ],
        compiler_params=room(18),
        cost_estimate=cost(readers * 4e8, 8e6),
    )(*lists, *queries, *blocks)


def layers(q_lin, k_lin, v_lin, q_soft, k_soft, v_soft, import_ids, import_counts):
    select, vectors = (jnp.asarray(t) for t in feature_tables())
    me = lax.axis_index("files").astype(jnp.int32).reshape(1)
    place = lax.axis_index("seq").astype(jnp.int32).reshape(1)
    shards = lax.axis_size("seq")
    steps = (HEADS // GROUP,)
    heads16 = pl.BlockSpec((GROUP * FEAT, TOK), lambda g: (g, 0))
    heads128 = pl.BlockSpec((TOK, GROUP * 128), lambda g: (0, g))
    mine = (me, import_ids[0, 0], import_counts[0]) + in_hbm(k_soft[0], v_soft[0], q_soft[0])

    sent = pl.pallas_call(
        pack_kernel,
        name="pack",
        out_shape=shape(2 * TOK + QROWS, HALF),
        in_specs=[SMEM] * 3 + [HBM] * 3,
        out_specs=VMEM,
        scratch_shapes=[pltpu.SemaphoreType.DMA((3,))],
        compiler_params=room(4),
        cost_estimate=cost(0, 2e6),
    )(*mine)
    mate = swap_cores(sent)
    pair = [shape(2, 2, TOK, HALF), shape(2, QROWS, HALF)]
    kv, q = pl.pallas_call(
        own_kernel,
        name="own",
        out_shape=pair,
        in_specs=[SMEM] * 3 + [HBM] * 3,
        out_specs=[VMEM] * 2,
        scratch_shapes=[pltpu.SemaphoreType.DMA((3,))],
        compiler_params=room(6),
        cost_estimate=cost(0, 2e6),
    )(*mine)

    kv, q = pl.pallas_call(
        merge_kernel,
        name="merge",
        out_shape=pair,
        in_specs=[VMEM, ANY, ANY],
        out_specs=[ANY] * 2,
        scratch_shapes=[pltpu.SemaphoreType.DMA((3,))],
        input_output_aliases={1: 0, 2: 1},
        compiler_params=room(4),
        cost_estimate=cost(0, 2e6),
    )(mate, kv, q)
    kv_right = move(kv, "kv", -1)
    kv_left = move(kv, "kv", 1)
    q_left = move(q, "q", 1)
    q_right = move(q, "q", -1)
    kv_far = move(kv_right, "kv", -1)
    q_far = move(q_left, "q", 1)

    state = pl.pallas_call(
        state_kernel,
        name="state",
        grid=steps,
        out_shape=hbm_shape(HEADS, FROWS, 128),
        in_specs=[heads16, heads128, whole(*select.shape), whole(*vectors.shape)],
        out_specs=pl.BlockSpec((GROUP, FROWS, 128), lambda g: (g, 0, 0)),
        compiler_params=room(8),
        cost_estimate=cost(1e9, 4e6),
    )(*in_hbm(k_lin[0].T, v_lin[0], select, vectors))
    slices = lax.all_to_all(state.reshape(shards, HEADS * FROWS // shards, 128), "seq", 0, 0, tiled=True)

    num, den, phi = pl.pallas_call(
        local_kernel,
        name="local",
        grid=steps,
        out_shape=[hbm_shape(TOK, D), hbm_shape(TOK, 128, dtype=F32), hbm_shape(HEADS, FROWS, TOK)],
        in_specs=[heads16, heads16, heads128, whole(*select.shape), whole(*vectors.shape)],
        out_specs=[heads128, whole(TOK, 128), pl.BlockSpec((GROUP, FROWS, TOK), lambda g: (g, 0, 0))],
        compiler_params=room(10),
        cost_estimate=cost(4e9, 8e6),
    )(*in_hbm(q_lin[0].T, k_lin[0].T, v_lin[0], select, vectors))

    blocks = (kv, kv_right, kv_far, kv_left)
    slices, num, den, phi = lax.optimization_barrier((slices, num, den, phi))
    prefix = pl.pallas_call(
        prefix_kernel,
        name="prefix",
        out_shape=hbm_shape(*slices.shape),
        in_specs=[SMEM, VMEM],
        out_specs=VMEM,
        compiler_params=room(6),
        cost_estimate=cost(0, 2e6),
    )(place, slices)
    before = lax.all_to_all(prefix, "seq", 0, 0, tiled=True).reshape(HEADS, FROWS, 128)
    lists = pl.pallas_call(
        search_kernel,
        name="search",
        out_shape=[shape(2 * SIDE, 128, dtype=jnp.int32), shape(2 * SIDE, dtype=jnp.int32)],
        in_specs=[SMEM] + [ANY] * SIDE,
        out_specs=[SMEM] * 2,
        scratch_shapes=[
            pltpu.VMEM((2 * SIDE, 128), jnp.int32),
            pltpu.VMEM((2 * SIDE, QROWS - TOK, 128), BF),
            pltpu.SemaphoreType.DMA((SIDE + 1,)),
        ],
        compiler_params=room(2),
        cost_estimate=cost(0, 1e5),
    )(me, q_far, q_left, q_right, q)
    (to_far,) = attend("attend_far", 0, lists, (q_far,), blocks)
    to_far, q_left = lax.optimization_barrier((to_far, q_left))
    from_far = move(to_far, "q", 2)
    (to_left,) = attend("attend_left", 2, lists, (q_left,), blocks)
    to_left, q_right = lax.optimization_barrier((to_left, q_right))
    from_right = move(to_left, "q", -1)
    (to_right,) = attend("attend_right", 4, lists, (q_right,), blocks)
    to_right, q = lax.optimization_barrier((to_right, q))
    from_left = move(to_right, "q", 1)
    (here,) = attend("attend_own", 6, lists, (q,), blocks)
    kept, send = pl.pallas_call(
        join_kernel,
        name="join",
        out_shape=[shape(TOK, HALF)] * 2,
        in_specs=[VMEM] * 4,
        out_specs=[VMEM] * 2,
        scratch_shapes=[pltpu.VMEM((2, 4, TOK, 128), F32)],
        compiler_params=room(8),
        cost_estimate=cost(0, 4e6),
    )(here, from_right, from_left, from_far)
    other = swap_cores(send)
    soft_out = pl.pallas_call(
        place_kernel,
        name="place",
        out_shape=shape(TOK, SM_W),
        in_specs=[SMEM, VMEM, VMEM],
        out_specs=HBM,
        scratch_shapes=[pltpu.SemaphoreType.DMA((2,))],
        compiler_params=room(4),
        cost_estimate=cost(0, 1e6),
    )(me, kept, other)

    lin_out = pl.pallas_call(
        finish_kernel,
        name="finish",
        grid=steps,
        out_shape=shape(TOK, D),
        in_specs=[
            heads128,
            whole(TOK, 128),
            pl.BlockSpec((GROUP, FROWS, TOK), lambda g: (g, 0, 0)),
            pl.BlockSpec((GROUP, FROWS, 128), lambda g: (g, 0, 0)),
        ],
        out_specs=heads128,
        compiler_params=room(8),
        cost_estimate=cost(4e8, 8e6),
    )(*in_hbm(num, den, phi), before)
    return lin_out[None], soft_out[None]


def solution(mesh):
    wide = P("files", "seq", None)
    return jax.shard_map(
        layers,
        mesh=mesh,
        in_specs=(wide,) * 7 + (P("files", "seq"),),
        out_specs=(wide, wide),
        check_vma=False,
    )
```

```python
import functools
import math

import jax
import jax.numpy as jnp
import numpy as np
from jax import lax
from jax.experimental import pallas as pl
from jax.experimental.pallas import tpu as pltpu
from jax.sharding import PartitionSpec as P

D = 2560
HEADS = 20
FEAT = 16
FEATS = 153
FROWS = 160
FPAD = 256
SM_HD = 128
SM_W = 1280
BLK = 128
TOK = 256
LISTED = 8
GROUP = 4
HALF = 640
HALF_HEADS = 5
QROWS = 272
SIDE = 4
CORES = 2
JOIN_ROWS = 64

inv_root_two = 0.7071067811865476
TO_LOG2 = math.log2(math.e) / math.sqrt(SM_HD)
NEG = -1e30
BF = jnp.bfloat16
F32 = jnp.float32
NT = (((1,), (1,)), ((), ()))


def along(what, step):
    pairs = []
    for x in range(SIDE):
        for y in range(SIDE):
            for c in range(CORES):
                on_x = (c == 0) == (what == "kv")
                x2 = (x + step) % SIDE if on_x else x
                y2 = y if on_x else (y + step) % SIDE
                pairs.append(((x * SIDE + y) * CORES + c, (x2 * SIDE + y2) * CORES + c))
    return pairs


def move(a, what, step):
    return lax.ppermute(a, "files", along(what, step))


def swap_cores(a):
    return lax.ppermute(a, "files", [(i, i ^ 1) for i in range(SIDE * SIDE * CORES)])


def feature_tables():
    rows, cols = np.triu_indices(FEAT)
    select = np.zeros((GROUP, 2, FROWS, GROUP * FEAT), np.float32)
    for j in range(GROUP):
        for f in range(FEAT):
            select[j, 0, 1 + f, j * FEAT + f] = 0.5
        for n in range(len(rows)):
            select[j, 0, 1 + FEAT + n, j * FEAT + rows[n]] = 0.5
            select[j, 1, 1 + FEAT + n, j * FEAT + cols[n]] = 0.5
    vectors = np.zeros((3, FROWS), np.float32)
    vectors[0, 0] = 1.0
    vectors[1, : 1 + FEAT] = 1.0
    vectors[2, :FEATS] = 1.0
    vectors[2, 1 + FEAT : FEATS] = np.where(rows == cols, inv_root_two, 1.0).astype(np.float32)
    vectors = np.ascontiguousarray(np.broadcast_to(vectors[:, :, None], (3, FROWS, 128)))
    return select.reshape(GROUP, 2 * FROWS, GROUP * FEAT).astype(jnp.bfloat16), vectors


def column(j):
    return slice(j * 128, (j + 1) * 128)


def features(select, x, vectors):
    first, second, factor = (jnp.concatenate([vectors[i], vectors[i]], axis=1) for i in range(3))
    ab = jnp.dot(select, x, preferred_element_type=F32)
    return ((ab[:FROWS] + first) * (ab[FROWS:] + second) * factor).astype(BF)


def taller(phi):
    return jnp.concatenate([phi, jnp.zeros((FPAD - FROWS, phi.shape[1]), BF)], axis=0)


def with_ones(values):
    return jnp.concatenate([values, jnp.ones(values.shape, BF)], axis=1)


def state_kernel(k_ref, v_ref, select_ref, vector_ref, out_ref):
    row = lax.broadcasted_iota(jnp.int32, (16, 128), 0)
    lane = lax.broadcasted_iota(jnp.int32, (FROWS, 128), 1)
    norms = jnp.zeros((FROWS, 128), F32)
    phis = [features(select_ref[j], k_ref[...], vector_ref) for j in range(GROUP)]
    boths = [jnp.dot(phis[j], with_ones(v_ref[:, column(j)]), preferred_element_type=F32) for j in range(GROUP)]
    for j in range(GROUP):
        norms = jnp.where(lane == j, boths[j][:, 128:], norms)
        out_ref[j] = boths[j][:, :128].astype(BF)
    flat = jnp.concatenate([norms, jnp.zeros((FPAD - FROWS, 128), F32)], axis=0).T
    high = flat.astype(BF).astype(F32)
    low = flat - high
    at = row + (FROWS - 16 - FEATS)
    for j in range(GROUP):
        tail = out_ref[j, FROWS - 16 :].astype(F32)
        pieces = (high[j : j + 1, :128], high[j : j + 1, 128:], low[j : j + 1, :128], low[j : j + 1, 128:])
        for i, piece in enumerate(pieces):
            tail = jnp.where(at == i, piece, tail)
        out_ref[j, FROWS - 16 :] = tail.astype(BF)


def prefix_kernel(place_ref, in_ref, out_ref):
    rows = in_ref.shape[1]
    row = lax.broadcasted_iota(jnp.int32, (rows, 128), 0) + (place_ref[0] & 1) * (FROWS // 2)
    row = jnp.where(row >= FROWS, row - FROWS, row)
    row = jnp.where(row >= FROWS, row - FROWS, row)
    high = (row == FEATS) | (row == FEATS + 1)
    low = (row == FEATS + 2) | (row == FEATS + 3)
    total = jnp.zeros((rows, 128), F32)
    for z in range(in_ref.shape[0]):
        both = total + pltpu.roll(total, rows - 2, 0)
        top = both.astype(BF).astype(F32)
        rest = pltpu.roll(both - top, 2, 0)
        out_ref[z] = jnp.where(high, top, jnp.where(low, rest, total)).astype(BF)
        total = total + in_ref[z].astype(F32)


def local_kernel(q_ref, k_ref, v_ref, select_ref, vector_ref, num_ref, den_ref, phi_ref):
    causal = lax.broadcasted_iota(jnp.int32, (TOK, TOK), 0) >= lax.broadcasted_iota(jnp.int32, (TOK, TOK), 1)
    lane = lax.broadcasted_iota(jnp.int32, (TOK, 128), 1)
    group = pl.program_id(0)

    @pl.when(group == 0)
    def _():
        den_ref[...] = jnp.zeros((TOK, 128), F32)

    den = den_ref[...]
    phis_q = [features(select_ref[j], q_ref[...], vector_ref) for j in range(GROUP)]
    phis_k = [features(select_ref[j], k_ref[...], vector_ref) for j in range(GROUP)]
    for j in range(GROUP):
        phi_ref[j] = phis_q[j]
    turned = [taller(p).T for p in phis_q]
    weights = [jnp.dot(turned[j], taller(phis_k[j]), preferred_element_type=F32) for j in range(GROUP)]
    weights = [jnp.where(causal, w, 0.0).astype(BF) for w in weights]
    boths = [jnp.dot(weights[j], with_ones(v_ref[:, column(j)]), preferred_element_type=F32) for j in range(GROUP)]
    for j in range(GROUP):
        num_ref[:, column(j)] = boths[j][:, :128].astype(BF)
        den = jnp.where(lane == group * GROUP + j, boths[j][:, 128:], den)
    den_ref[...] = den


def finish_kernel(num_ref, den_ref, phi_ref, state_ref, out_ref):
    lane = lax.broadcasted_iota(jnp.int32, (TOK, 128), 1)
    group = pl.program_id(0)
    at = FEATS - (FROWS - 16)
    phis = [taller(phi_ref[j]).T for j in range(GROUP)]
    carried = [jnp.dot(phis[j], taller(state_ref[j]), preferred_element_type=F32) for j in range(GROUP)]
    dens = []
    for j in range(GROUP):
        tail = state_ref[j, FROWS - 16 :].astype(F32)
        n0 = tail[at : at + 1] + tail[at + 2 : at + 3]
        n1 = tail[at + 1 : at + 2] + tail[at + 3 : at + 4]
        phi32 = phis[j].astype(F32)
        den = jnp.where(lane == group * GROUP + j, den_ref[...], 0.0) + phi32[:, :128] * n0 + phi32[:, 128:] * n1
        dens.append(jnp.sum(den, axis=1, keepdims=True))
    for j in range(GROUP):
        out_ref[:, column(j)] = ((num_ref[:, column(j)].astype(F32) + carried[j]) / dens[j]).astype(BF)


def halves(core, refs):
    at = pl.ds(pl.multiple_of(core * HALF, 128), HALF)
    return [r.at[:, at] for r in refs]


def listed_rows(ids_ref, count_ref):
    lane = lax.broadcasted_iota(jnp.int32, (QROWS - TOK, HALF), 1)
    listed = jnp.full((QROWS - TOK, HALF), -1.0, F32)
    for i in range(LISTED):
        entry = jnp.where(i < count_ref[0], ids_ref[i], -1).astype(F32)
        listed = jnp.where(lane == i, entry, listed)
    return listed.astype(BF)


def pack_kernel(me_ref, ids_ref, count_ref, k_ref, v_ref, q_ref, out_ref, sems):
    copies = [
        pltpu.make_async_copy(half, out_ref.at[pl.ds(i * TOK, TOK)], sems.at[i])
        for i, half in enumerate(halves(1 - (me_ref[0] & 1), (k_ref, v_ref, q_ref)))
    ]
    for c in copies:
        c.start()
    out_ref[3 * TOK :] = listed_rows(ids_ref, count_ref)
    for c in copies:
        c.wait()


def own_kernel(me_ref, ids_ref, count_ref, k_ref, v_ref, q_ref, kv_ref, both_ref, sems):
    targets = (kv_ref.at[0, 0], kv_ref.at[0, 1], both_ref.at[0, pl.ds(0, TOK)])
    copies = [
        pltpu.make_async_copy(half, to, sems.at[i])
        for i, (half, to) in enumerate(zip(halves(me_ref[0] & 1, (k_ref, v_ref, q_ref)), targets, strict=True))
    ]
    for c in copies:
        c.start()
    both_ref[0, TOK:QROWS] = listed_rows(ids_ref, count_ref)
    for c in copies:
        c.wait()


def merge_kernel(mate_ref, kv_in, both_in, kv_ref, both_ref, sems):
    del kv_in, both_in
    pieces = ((pl.ds(0, TOK), kv_ref.at[1, 0]), (pl.ds(TOK, TOK), kv_ref.at[1, 1]), (pl.ds(2 * TOK, QROWS), both_ref.at[1]))
    copies = [pltpu.make_async_copy(mate_ref.at[at], to, sems.at[i]) for i, (at, to) in enumerate(pieces)]
    for c in copies:
        c.start()
    for c in copies:
        c.wait()


def search_kernel(me_ref, *refs):
    q_in, (found_ref, count_ref, wanted, ids, sems) = refs[:SIDE], refs[SIDE:]
    me = me_ref[0]
    core, y, x = me & 1, (me >> 1) & (SIDE - 1), me >> 3
    rows = pl.ds(TOK, QROWS - TOK)
    copies = [
        pltpu.make_async_copy(q_in[i].at[:, rows, pl.ds(0, 128)], ids.at[pl.ds(2 * i, 2)], sems.at[i]) for i in range(SIDE)
    ]
    for c in copies:
        c.start()
    for c in copies:
        c.wait()
    entry = jnp.concatenate([ids[r].astype(F32)[0:1] for r in range(2 * SIDE)], axis=0).astype(jnp.int32)
    xo, yo, co = entry >> 4, (entry >> 2) & (SIDE - 1), (entry >> 1) & 1
    on_x = core == 0
    line = jnp.where(on_x, yo, xo) == jnp.where(on_x, y, x)
    away = jnp.where(on_x, xo - x, yo - y) & (SIDE - 1)
    code = (away * 2 + (co ^ core)) * 2 + (entry & 1)
    wanted[...] = jnp.where((entry >= 0) & line, code, -1)
    pltpu.async_copy(wanted, found_ref, sems.at[SIDE]).wait()

    def search(r, carry):
        count = jnp.int32(0)
        for i in range(LISTED):
            entry = found_ref[r, i]
            found_ref[r, count] = entry
            count = count + (entry >= 0).astype(jnp.int32)
        count_ref[r] = count
        return carry

    lax.fori_loop(0, 2 * SIDE, search, 0)


def attend_kernel(own, base, readers, found, counts, *refs):
    groups = readers // 2
    q_in, kv_in, outs = refs[:groups], refs[groups : groups + SIDE], refs[groups + SIDE : readers + SIDE]
    q_buf, g_buf, s_buf, m_buf, a_buf, q_sems, g_sems = refs[readers + SIDE :]
    copies = [pltpu.make_async_copy(q_in[i], q_buf.at[pl.ds(2 * i, 2)], q_sems.at[i]) for i in range(groups)]
    for c in copies:
        c.start()
    lane = lax.broadcasted_iota(jnp.int32, (TOK, 128), 1)
    heads = [(h, slice(h * 128, (h + 1) * 128)) for h in range(HALF_HEADS)]

    def fetch(r, slot):
        def one(i, carry):
            code = found[base + r, i]
            rows = pl.ds(pl.multiple_of((code & 1) * BLK, BLK), BLK)
            for away in range(SIDE):

                @pl.when((code >> 2) == away)
                def _():
                    source = kv_in[away].at[(code >> 1) & 1, :, rows, :]
                    pltpu.make_async_copy(source, g_buf.at[slot, i], g_sems.at[slot, i]).start()

            return carry

        lax.fori_loop(0, counts[base + r], one, 0)

    def arrived(r, slot):
        def one(i, carry):
            source = kv_in[0].at[0, :, pl.ds(0, BLK), :]
            pltpu.make_async_copy(source, g_buf.at[slot, i], g_sems.at[slot, i]).wait()
            return carry

        lax.fori_loop(0, counts[base + r], one, 0)

    def blank(slot, i):
        g_buf[slot, i, 1] = jnp.zeros((BLK, HALF), BF)

    def reader(r, slot, out_ref):
        count = counts[base + r]
        pairs = (count + 1) >> 1

        @pl.when((count & 1) == 1)
        def _():
            blank(slot, count)

        if not own:

            @pl.when(count == 0)
            def _():
                blank(slot, 0)
                blank(slot, 1)

        def blocks(j, kind, at):
            return jnp.concatenate([g_buf[slot, 2 * j, kind, :, at], g_buf[slot, 2 * j + 1, kind, :, at]], axis=0)

        def score(j, fresh):
            for h, at in heads:
                s = lax.dot_general(q_buf[r, 0:TOK, at], blocks(j, 0, at), NT, preferred_element_type=F32)
                s0, s1 = s[:, :128], jnp.where(2 * j + 1 < count, s[:, 128:], NEG)
                if fresh:
                    s0 = jnp.where(count > 0, s0, NEG)
                s_buf[j, h, :, 0:128] = s0
                s_buf[j, h, :, 128:256] = s1
                m = jnp.maximum(s0, s1)
                m_buf[h] = m if fresh else jnp.maximum(m_buf[h], m)

        def weigh(j, fresh):
            for h, at in heads:
                m = m_buf[h]
                p = jnp.exp2(s_buf[j, h] * TO_LOG2 - jnp.concatenate([m, m], axis=1)).astype(BF)
                a = jnp.dot(p, with_ones(blocks(j, 1, at)), preferred_element_type=F32)
                a_buf[h] = a if fresh else a_buf[h] + a

        if own:
            for h, at in heads:
                parts = []
                for b in range(2):
                    rows = slice(b * BLK, (b + 1) * BLK)
                    k = own_kv[r, 0, rows, at]
                    parts.append(lax.dot_general(q_buf[r, rows, at], k, NT, preferred_element_type=F32))
                s = jnp.concatenate(parts, axis=0)
                s_buf[LISTED // 2, h, :, 0:128] = s
                m_buf[h] = s
        else:
            score(0, True)
        start = 0 if own else 1

        def more_scores(j, carry):
            score(j, False)
            return carry

        lax.fori_loop(start, pairs, more_scores, 0)
        tops = jnp.zeros((TOK, 128), F32)
        for h, at in heads:
            m = jnp.broadcast_to(jnp.max(m_buf[h], axis=1, keepdims=True) * TO_LOG2, (TOK, 128))
            m_buf[h] = m
            tops = jnp.where(lane == h, m, tops)
        if own:
            for h, at in heads:
                p = jnp.exp2(s_buf[LISTED // 2, h, :, 0:128] * TO_LOG2 - m_buf[h]).astype(BF)
                parts = []
                for b in range(2):
                    rows = slice(b * BLK, (b + 1) * BLK)
                    v = with_ones(own_kv[r, 1, rows, at])
                    parts.append(jnp.dot(p[rows], v, preferred_element_type=F32))
                a_buf[h] = jnp.concatenate(parts, axis=0)
        else:
            weigh(0, True)

        def more_weights(j, carry):
            weigh(j, False)
            return carry

        lax.fori_loop(start, pairs, more_weights, 0)
        totals = jnp.ones((TOK, 128), F32)
        for h, at in heads:
            total = a_buf[h, :, 128:]
            out_ref[slot, 0:TOK, at] = (a_buf[h, :, :128] / total).astype(BF)
            totals = jnp.where(lane == h, total, totals)
        sizes = tops + jnp.log2(totals)
        if not own:
            sizes = jnp.where(jnp.logical_and(count == 0, lane < HALF_HEADS), NEG, sizes)
        high = sizes.astype(BF).astype(F32)
        middle = (sizes - high).astype(BF).astype(F32)
        low = sizes - high - middle
        packed = high + pltpu.roll(middle, HALF_HEADS, 1) + pltpu.roll(low, 2 * HALF_HEADS, 1)
        out_ref[slot, TOK:QROWS, :] = jnp.zeros((QROWS - TOK, HALF), BF)
        out_ref[slot, TOK:QROWS, 0:TOK] = packed.T[0 : QROWS - TOK].astype(BF)

    own_kv = kv_in[0]
    fetch(0, 0)
    for c in copies:
        c.wait()
    for g, out_ref in enumerate(outs):

        def one(i, carry, g=g, out_ref=out_ref):
            r = 2 * g + i

            @pl.when(r + 1 < readers)
            def _():
                fetch(r + 1, 1 - i)

            arrived(r, i)
            reader(r, i, out_ref)
            return carry

        lax.fori_loop(0, 2, one, 0)


def join_kernel(*refs):
    parts, outs, size_ref = refs[:4], refs[4:6], refs[6]
    for r in range(2):
        for i, p in enumerate(parts):
            packed = p[r, TOK:QROWS, 0:TOK].astype(F32)
            packed = jnp.concatenate([packed, jnp.zeros((128 - (QROWS - TOK), TOK), F32)], axis=0).T
            size_ref[r, i] = packed + pltpu.roll(packed, 128 - HALF_HEADS, 1) + pltpu.roll(packed, 128 - 2 * HALF_HEADS, 1)
    for r in range(2):
        for t in range(TOK // JOIN_ROWS):
            rows = slice(t * JOIN_ROWS, (t + 1) * JOIN_ROWS)
            sizes = [size_ref[r, i, rows] for i in range(4)]
            top = functools.reduce(jnp.maximum, sizes)
            shares = [jnp.exp2(s - top) for s in sizes]
            total = functools.reduce(jnp.add, shares)
            shares = [s / total for s in shares]
            for h in range(HALF_HEADS):
                at = slice(h * 128, (h + 1) * 128)
                o = sum(s[:, h : h + 1] * p[r, rows, at].astype(F32) for s, p in zip(shares, parts, strict=True))
                outs[r][rows, at] = o.astype(BF)


def place_kernel(me_ref, kept_ref, other_ref, out_ref, sems):
    core = me_ref[0] & 1
    copies = [
        pltpu.make_async_copy(half, to, sems.at[i])
        for i, (half, to) in enumerate(zip((kept_ref, other_ref), halves(core, (out_ref,)) + halves(1 - core, (out_ref,)), strict=True))
    ]
    for c in copies:
        c.start()
    for c in copies:
        c.wait()


def shape(*dims, dtype=BF):
    return jax.ShapeDtypeStruct(dims, dtype)


SMEM = pl.BlockSpec(memory_space=pltpu.SMEM)
VMEM = pl.BlockSpec(memory_space=pltpu.VMEM)
ANY = pl.BlockSpec(memory_space=pl.ANY)
HBM = pl.BlockSpec(memory_space=pltpu.HBM)


def room(mib):
    return pltpu.CompilerParams(vmem_limit_bytes=mib * 1024 * 1024)


def cost(flops, moved):
    return pl.CostEstimate(flops=int(flops), bytes_accessed=int(moved), transcendentals=0)


def in_hbm(*arrays):
    return tuple(pltpu.with_memory_space_constraint(a, pltpu.HBM) for a in arrays)


def hbm_shape(*dims, dtype=BF):
    return pltpu.HBM(dims, dtype)


def whole(*dims):
    return pl.BlockSpec(dims, lambda g: (0,) * len(dims))


def attend(name, base, lists, queries, blocks):
    own = name == "attend_own"
    groups = len(queries)
    readers = 2 * groups
    first = VMEM if own else ANY
    return pl.pallas_call(
        functools.partial(attend_kernel, own, base, readers),
        out_shape=[shape(2, QROWS, HALF)] * groups,
        in_specs=[SMEM, SMEM] + [ANY] * groups + [first] + [ANY] * (SIDE - 1),
        out_specs=[VMEM] * groups,
        scratch_shapes=[
            pltpu.VMEM((readers, QROWS, HALF), BF),
            pltpu.VMEM((2, LISTED, 2, BLK, HALF), BF),
            pltpu.VMEM((LISTED // 2 + 1, HALF_HEADS, TOK, 256), F32),
            pltpu.VMEM((HALF_HEADS, TOK, 128), F32),
            pltpu.VMEM((HALF_HEADS, TOK, 256), F32),
            pltpu.SemaphoreType.DMA((groups,)),
            pltpu.SemaphoreType.DMA((2, LISTED)),
        ],
        compiler_params=room(18),
        cost_estimate=cost(readers * 4e8, 8e6),
    )(*lists, *queries, *blocks)


def layers(q_lin, k_lin, v_lin, q_soft, k_soft, v_soft, import_ids, import_counts):
    select, vectors = (jnp.asarray(t) for t in feature_tables())
    me = lax.axis_index("files").astype(jnp.int32).reshape(1)
    place = lax.axis_index("seq").astype(jnp.int32).reshape(1)
    shards = lax.axis_size("seq")
    steps = (HEADS // GROUP,)
    heads16 = pl.BlockSpec((GROUP * FEAT, TOK), lambda g: (g, 0))
    heads128 = pl.BlockSpec((TOK, GROUP * 128), lambda g: (0, g))
    mine = (me, import_ids[0, 0], import_counts[0]) + in_hbm(k_soft[0], v_soft[0], q_soft[0])

    sent = pl.pallas_call(
        pack_kernel,
        name="pack",
        out_shape=shape(2 * TOK + QROWS, HALF),
        in_specs=[SMEM] * 3 + [HBM] * 3,
        out_specs=VMEM,
        scratch_shapes=[pltpu.SemaphoreType.DMA((3,))],
        compiler_params=room(4),
        cost_estimate=cost(0, 2e6),
    )(*mine)
    mate = swap_cores(sent)
    pair = [shape(2, 2, TOK, HALF), shape(2, QROWS, HALF)]
    kv, q = pl.pallas_call(
        own_kernel,
        name="own",
        out_shape=pair,
        in_specs=[SMEM] * 3 + [HBM] * 3,
        out_specs=[VMEM] * 2,
        scratch_shapes=[pltpu.SemaphoreType.DMA((3,))],
        compiler_params=room(6),
        cost_estimate=cost(0, 2e6),
    )(*mine)

    kv, q = pl.pallas_call(
        merge_kernel,
        name="merge",
        out_shape=pair,
        in_specs=[VMEM, ANY, ANY],
        out_specs=[ANY] * 2,
        scratch_shapes=[pltpu.SemaphoreType.DMA((3,))],
        input_output_aliases={1: 0, 2: 1},
        compiler_params=room(4),
        cost_estimate=cost(0, 2e6),
    )(mate, kv, q)
    kv_right = move(kv, "kv", -1)
    kv_left = move(kv, "kv", 1)
    q_left = move(q, "q", 1)
    q_right = move(q, "q", -1)
    kv_far = move(kv_right, "kv", -1)
    q_far = move(q_left, "q", 1)

    state = pl.pallas_call(
        state_kernel,
        name="state",
        grid=steps,
        out_shape=hbm_shape(HEADS, FROWS, 128),
        in_specs=[heads16, heads128, whole(*select.shape), whole(*vectors.shape)],
        out_specs=pl.BlockSpec((GROUP, FROWS, 128), lambda g: (g, 0, 0)),
        compiler_params=room(8),
        cost_estimate=cost(1e9, 4e6),
    )(*in_hbm(k_lin[0].T, v_lin[0], select, vectors))
    slices = lax.all_to_all(state.reshape(shards, HEADS * FROWS // shards, 128), "seq", 0, 0, tiled=True)

    num, den, phi = pl.pallas_call(
        local_kernel,
        name="local",
        grid=steps,
        out_shape=[hbm_shape(TOK, D), hbm_shape(TOK, 128, dtype=F32), hbm_shape(HEADS, FROWS, TOK)],
        in_specs=[heads16, heads16, heads128, whole(*select.shape), whole(*vectors.shape)],
        out_specs=[heads128, whole(TOK, 128), pl.BlockSpec((GROUP, FROWS, TOK), lambda g: (g, 0, 0))],
        compiler_params=room(10),
        cost_estimate=cost(4e9, 8e6),
    )(*in_hbm(q_lin[0].T, k_lin[0].T, v_lin[0], select, vectors))

    blocks = (kv, kv_right, kv_far, kv_left)
    slices, num, den, phi = lax.optimization_barrier((slices, num, den, phi))
    prefix = pl.pallas_call(
        prefix_kernel,
        name="prefix",
        out_shape=hbm_shape(*slices.shape),
        in_specs=[SMEM, VMEM],
        out_specs=VMEM,
        compiler_params=room(6),
        cost_estimate=cost(0, 2e6),
    )(place, slices)
    before = lax.all_to_all(prefix, "seq", 0, 0, tiled=True).reshape(HEADS, FROWS, 128)
    lists = pl.pallas_call(
        search_kernel,
        name="search",
        out_shape=[shape(2 * SIDE, 128, dtype=jnp.int32), shape(2 * SIDE, dtype=jnp.int32)],
        in_specs=[SMEM] + [ANY] * SIDE,
        out_specs=[SMEM] * 2,
        scratch_shapes=[
            pltpu.VMEM((2 * SIDE, 128), jnp.int32),
            pltpu.VMEM((2 * SIDE, QROWS - TOK, 128), BF),
            pltpu.SemaphoreType.DMA((SIDE + 1,)),
        ],
        compiler_params=room(2),
        cost_estimate=cost(0, 1e5),
    )(me, q_far, q_left, q_right, q)
    (to_far,) = attend("attend_far", 0, lists, (q_far,), blocks)
    to_far, q_left = lax.optimization_barrier((to_far, q_left))
    from_far = move(to_far, "q", 2)
    (to_left,) = attend("attend_left", 2, lists, (q_left,), blocks)
    to_left, q_right = lax.optimization_barrier((to_left, q_right))
    from_right = move(to_left, "q", -1)
    (to_right,) = attend("attend_right", 4, lists, (q_right,), blocks)
    to_right, q = lax.optimization_barrier((to_right, q))
    from_left = move(to_right, "q", 1)
    (here,) = attend("attend_own", 6, lists, (q,), blocks)
    kept, send = pl.pallas_call(
        join_kernel,
        name="join",
        out_shape=[shape(TOK, HALF)] * 2,
        in_specs=[VMEM] * 4,
        out_specs=[VMEM] * 2,
        scratch_shapes=[pltpu.VMEM((2, 4, TOK, 128), F32)],
        compiler_params=room(8),
        cost_estimate=cost(0, 4e6),
    )(here, from_right, from_left, from_far)
    other = swap_cores(send)
    soft_out = pl.pallas_call(
        place_kernel,
        name="place",
        out_shape=shape(TOK, SM_W),
        in_specs=[SMEM, VMEM, VMEM],
        out_specs=HBM,
        scratch_shapes=[pltpu.SemaphoreType.DMA((2,))],
        compiler_params=room(4),
        cost_estimate=cost(0, 1e6),
    )(me, kept, other)

    lin_out = pl.pallas_call(
        finish_kernel,
        name="finish",
        grid=steps,
        out_shape=shape(TOK, D),
        in_specs=[
            heads128,
            whole(TOK, 128),
            pl.BlockSpec((GROUP, FROWS, TOK), lambda g: (g, 0, 0)),
            pl.BlockSpec((GROUP, FROWS, 128), lambda g: (g, 0, 0)),
        ],
        out_specs=heads128,
        compiler_params=room(8),
        cost_estimate=cost(4e8, 8e6),
    )(*in_hbm(num, den, phi), before)
    return lin_out[None], soft_out[None]


def solution(mesh):
    wide = P("files", "seq", None)
    return jax.shard_map(
        layers,
        mesh=mesh,
        in_specs=(wide,) * 7 + (P("files", "seq"),),
        out_specs=(wide, wide),
        check_vma=False,
    )
```
